32 devices in a mesh: dp: 8 (over y, x, core), ctx: 4 (over z).
Axes of the slice: x: 2, y: 2, z: 4, core: 2. Of those that a mesh axis runs over, the one named last changes fastest.
Arguments:
- hidden_in: float32 [8, 512, 960], P('dp', 'ctx'), may hold values from -6 to 6
- segments: int32 [8, 512], P('dp'), may hold values from 0 to 3, never falling along the last dimension, each value on 1 to 256 neighbouring positions
- attn_flat: bfloat16 [19200, 128], P(('dp', 'ctx')), may hold values from -6 to 6
- mlp_flat: bfloat16 [57600, 128], P(('dp', 'ctx')), may hold values from -6 to 6
- norm_one: float32 [960], replicated, may hold values from 0.1 to 1.9
- norm_two: float32 [960], replicated, may hold values from 0.1 to 1.9
- cotangent: float32 [8, 512, 960], P('dp', 'ctx'), may hold values from -6 to 6
Outputs:
- block_out: float32 [8, 512, 960], P('dp', 'ctx')
- grad_in: float32 [8, 512, 960], P('dp', 'ctx')
- attn_grad: float32 [19200, 128], P(('dp', 'ctx'))
- mlp_grad: float32 [57600, 128], P(('dp', 'ctx'))
- norm_one_grad: float32 [960], replicated
- norm_two_grad: float32 [960], replicated
The draws below stay inside these ranges and needn't reach their ends.
Inputs may be any that keep to these rules, and one draw needn't show every extreme that they name: `segments`: segment numbers never fall along a sequence; each document covers at most 256 positions, some document exactly that many.
All inputs are finite; a program needn't handle non-finite values.
Results may differ from the reference program's by a relative error of at most 0.015.
Values may be sent and summed in bfloat16 or wider, within the bound.
No kernel may reach another device: no remote copies, remote signals or barrier semaphores. Data moves between devices by JAX's collectives and lax.ppermute only.
A program may use at most 128 MiB of HBM per device.

```python
import math
import jax
import jax.numpy as jnp
import numpy as np
from jax import lax

D = 960
HEADS = 15
KV_HEADS = 5
HEAD_DIM = 64
FFN = 2560
LEN = 512
SEQS = 8
N_DP = 8
N_CTX = 4


def pack_drawn(matrices):
    pieces = jnp.concatenate([matrix.reshape(N_CTX, -1) for matrix in matrices], axis=1)
    return pieces.reshape(N_CTX, N_DP, -1).transpose(1, 0, 2).reshape(-1, 128)


def draw_matrix(key, height, width_cols, scale):
    return jax.random.truncated_normal(key, -6.0, 6.0, (height, width_cols), jnp.float32) * scale


def draw_attn_flat(key, part):
    qwidth = HEADS * HEAD_DIM
    kwidth = KV_HEADS * HEAD_DIM
    w_query = draw_matrix(jax.random.fold_in(key, 11), D, qwidth, D ** (-0.5))
    w_key = draw_matrix(jax.random.fold_in(key, 12), D, kwidth, D ** (-0.5))
    w_value = draw_matrix(jax.random.fold_in(key, 13), D, kwidth, D ** (-0.5))
    w_out = draw_matrix(jax.random.fold_in(key, 14), qwidth, D, 8.0 * qwidth ** (-0.5))
    return pack_drawn([w_query, w_key, w_value, w_out]).astype(jnp.bfloat16)


def draw_mlp_flat(key, part):
    w_gate = draw_matrix(jax.random.fold_in(key, 21), D, FFN, D ** (-0.5))
    w_up = draw_matrix(jax.random.fold_in(key, 22), D, FFN, D ** (-0.5))
    w_down = draw_matrix(jax.random.fold_in(key, 23), FFN, D, FFN ** (-0.5))
    return pack_drawn([w_gate, w_up, w_down]).astype(jnp.bfloat16)


def block_scale(key, extent, split, smallest, largest):
    def one(position, blocks):
        steps = jax.random.uniform(jax.random.fold_in(jax.random.fold_in(key, 6), position), (blocks,), jnp.float32, smallest / len(split), largest / len(split))
        return jnp.repeat(jnp.exp(steps), extent[position] // blocks).reshape((-1,) + (1,) * (len(extent) - position - 1))

    gain = one(*split[0])
    for cut in split[1:]:
        gain = gain * one(*cut)
    return gain


def split_up(count, total, reach, skew):
    loads = [(1 << 20) // math.isqrt(grade ** skew) + 1 for grade in range(2, count + 1)]
    rest, counts = total - reach - (count - 1), [1] * (count - 1)
    while rest > 0:
        free = [i for i in range(count - 1) if counts[i] < reach]
        mass, budget = sum([loads[i] for i in free]), rest
        for i in free:
            more = min(reach - counts[i], max(1, budget * loads[i] // mass), rest)
            counts[i] = counts[i] + more
            rest = rest - more
    return np.array([reach] + counts)


def uneven_parts(stream_key, amount, total, bound, skew):
    if amount == 2:
        one = jax.random.randint(stream_key, (), max(1, total - bound), min(bound, total - 1) + 1)
        return jnp.stack([one, total - one])
    tallies = jnp.asarray(split_up(amount, total, bound, skew), jnp.int32)
    couples = (amount - 1) // 2
    donor, sink = tallies[1:1 + 2 * couples:2], tallies[2:2 + 2 * couples:2]
    margin = jnp.minimum(donor - 1, bound - sink)
    moved = jax.random.randint(jax.random.fold_in(stream_key, 1), (couples,), 0, 1 << 20) % (margin + 1)
    tallies = tallies.at[1:1 + 2 * couples:2].set(donor - moved).at[2:2 + 2 * couples:2].set(sink + moved)
    return tallies[jax.random.permutation(jax.random.fold_in(stream_key, 2), amount)]


def scatter_about(own_key, shape, deviation, limit, split=(), held_as=jnp.bfloat16):
    factor_of = block_scale(own_key, shape, split, -0.22, 0.18) if split else 1.0
    entries = jax.random.normal(own_key, shape, jnp.float32) * deviation * factor_of
    return jnp.minimum(jnp.maximum(entries, -limit), limit).astype(held_as)


def setup_inputs(seed: int = 0) -> dict:
    arg_keys = jax.random.split(jax.random.key(seed), 8)
    hidden_in = scatter_about(arg_keys[0], (SEQS, LEN, D), 1.0, 6.0, ((0, 8), (1, 4)), jnp.float32)
    segments = jax.vmap(lambda own: jnp.searchsorted(jnp.cumsum(uneven_parts(own, 4, LEN, LEN // 2, 1)), jnp.arange(LEN), side="right"))(jax.random.split(arg_keys[1], SEQS)).reshape((SEQS, LEN)).astype(jnp.int32)
    attn_flat = draw_attn_flat(jax.random.fold_in(arg_keys[7], 71), 0)
    mlp_flat = draw_mlp_flat(jax.random.fold_in(arg_keys[7], 71), 0)
    norm_one = jnp.clip(1.0 + 0.18 * jax.random.normal(arg_keys[4], (D,), jnp.float32), 0.1, 1.9)
    norm_two = jnp.clip(1.0 + 0.18 * jax.random.normal(arg_keys[5], (D,), jnp.float32), 0.1, 1.9)
    cotangent = scatter_about(arg_keys[6], (SEQS, LEN, D), 1.0, 6.0, ((0, 8), (1, 4)), jnp.float32)
    return {"hidden_in": hidden_in, "segments": segments, "attn_flat": attn_flat, "mlp_flat": mlp_flat, "norm_one": norm_one, "norm_two": norm_two, "cotangent": cotangent}


EPS = 1e-05
THETA = 100000.0

def positions_of(segment_ids):
    earlier = (segment_ids[..., None, :] < segment_ids[..., :, None]).astype(jnp.int32)
    total_len = segment_ids.shape[-1]
    return jnp.arange(total_len, dtype=jnp.int32) - lax.optimization_barrier(jnp.sum(earlier, axis=-1)).astype(jnp.int32)

def rope_tables(positions):
    half_dim = HEAD_DIM // 2
    frequency = THETA ** (-2.0 * jnp.arange(half_dim, dtype=jnp.float32) / HEAD_DIM)
    angles = positions.astype(jnp.float32)[:, None] * frequency[None, :]
    return (jnp.cos(angles)[:, None, :], jnp.sin(angles)[:, None, :])

def rotate(vectors, cosine_table, sine_table):
    half_dim = vectors.shape[-1] // 2
    lower_half = vectors[..., :half_dim]
    upper_half = vectors[..., half_dim:]
    return jnp.concatenate([lower_half * cosine_table - upper_half * sine_table, upper_half * cosine_table + lower_half * sine_table], axis=-1)

def unrotate(grad_rows, cosine_table, sine_table):
    half_dim = grad_rows.shape[-1] // 2
    lower_half = grad_rows[..., :half_dim]
    upper_half = grad_rows[..., half_dim:]
    return jnp.concatenate([lower_half * cosine_table + upper_half * sine_table, upper_half * cosine_table - lower_half * sine_table], axis=-1)

def unpack_blocks(flat_rows, shapes):
    pieces = flat_rows.reshape(N_DP, N_CTX, -1).transpose(1, 0, 2).reshape(N_CTX, -1)
    matrices = []
    offset = 0
    for height, width_cols in shapes:
        length = height * width_cols // N_CTX
        matrices.append(pieces[:, offset:offset + length].reshape(height, width_cols))
        offset = offset + length
    return matrices

def pack_blocks(matrices):
    pieces = jnp.concatenate([matrix.reshape(N_CTX, -1) for matrix in matrices], axis=1)
    return pieces.reshape(N_CTX, N_DP, -1).transpose(1, 0, 2).reshape(-1, 128)

def norm_forward(residual, gain_vec):
    inverse = lax.rsqrt(lax.optimization_barrier(jnp.mean(residual * residual, axis=-1, keepdims=True)) + EPS)
    return (inverse, residual * inverse * gain_vec)

def norm_backward(residual, inverse, gain_vec, grad_normed):
    scaled = grad_normed * gain_vec
    cubed = inverse * inverse * inverse
    grad_resid = inverse * scaled - residual * cubed * lax.optimization_barrier(jnp.mean(scaled * residual, axis=-1, keepdims=True))
    grad_gain = lax.optimization_barrier(jnp.sum(grad_normed * residual * inverse, axis=0))
    return (grad_resid, grad_gain)

def reference(hidden_in, segments, attn_flat, mlp_flat, norm_one, norm_two, cotangent):
    groups = HEADS // KV_HEADS
    qwidth = HEADS * HEAD_DIM
    kwidth = KV_HEADS * HEAD_DIM
    w_query, w_key, w_value, w_out = unpack_blocks(attn_flat, ((D, qwidth), (D, kwidth), (D, kwidth), (qwidth, D)))
    w_gate, w_up, w_down = unpack_blocks(mlp_flat, ((D, FFN), (D, FFN), (FFN, D)))
    score_scale = HEAD_DIM ** (-0.5)
    low = jnp.bfloat16
    wide = jnp.float32

    def per_sequence(totals, seq_items):
        residual, segment_row, cot_rows = seq_items
        row_count = residual.shape[0]
        cosine_table, sine_table = rope_tables(positions_of(segment_row))
        key_index = jnp.arange(row_count, dtype=jnp.int32)
        allowed = (segment_row[:, None] == segment_row[None, :]) & (key_index[None, :] <= key_index[:, None])
        inv_one, normed_one = norm_forward(residual, norm_one)
        normed_one = normed_one.astype(low)
        query = jnp.dot(normed_one, w_query, preferred_element_type=wide).reshape(row_count, HEADS, HEAD_DIM)
        key_raw = jnp.dot(normed_one, w_key, preferred_element_type=wide).reshape(row_count, KV_HEADS, HEAD_DIM)
        value_low = jnp.dot(normed_one, w_value, preferred_element_type=wide).reshape(row_count, KV_HEADS, HEAD_DIM).astype(low)
        query_rot = rotate(query, cosine_table, sine_table).astype(low).reshape(row_count, KV_HEADS, groups, HEAD_DIM)
        key_rot = rotate(key_raw, cosine_table, sine_table).astype(low)
        scores = jnp.einsum('qkgd,lkd->kgql', query_rot.astype(wide), key_rot.astype(wide)) * score_scale
        scores = jnp.where(allowed[None, None], scores, -jnp.inf)
        row_top = lax.optimization_barrier(jnp.max(scores, axis=-1, keepdims=True))
        log_total = row_top + jnp.log(lax.optimization_barrier(jnp.sum(jnp.exp(scores - row_top), axis=-1, keepdims=True)))
        attn_probs = jnp.exp(scores - log_total)
        probs_low = attn_probs.astype(low)
        head_mix = jnp.einsum('kgql,lkd->qkgd', probs_low.astype(wide), value_low.astype(wide))
        head_mix = head_mix.reshape(row_count, qwidth).astype(low)
        middle = residual + jnp.dot(head_mix, w_out, preferred_element_type=wide)
        inv_two, normed_two = norm_forward(middle, norm_two)
        normed_two = normed_two.astype(low)
        gate_pre = jnp.dot(normed_two, w_gate, preferred_element_type=wide)
        up_proj = jnp.dot(normed_two, w_up, preferred_element_type=wide)
        gate_sigmoid = jax.nn.sigmoid(gate_pre)
        active = (gate_pre * gate_sigmoid * up_proj).astype(low)
        block_rows = middle + jnp.dot(active, w_down, preferred_element_type=wide)
        cot_low = cot_rows.astype(low)
        grad_active = jnp.dot(cot_low, w_down.T, preferred_element_type=wide)
        grad_w_down = jnp.dot(active.T, cot_low, preferred_element_type=wide)
        grad_gate = (grad_active * up_proj * gate_sigmoid * (1.0 + gate_pre * (1.0 - gate_sigmoid))).astype(low)
        grad_up = (grad_active * gate_pre * gate_sigmoid).astype(low)
        grad_w_gate = jnp.dot(normed_two.T, grad_gate, preferred_element_type=wide)
        grad_w_up = jnp.dot(normed_two.T, grad_up, preferred_element_type=wide)
        grad_normed_two = jnp.dot(grad_gate, w_gate.T, preferred_element_type=wide) + jnp.dot(grad_up, w_up.T, preferred_element_type=wide)
        grad_middle, grad_gain_two = norm_backward(middle, inv_two, norm_two, grad_normed_two)
        grad_middle = cot_rows + grad_middle
        grad_mid_low = grad_middle.astype(low)
        grad_w_out = jnp.dot(head_mix.T, grad_mid_low, preferred_element_type=wide)
        grad_mix = jnp.dot(grad_mid_low, w_out.T, preferred_element_type=wide).astype(low)
        grad_mix = grad_mix.reshape(row_count, KV_HEADS, groups, HEAD_DIM)
        grad_probs = jnp.einsum('qkgd,lkd->kgql', grad_mix.astype(wide), value_low.astype(wide))
        grad_value = jnp.einsum('kgql,qkgd->lkd', probs_low.astype(wide), grad_mix.astype(wide))
        grad_scores = attn_probs * (grad_probs - lax.optimization_barrier(jnp.sum(attn_probs * grad_probs, axis=-1, keepdims=True)))
        grad_scores_low = (grad_scores * score_scale).astype(low)
        grad_query = jnp.einsum('kgql,lkd->qkgd', grad_scores_low.astype(wide), key_rot.astype(wide)).reshape(row_count, HEADS, HEAD_DIM)
        grad_key = jnp.einsum('kgql,qkgd->lkd', grad_scores_low.astype(wide), query_rot.astype(wide))
        grad_query = unrotate(grad_query, cosine_table, sine_table).reshape(row_count, qwidth).astype(low)
        grad_key = unrotate(grad_key, cosine_table, sine_table).reshape(row_count, kwidth).astype(low)
        grad_value = grad_value.reshape(row_count, kwidth).astype(low)
        grad_w_query = jnp.dot(normed_one.T, grad_query, preferred_element_type=wide)
        grad_w_key = jnp.dot(normed_one.T, grad_key, preferred_element_type=wide)
        grad_w_value = jnp.dot(normed_one.T, grad_value, preferred_element_type=wide)
        grad_normed_one = jnp.dot(grad_query, w_query.T, preferred_element_type=wide) + jnp.dot(grad_key, w_key.T, preferred_element_type=wide) + jnp.dot(grad_value, w_value.T, preferred_element_type=wide)
        grad_resid, grad_gain_one = norm_backward(residual, inv_one, norm_one, grad_normed_one)
        grad_resid = grad_middle + grad_resid
        terms = (grad_w_query, grad_w_key, grad_w_value, grad_w_out, grad_w_gate, grad_w_up, grad_w_down, grad_gain_one, grad_gain_two)
        new_totals = tuple((total + term for total, term in zip(totals, terms)))
        return (new_totals, (block_rows, grad_resid))
    start_totals = (jnp.zeros((D, qwidth), wide), jnp.zeros((D, kwidth), wide), jnp.zeros((D, kwidth), wide), jnp.zeros((qwidth, D), wide), jnp.zeros((D, FFN), wide), jnp.zeros((D, FFN), wide), jnp.zeros((FFN, D), wide), jnp.zeros((D,), wide), jnp.zeros((D,), wide))
    totals, (block_out, grad_in) = lax.scan(per_sequence, start_totals, (hidden_in, segments, cotangent))
    attn_grad = pack_blocks(list(totals[0:4]))
    mlp_grad = pack_blocks(list(totals[4:7]))
    return (block_out, grad_in, attn_grad, mlp_grad, totals[7], totals[8])
```

```python
import jax
import jax.numpy as jnp
from jax import lax
from jax.sharding import PartitionSpec as P

D = 960
HEADS = 15
KV_HEADS = 5
HEAD_DIM = 64
FFN = 2560


EPS = 1e-05
THETA = 100000.0


def positions_of(segment_ids):
    earlier = (segment_ids[..., None, :] < segment_ids[..., :, None]).astype(jnp.int32)
    total_len = segment_ids.shape[-1]
    return jnp.arange(total_len, dtype=jnp.int32) - jnp.sum(earlier, axis=-1)


def rope_tables(positions):
    half_dim = HEAD_DIM // 2
    frequency = THETA ** (-2.0 * jnp.arange(half_dim, dtype=jnp.float32) / HEAD_DIM)
    angles = positions.astype(jnp.float32)[:, None] * frequency[None, :]
    return (jnp.cos(angles)[:, None, :], jnp.sin(angles)[:, None, :])


def rotate(vectors, cosine_table, sine_table):
    half_dim = vectors.shape[-1] // 2
    lower_half = vectors[..., :half_dim]
    upper_half = vectors[..., half_dim:]
    return jnp.concatenate(
        [
            lower_half * cosine_table - upper_half * sine_table,
            upper_half * cosine_table + lower_half * sine_table,
        ],
        axis=-1,
    )


def unrotate(grad_rows, cosine_table, sine_table):
    half_dim = grad_rows.shape[-1] // 2
    lower_half = grad_rows[..., :half_dim]
    upper_half = grad_rows[..., half_dim:]
    return jnp.concatenate(
        [
            lower_half * cosine_table + upper_half * sine_table,
            upper_half * cosine_table - lower_half * sine_table,
        ],
        axis=-1,
    )


def unpack_blocks(flat_rows, shapes, dp_count, ctx_count):
    pieces = flat_rows.reshape(dp_count, ctx_count, -1).transpose(1, 0, 2).reshape(ctx_count, -1)
    matrices = []
    offset = 0
    for height, width_cols in shapes:
        length = height * width_cols // ctx_count
        matrices.append(pieces[:, offset : offset + length].reshape(height, width_cols))
        offset = offset + length
    return matrices


def norm_forward(residual, gain_vec):
    inverse = lax.rsqrt(jnp.mean(residual * residual, axis=-1, keepdims=True) + EPS)
    return (inverse, residual * inverse * gain_vec)


def norm_backward(residual, inverse, gain_vec, grad_normed):
    scaled = grad_normed * gain_vec
    cubed = inverse * inverse * inverse
    grad_resid = inverse * scaled - residual * cubed * jnp.mean(
        scaled * residual, axis=-1, keepdims=True
    )
    grad_gain = jnp.sum(grad_normed * residual * inverse, axis=0)
    return (grad_resid, grad_gain)


def masked_scores(query_rot, key_whole, allowed, score_scale):
    scores = (
        jnp.einsum("sqkgd,slkd->skgql", query_rot, key_whole, preferred_element_type=jnp.float32)
        * score_scale
    )
    return jnp.where(allowed, scores, -jnp.inf)


def left_dot(left_cols, right_rows):
    return lax.dot_general(
        left_cols, right_rows, (((0,), (0,)), ((), ())), preferred_element_type=jnp.float32
    )


def body_rows(hidden_in, segments, attn_flat, mlp_flat, norm_one, norm_two, cotangent):
    seq_count, local_len, model_width = hidden_in.shape
    seq_len = segments.shape[1]
    row_count = seq_count * local_len
    groups = HEADS // KV_HEADS
    qwidth = HEADS * HEAD_DIM
    kwidth = KV_HEADS * HEAD_DIM
    score_scale = HEAD_DIM ** (-0.5)
    low = jnp.bfloat16
    wide = jnp.float32
    dp_count = lax.axis_size("dp")
    ctx_count = lax.axis_size("ctx")
    attn_shapes = ((D, qwidth), (D, kwidth), (D, kwidth), (qwidth, D))
    mlp_shapes = ((D, FFN), (D, FFN), (FFN, D))
    start_row = lax.axis_index("ctx") * local_len
    attn_whole, mlp_whole = (
        lax.all_gather(attn_flat, ("dp", "ctx"), axis=0, tiled=True),
        lax.all_gather(mlp_flat, ("dp", "ctx"), axis=0, tiled=True),
    )
    w_query, w_key, w_value, w_out = unpack_blocks(attn_whole, attn_shapes, dp_count, ctx_count)
    w_gate, w_up, w_down = unpack_blocks(mlp_whole, mlp_shapes, dp_count, ctx_count)
    pos_all = positions_of(segments)
    pos_local = lax.dynamic_slice_in_dim(pos_all, start_row, local_len, 1)
    seg_local = lax.dynamic_slice_in_dim(segments, start_row, local_len, 1)
    cosine_table, sine_table = rope_tables(pos_local.reshape(-1))
    key_index = jnp.arange(seq_len, dtype=jnp.int32)
    query_index = start_row + jnp.arange(local_len, dtype=jnp.int32)
    allowed = (seg_local[:, :, None] == segments[:, None, :]) & (
        key_index[None, None, :] <= query_index[None, :, None]
    )
    allowed = allowed[:, None, None]
    residual = hidden_in.reshape(row_count, model_width)
    inv_one, normed_one = norm_forward(residual, norm_one)
    normed_one = normed_one.astype(low)
    query = jnp.dot(normed_one, w_query, preferred_element_type=wide).reshape(
        row_count, HEADS, HEAD_DIM
    )
    key_raw = jnp.dot(normed_one, w_key, preferred_element_type=wide).reshape(
        row_count, KV_HEADS, HEAD_DIM
    )
    value_low = jnp.dot(normed_one, w_value, preferred_element_type=wide).astype(low)
    query_rot = (
        rotate(query, cosine_table, sine_table)
        .astype(low)
        .reshape(seq_count, local_len, KV_HEADS, groups, HEAD_DIM)
    )
    key_rot = rotate(key_raw, cosine_table, sine_table).astype(low)
    kv_local = jnp.concatenate(
        [
            key_rot.reshape(seq_count, local_len, kwidth),
            value_low.reshape(seq_count, local_len, kwidth),
        ],
        axis=2,
    )
    kv_whole = lax.all_gather(kv_local, "ctx", axis=1, tiled=True)
    key_whole = kv_whole[:, :, :kwidth].reshape(seq_count, seq_len, KV_HEADS, HEAD_DIM)
    value_whole = kv_whole[:, :, kwidth:].reshape(seq_count, seq_len, KV_HEADS, HEAD_DIM)
    scores = masked_scores(query_rot, key_whole, allowed, score_scale)
    row_top = jnp.max(scores, axis=-1, keepdims=True)
    log_total = row_top + jnp.log(jnp.sum(jnp.exp(scores - row_top), axis=-1, keepdims=True))
    probs_low = jnp.exp(scores - log_total).astype(low)
    head_mix = jnp.einsum("skgql,slkd->sqkgd", probs_low, value_whole, preferred_element_type=wide)
    head_mix = head_mix.reshape(row_count, qwidth).astype(low)
    middle = residual + jnp.dot(head_mix, w_out, preferred_element_type=wide)
    inv_two, normed_two = norm_forward(middle, norm_two)
    normed_two = normed_two.astype(low)
    gate_pre = jnp.dot(normed_two, w_gate, preferred_element_type=wide)
    up_proj = jnp.dot(normed_two, w_up, preferred_element_type=wide)
    gate_sigmoid = jax.nn.sigmoid(gate_pre)
    active = (gate_pre * gate_sigmoid * up_proj).astype(low)
    block_rows = middle + jnp.dot(active, w_down, preferred_element_type=wide)
    one_cols, mix_cols, two_cols, active_cols = (
        lax.all_to_all(normed_one, "ctx", split_axis=1, concat_axis=0, tiled=True),
        lax.all_to_all(head_mix, "ctx", split_axis=1, concat_axis=0, tiled=True),
        lax.all_to_all(normed_two, "ctx", split_axis=1, concat_axis=0, tiled=True),
        lax.all_to_all(active, "ctx", split_axis=1, concat_axis=0, tiled=True),
    )
    cot_rows = cotangent.reshape(row_count, model_width)
    cot_low = cot_rows.astype(low)
    grad_active = jnp.dot(cot_low, w_down.T, preferred_element_type=wide)
    grad_gate = (
        grad_active * up_proj * gate_sigmoid * (1.0 + gate_pre * (1.0 - gate_sigmoid))
    ).astype(low)
    grad_up = (grad_active * gate_pre * gate_sigmoid).astype(low)
    grad_normed_two = jnp.dot(grad_gate, w_gate.T, preferred_element_type=wide) + jnp.dot(
        grad_up, w_up.T, preferred_element_type=wide
    )
    grad_middle, grad_gain_two = norm_backward(middle, inv_two, norm_two, grad_normed_two)
    grad_middle = cot_rows + grad_middle
    grad_mid_low = grad_middle.astype(low)
    grad_mix = jnp.dot(grad_mid_low, w_out.T, preferred_element_type=wide).astype(low)
    grad_mix = grad_mix.reshape(seq_count, local_len, KV_HEADS, groups, HEAD_DIM)
    attn_probs = jnp.exp(masked_scores(query_rot, key_whole, allowed, score_scale) - log_total)
    probs_low = attn_probs.astype(low)
    grad_probs = jnp.einsum("sqkgd,slkd->skgql", grad_mix, value_whole, preferred_element_type=wide)
    grad_value_all = jnp.einsum(
        "skgql,sqkgd->slkd", probs_low, grad_mix, preferred_element_type=wide
    )
    grad_scores = attn_probs * (
        grad_probs - jnp.sum(attn_probs * grad_probs, axis=-1, keepdims=True)
    )
    grad_scores_low = (grad_scores * score_scale).astype(low)
    grad_query = jnp.einsum(
        "skgql,slkd->sqkgd", grad_scores_low, key_whole, preferred_element_type=wide
    )
    grad_key_all = jnp.einsum(
        "skgql,sqkgd->slkd", grad_scores_low, query_rot, preferred_element_type=wide
    )
    kv_terms = jnp.concatenate(
        [
            grad_key_all.reshape(seq_count, seq_len, kwidth),
            grad_value_all.reshape(seq_count, seq_len, kwidth),
        ],
        axis=2,
    )
    kv_owned = lax.psum_scatter(
        kv_terms.astype(jnp.bfloat16), "ctx", scatter_dimension=1, tiled=True
    ).astype(jnp.float32)
    grad_key = kv_owned[:, :, :kwidth].reshape(row_count, KV_HEADS, HEAD_DIM)
    grad_value = kv_owned[:, :, kwidth:].reshape(row_count, kwidth).astype(low)
    grad_query = (
        unrotate(grad_query.reshape(row_count, HEADS, HEAD_DIM), cosine_table, sine_table)
        .reshape(row_count, qwidth)
        .astype(low)
    )
    grad_key = unrotate(grad_key, cosine_table, sine_table).reshape(row_count, kwidth).astype(low)
    grad_normed_one = (
        jnp.dot(grad_query, w_query.T, preferred_element_type=wide)
        + jnp.dot(grad_key, w_key.T, preferred_element_type=wide)
        + jnp.dot(grad_value, w_value.T, preferred_element_type=wide)
    )
    grad_resid, grad_gain_one = norm_backward(residual, inv_one, norm_one, grad_normed_one)
    grad_resid = grad_middle + grad_resid
    gathered = (
        lax.all_gather(grad_query, "ctx", axis=0, tiled=True),
        lax.all_gather(grad_key, "ctx", axis=0, tiled=True),
        lax.all_gather(grad_value, "ctx", axis=0, tiled=True),
        lax.all_gather(grad_mid_low, "ctx", axis=0, tiled=True),
        lax.all_gather(grad_gate, "ctx", axis=0, tiled=True),
        lax.all_gather(grad_up, "ctx", axis=0, tiled=True),
        lax.all_gather(cot_low, "ctx", axis=0, tiled=True),
    )
    all_query, all_key, all_value, all_mid, all_gate, all_up, all_cot = gathered
    attn_terms = jnp.concatenate(
        [
            left_dot(one_cols, all_query).reshape(-1),
            left_dot(one_cols, all_key).reshape(-1),
            left_dot(one_cols, all_value).reshape(-1),
            left_dot(mix_cols, all_mid).reshape(-1),
        ]
    ).reshape(-1, 128)
    mlp_terms = jnp.concatenate(
        [
            left_dot(two_cols, all_gate).reshape(-1),
            left_dot(two_cols, all_up).reshape(-1),
            left_dot(active_cols, all_cot).reshape(-1),
        ]
    ).reshape(-1, 128)
    attn_grad, mlp_grad = (
        lax.psum_scatter(
            attn_terms.astype(jnp.bfloat16), "dp", scatter_dimension=0, tiled=True
        ).astype(jnp.float32),
        lax.psum_scatter(
            mlp_terms.astype(jnp.bfloat16), "dp", scatter_dimension=0, tiled=True
        ).astype(jnp.float32),
    )
    gain_sums = lax.psum(jnp.stack([grad_gain_one, grad_gain_two]), ("dp", "ctx"))
    return (
        block_rows.reshape(seq_count, local_len, model_width),
        grad_resid.reshape(seq_count, local_len, model_width),
        attn_grad,
        mlp_grad,
        gain_sums[0],
        gain_sums[1],
    )


def gain_total(gain_rows):
    total = gain_rows
    for step in range(1, lax.axis_size("ctx")):
        total = total + lax.ppermute(gain_rows, "ctx", swap_pairs("ctx", step))
    step = 1
    while step < lax.axis_size("dp"):
        total = total + lax.ppermute(total, "dp", swap_pairs("dp", step))
        step = 2 * step
    return total


def swap_pairs(axis, step):
    return [(place, place ^ step) for place in range(lax.axis_size(axis))]


def spread(rows):
    return [rows] + [
        lax.ppermute(rows, "ctx", swap_pairs("ctx", step)) for step in range(1, lax.axis_size("ctx"))
    ]


def collect(parts):
    total = parts[0]
    for step in range(1, lax.axis_size("ctx")):
        moved = lax.ppermute(parts[step].astype(jnp.bfloat16), "ctx", swap_pairs("ctx", step))
        total = total + moved.astype(jnp.float32)
    return total


def trade(blocks):
    here = lax.axis_index("ctx")
    got = [lax.dynamic_index_in_dim(blocks, here, 0, False)]
    for step in range(1, lax.axis_size("ctx")):
        block = lax.dynamic_index_in_dim(blocks, here ^ step, 0, False)
        got.append(lax.ppermute(block, "ctx", swap_pairs("ctx", step)))
    return got


def in_order(pieces):
    here = lax.axis_index("ctx")
    step = 1
    while step < len(pieces):
        bit = (here & step) != 0
        pieces = [
            jnp.where(bit, pieces[place ^ step], pieces[place]) for place in range(len(pieces))
        ]
        step = 2 * step
    return jnp.stack(pieces)


def columns_apply(dp_count, ctx_count, rows):
    unit = FFN // 128
    return (
        rows % unit == 0
        and FFN % (128 * ctx_count) == 0
        and D % ctx_count == 0
        and ctx_count & (ctx_count - 1) == 0
        and dp_count & (dp_count - 1) == 0
        and rows % ctx_count == 0
        and (2 * (D // ctx_count) % (rows // unit)) * unit % ctx_count == 0
        and (rows - (2 * (D // ctx_count) % (rows // unit)) * unit) % ctx_count == 0
    )


def mlp_sizes(rows, ctx_count):
    unit = FFN // 128
    held = rows // unit
    tall = 2 * (D // ctx_count)
    return unit, unit // ctx_count, held, tall // held, tall % held


def gather_mlp(flat):
    ctx_count = lax.axis_size("ctx")
    place = lax.axis_index("dp")
    rows = flat.shape[0]
    unit, part, held, edge, rest = mlp_sizes(rows, ctx_count)
    cut = rest * unit

    def by_column(block, count):
        return (
            block.reshape(count, ctx_count, part, 128)
            .transpose(1, 0, 2, 3)
            .reshape(ctx_count, count * part, 128)
        )

    full = by_column(flat, held)
    tail = flat[cut:].reshape(ctx_count, -1, 128)
    mixed = jnp.concatenate([by_column(flat[:cut], rest), tail], axis=1)
    got = in_order(trade(jnp.where(place < edge, full, mixed)))
    kept = jnp.concatenate([got[:, : rest * part], tail], axis=1)
    block = jnp.where(
        place < edge, got, jnp.where(place == edge, kept, flat.reshape(ctx_count, -1, 128))
    )
    whole = lax.all_gather(block.reshape(rows, 128), "dp", axis=0, tiled=True)
    whole = whole.reshape(-1, ctx_count, rows // ctx_count, 128)
    tall = jnp.concatenate(
        [
            whole[:edge]
            .reshape(edge, ctx_count, held, part, 128)
            .transpose(1, 0, 2, 3, 4)
            .reshape(ctx_count, edge * held, part * 128),
            whole[edge, :, : rest * part].reshape(ctx_count, rest, part * 128),
        ],
        axis=1,
    )
    half = tall.shape[1] // 2
    w_gate = tall[:, :half].reshape(D, part * 128)
    w_up = tall[:, half:].reshape(D, part * 128)
    w_down = jnp.concatenate(
        [whole[edge, :, rest * part :].reshape(-1, 128), whole[edge + 1 :].reshape(-1, 128)], axis=0
    ).reshape(FFN // ctx_count, D)
    return w_gate, w_up, w_down


def scatter_mlp(grad_w_gate, grad_w_up, grad_w_down, rows):
    ctx_count = lax.axis_size("ctx")
    place = lax.axis_index("dp")
    unit, part, held, edge, rest = mlp_sizes(rows, ctx_count)
    low = jnp.bfloat16
    tall = jnp.concatenate(
        [
            grad_w_gate.astype(low).reshape(ctx_count, -1, part, 128),
            grad_w_up.astype(low).reshape(ctx_count, -1, part, 128),
        ],
        axis=1,
    )
    down = grad_w_down.astype(low).reshape(-1, 128)
    first = (
        tall[:, : edge * held]
        .reshape(ctx_count, edge, held * part, 128)
        .transpose(1, 0, 2, 3)
        .reshape(edge * rows, 128)
    )
    cut = rest * unit
    middle = jnp.concatenate(
        [
            tall[:, edge * held :].reshape(ctx_count, rest * part, 128),
            down[: rows - cut].reshape(ctx_count, -1, 128),
        ],
        axis=1,
    ).reshape(rows, 128)
    terms = jnp.concatenate([first, middle, down[rows - cut :]], axis=0)
    own = lax.psum_scatter(terms, "dp", scatter_dimension=0, tiled=True)
    blocks = own.reshape(ctx_count, rows // ctx_count, 128)
    got = in_order(trade(blocks))

    def by_row(block, count):
        return block.reshape(ctx_count, count, part, 128).transpose(1, 0, 2, 3).reshape(-1, 128)

    full = by_row(got, held)
    mixed = jnp.concatenate(
        [by_row(got[:, : rest * part], rest), blocks[:, rest * part :].reshape(-1, 128)], axis=0
    )
    out = jnp.where(place < edge, full, jnp.where(place == edge, mixed, own))
    return out.astype(jnp.float32)


def body(hidden_in, segments, attn_flat, mlp_flat, norm_one, norm_two, cotangent):
    if not columns_apply(lax.axis_size("dp"), lax.axis_size("ctx"), mlp_flat.shape[0]):
        return body_rows(hidden_in, segments, attn_flat, mlp_flat, norm_one, norm_two, cotangent)
    return body_columns(hidden_in, segments, attn_flat, mlp_flat, norm_one, norm_two, cotangent)


def body_columns(hidden_in, segments, attn_flat, mlp_flat, norm_one, norm_two, cotangent):
    seq_count, local_len, model_width = hidden_in.shape
    seq_len = segments.shape[1]
    row_count = seq_count * local_len
    groups = HEADS // KV_HEADS
    qwidth = HEADS * HEAD_DIM
    kwidth = KV_HEADS * HEAD_DIM
    score_scale = HEAD_DIM ** (-0.5)
    low = jnp.bfloat16
    wide = jnp.float32
    dp_count = lax.axis_size("dp")
    ctx_count = lax.axis_size("ctx")
    here = lax.axis_index("ctx")
    attn_shapes = ((D, qwidth), (D, kwidth), (D, kwidth), (qwidth, D))
    back = -(-(seq_len // 2 - 1) // local_len)
    start_row = here * local_len

    attn_near = in_order(spread(attn_flat)).reshape(-1, 128)
    attn_whole = lax.all_gather(attn_near, "dp", axis=0, tiled=True)
    w_query, w_key, w_value, w_out = unpack_blocks(attn_whole, attn_shapes, dp_count, ctx_count)
    w_gate, w_up, w_down = gather_mlp(mlp_flat)

    pos_all = positions_of(segments)
    pos_local = lax.dynamic_slice_in_dim(pos_all, start_row, local_len, 1)
    seg_local = lax.dynamic_slice_in_dim(segments, start_row, local_len, 1)
    seg_near = lax.dynamic_slice_in_dim(
        jnp.pad(segments, ((0, 0), (back * local_len, 0)), constant_values=-1),
        start_row,
        (back + 1) * local_len,
        1,
    )
    cosine_table, sine_table = rope_tables(pos_local.reshape(-1))
    key_index = jnp.arange((back + 1) * local_len, dtype=jnp.int32) - back * local_len
    query_index = jnp.arange(local_len, dtype=jnp.int32)
    allowed = (seg_local[:, :, None] == seg_near[:, None, :]) & (
        key_index[None, None, :] <= query_index[None, :, None]
    )
    allowed = allowed[:, None, None]

    residual = hidden_in.reshape(row_count, model_width)
    cot_rows = cotangent.reshape(row_count, model_width)
    cot_low = cot_rows.astype(low)
    cot_all = jnp.concatenate(spread(cot_low), axis=0)
    inv_one, normed_one = norm_forward(residual, norm_one)
    normed_one = normed_one.astype(low)

    def cols(rows):
        blocks = rows.reshape(row_count, ctx_count, -1).transpose(1, 0, 2)
        return jnp.concatenate(trade(blocks), axis=0)

    one_cols = cols(normed_one)
    query = jnp.dot(normed_one, w_query, preferred_element_type=wide).reshape(
        row_count, HEADS, HEAD_DIM
    )
    key_raw = jnp.dot(normed_one, w_key, preferred_element_type=wide).reshape(
        row_count, KV_HEADS, HEAD_DIM
    )
    value_low = jnp.dot(normed_one, w_value, preferred_element_type=wide).astype(low)
    key_rot = rotate(key_raw, cosine_table, sine_table).astype(low)
    kv_local = jnp.concatenate(
        [
            key_rot.reshape(seq_count, local_len, kwidth),
            value_low.reshape(seq_count, local_len, kwidth),
        ],
        axis=2,
    )
    up_pairs = [
        [(place, place + step) for place in range(ctx_count - step)] for step in range(back + 1)
    ]
    down_pairs = [[(right, left) for left, right in pairs] for pairs in up_pairs]
    kv_near = jnp.concatenate(
        [lax.ppermute(kv_local, "ctx", up_pairs[step]) for step in range(back, 0, -1)] + [kv_local],
        axis=1,
    )
    query_rot = (
        rotate(query, cosine_table, sine_table)
        .astype(low)
        .reshape(seq_count, local_len, KV_HEADS, groups, HEAD_DIM)
    )
    near_len = (back + 1) * local_len
    key_near = kv_near[:, :, :kwidth].reshape(seq_count, near_len, KV_HEADS, HEAD_DIM)
    value_near = kv_near[:, :, kwidth:].reshape(seq_count, near_len, KV_HEADS, HEAD_DIM)
    scores = masked_scores(query_rot, key_near, allowed, score_scale)
    row_top = jnp.max(scores, axis=-1, keepdims=True)
    log_total = row_top + jnp.log(jnp.sum(jnp.exp(scores - row_top), axis=-1, keepdims=True))
    attn_probs = jnp.exp(scores - log_total)
    probs_low = attn_probs.astype(low)
    head_mix = jnp.einsum("skgql,slkd->sqkgd", probs_low, value_near, preferred_element_type=wide)
    head_mix = head_mix.reshape(row_count, qwidth).astype(low)
    middle = residual + jnp.dot(head_mix, w_out, preferred_element_type=wide)
    inv_two, normed_two = norm_forward(middle, norm_two)
    two_all = jnp.concatenate(spread(normed_two.astype(low)), axis=0)
    mix_cols = cols(head_mix)

    grad_active = jnp.dot(cot_all, w_down.T, preferred_element_type=wide)
    gate_pre = jnp.dot(two_all, w_gate, preferred_element_type=wide)
    up_proj = jnp.dot(two_all, w_up, preferred_element_type=wide)
    gate_sigmoid = jax.nn.sigmoid(gate_pre)
    active = (gate_pre * gate_sigmoid * up_proj).astype(low)
    grad_gate = (
        grad_active * up_proj * gate_sigmoid * (1.0 + gate_pre * (1.0 - gate_sigmoid))
    ).astype(low)
    grad_up = (grad_active * gate_pre * gate_sigmoid).astype(low)
    two_terms = jnp.dot(grad_gate, w_gate.T, preferred_element_type=wide) + jnp.dot(
        grad_up, w_up.T, preferred_element_type=wide
    )
    grad_normed_two = collect(jnp.split(two_terms, ctx_count, axis=0))
    block_terms = jnp.dot(active, w_down, preferred_element_type=wide)
    block_rows = middle + collect(jnp.split(block_terms, ctx_count, axis=0))
    mlp_grad = scatter_mlp(
        left_dot(two_all, grad_gate),
        left_dot(two_all, grad_up),
        left_dot(active, cot_all),
        mlp_flat.shape[0],
    )

    grad_middle, grad_gain_two = norm_backward(middle, inv_two, norm_two, grad_normed_two)
    grad_middle = cot_rows + grad_middle
    grad_mid_low = grad_middle.astype(low)
    mid_all = jnp.concatenate(spread(grad_mid_low), axis=0)
    grad_mix = jnp.dot(grad_mid_low, w_out.T, preferred_element_type=wide).astype(low)
    grad_mix = grad_mix.reshape(seq_count, local_len, KV_HEADS, groups, HEAD_DIM)
    grad_probs = jnp.einsum("sqkgd,slkd->skgql", grad_mix, value_near, preferred_element_type=wide)
    grad_value_near = jnp.einsum(
        "skgql,sqkgd->slkd", probs_low, grad_mix, preferred_element_type=wide
    )
    grad_scores = attn_probs * (
        grad_probs - jnp.sum(attn_probs * grad_probs, axis=-1, keepdims=True)
    )
    grad_scores_low = (grad_scores * score_scale).astype(low)
    grad_query = jnp.einsum(
        "skgql,slkd->sqkgd", grad_scores_low, key_near, preferred_element_type=wide
    )
    grad_key_near = jnp.einsum(
        "skgql,sqkgd->slkd", grad_scores_low, query_rot, preferred_element_type=wide
    )
    kv_terms = jnp.concatenate(
        [
            grad_key_near.reshape(seq_count, near_len, kwidth),
            grad_value_near.reshape(seq_count, near_len, kwidth),
        ],
        axis=2,
    )
    kv_owned = kv_terms[:, back * local_len :]
    for step in range(1, back + 1):
        first = (back - step) * local_len
        moved = lax.ppermute(
            kv_terms[:, first : first + local_len].astype(low), "ctx", down_pairs[step]
        )
        kv_owned = kv_owned + moved.astype(wide)
    grad_key = kv_owned[:, :, :kwidth].reshape(row_count, KV_HEADS, HEAD_DIM)
    grad_value = kv_owned[:, :, kwidth:].reshape(row_count, kwidth).astype(low)
    grad_query = (
        unrotate(grad_query.reshape(row_count, HEADS, HEAD_DIM), cosine_table, sine_table)
        .reshape(row_count, qwidth)
        .astype(low)
    )
    grad_key = unrotate(grad_key, cosine_table, sine_table).reshape(row_count, kwidth).astype(low)
    grad_kv = jnp.concatenate([grad_key, grad_value], axis=1)
    all_query = jnp.concatenate(spread(grad_query), axis=0)
    all_kv = jnp.concatenate(spread(grad_kv), axis=0)
    attn_terms = jnp.concatenate(
        [
            left_dot(one_cols, all_query).astype(low).reshape(-1),
            left_dot(one_cols, all_kv[:, :kwidth]).astype(low).reshape(-1),
            left_dot(one_cols, all_kv[:, kwidth:]).astype(low).reshape(-1),
            left_dot(mix_cols, mid_all).astype(low).reshape(-1),
        ]
    ).reshape(-1, 128)
    attn_grad = lax.psum_scatter(attn_terms, "dp", scatter_dimension=0, tiled=True).astype(wide)
    grad_normed_one = (
        jnp.dot(grad_query, w_query.T, preferred_element_type=wide)
        + jnp.dot(grad_key, w_key.T, preferred_element_type=wide)
        + jnp.dot(grad_value, w_value.T, preferred_element_type=wide)
    )
    grad_resid, grad_gain_one = norm_backward(residual, inv_one, norm_one, grad_normed_one)
    grad_resid = grad_middle + grad_resid
    gain_sums = gain_total(jnp.stack([grad_gain_one, grad_gain_two]))
    return (
        block_rows.reshape(seq_count, local_len, model_width),
        grad_resid.reshape(seq_count, local_len, model_width),
        attn_grad,
        mlp_grad,
        gain_sums[0],
        gain_sums[1],
    )


def solution(mesh):
    in_specs = (
        P("dp", "ctx", None),
        P("dp", None),
        P(("dp", "ctx"), None),
        P(("dp", "ctx"), None),
        P(),
        P(),
        P("dp", "ctx", None),
    )
    out_specs = (
        P("dp", "ctx", None),
        P("dp", "ctx", None),
        P(("dp", "ctx"), None),
        P(("dp", "ctx"), None),
        P(),
        P(),
    )
    return jax.shard_map(body, mesh=mesh, in_specs=in_specs, out_specs=out_specs, check_vma=False)
```

```python
import jax
import jax.numpy as jnp
from jax import lax
from jax.experimental import pallas as pl
from jax.experimental.pallas import tpu as pltpu
from jax.sharding import PartitionSpec as P

D = 960
HEADS = 15
KV_HEADS = 5
HEAD_DIM = 64
FFN = 2560


EPS = 1e-05
THETA = 100000.0


def positions_of(segment_ids):
    earlier = (segment_ids[..., None, :] < segment_ids[..., :, None]).astype(jnp.int32)
    total_len = segment_ids.shape[-1]
    return jnp.arange(total_len, dtype=jnp.int32) - jnp.sum(earlier, axis=-1)


def rope_tables(positions):
    half_dim = HEAD_DIM // 2
    frequency = THETA ** (-2.0 * jnp.arange(half_dim, dtype=jnp.float32) / HEAD_DIM)
    angles = positions.astype(jnp.float32)[:, None] * frequency[None, :]
    return (jnp.cos(angles)[:, None, :], jnp.sin(angles)[:, None, :])


def rotate(vectors, cosine_table, sine_table):
    half_dim = vectors.shape[-1] // 2
    lower_half = vectors[..., :half_dim]
    upper_half = vectors[..., half_dim:]
    return jnp.concatenate(
        [
            lower_half * cosine_table - upper_half * sine_table,
            upper_half * cosine_table + lower_half * sine_table,
        ],
        axis=-1,
    )


def unrotate(grad_rows, cosine_table, sine_table):
    half_dim = grad_rows.shape[-1] // 2
    lower_half = grad_rows[..., :half_dim]
    upper_half = grad_rows[..., half_dim:]
    return jnp.concatenate(
        [
            lower_half * cosine_table + upper_half * sine_table,
            upper_half * cosine_table - lower_half * sine_table,
        ],
        axis=-1,
    )


def unpack_blocks(flat_rows, shapes, dp_count, ctx_count):
    pieces = flat_rows.reshape(dp_count, ctx_count, -1).transpose(1, 0, 2).reshape(ctx_count, -1)
    matrices = []
    offset = 0
    for height, width_cols in shapes:
        length = height * width_cols // ctx_count
        matrices.append(pieces[:, offset : offset + length].reshape(height, width_cols))
        offset = offset + length
    return matrices


def norm_forward(residual, gain_vec):
    inverse = lax.rsqrt(jnp.mean(residual * residual, axis=-1, keepdims=True) + EPS)
    return (inverse, residual * inverse * gain_vec)


def norm_backward(residual, inverse, gain_vec, grad_normed):
    scaled = grad_normed * gain_vec
    cubed = inverse * inverse * inverse
    grad_resid = inverse * scaled - residual * cubed * jnp.mean(
        scaled * residual, axis=-1, keepdims=True
    )
    grad_gain = jnp.sum(grad_normed * residual * inverse, axis=0)
    return (grad_resid, grad_gain)


def masked_scores(query_rot, key_whole, allowed, score_scale):
    scores = (
        jnp.einsum("sqkgd,slkd->skgql", query_rot, key_whole, preferred_element_type=jnp.float32)
        * score_scale
    )
    return jnp.where(allowed, scores, -jnp.inf)


def left_dot(left_cols, right_rows):
    return lax.dot_general(
        left_cols, right_rows, (((0,), (0,)), ((), ())), preferred_element_type=jnp.float32
    )


def body_rows(hidden_in, segments, attn_flat, mlp_flat, norm_one, norm_two, cotangent):
    seq_count, local_len, model_width = hidden_in.shape
    seq_len = segments.shape[1]
    row_count = seq_count * local_len
    groups = HEADS // KV_HEADS
    qwidth = HEADS * HEAD_DIM
    kwidth = KV_HEADS * HEAD_DIM
    score_scale = HEAD_DIM ** (-0.5)
    low = jnp.bfloat16
    wide = jnp.float32
    dp_count = lax.axis_size("dp")
    ctx_count = lax.axis_size("ctx")
    attn_shapes = ((D, qwidth), (D, kwidth), (D, kwidth), (qwidth, D))
    mlp_shapes = ((D, FFN), (D, FFN), (FFN, D))
    start_row = lax.axis_index("ctx") * local_len
    attn_whole, mlp_whole = (
        lax.all_gather(attn_flat, ("dp", "ctx"), axis=0, tiled=True),
        lax.all_gather(mlp_flat, ("dp", "ctx"), axis=0, tiled=True),
    )
    w_query, w_key, w_value, w_out = unpack_blocks(attn_whole, attn_shapes, dp_count, ctx_count)
    w_gate, w_up, w_down = unpack_blocks(mlp_whole, mlp_shapes, dp_count, ctx_count)
    pos_all = positions_of(segments)
    pos_local = lax.dynamic_slice_in_dim(pos_all, start_row, local_len, 1)
    seg_local = lax.dynamic_slice_in_dim(segments, start_row, local_len, 1)
    cosine_table, sine_table = rope_tables(pos_local.reshape(-1))
    key_index = jnp.arange(seq_len, dtype=jnp.int32)
    query_index = start_row + jnp.arange(local_len, dtype=jnp.int32)
    allowed = (seg_local[:, :, None] == segments[:, None, :]) & (
        key_index[None, None, :] <= query_index[None, :, None]
    )
    allowed = allowed[:, None, None]
    residual = hidden_in.reshape(row_count, model_width)
    inv_one, normed_one = norm_forward(residual, norm_one)
    normed_one = normed_one.astype(low)
    query = jnp.dot(normed_one, w_query, preferred_element_type=wide).reshape(
        row_count, HEADS, HEAD_DIM
    )
    key_raw = jnp.dot(normed_one, w_key, preferred_element_type=wide).reshape(
        row_count, KV_HEADS, HEAD_DIM
    )
    value_low = jnp.dot(normed_one, w_value, preferred_element_type=wide).astype(low)
    query_rot = (
        rotate(query, cosine_table, sine_table)
        .astype(low)
        .reshape(seq_count, local_len, KV_HEADS, groups, HEAD_DIM)
    )
    key_rot = rotate(key_raw, cosine_table, sine_table).astype(low)
    kv_local = jnp.concatenate(
        [
            key_rot.reshape(seq_count, local_len, kwidth),
            value_low.reshape(seq_count, local_len, kwidth),
        ],
        axis=2,
    )
    kv_whole = lax.all_gather(kv_local, "ctx", axis=1, tiled=True)
    key_whole = kv_whole[:, :, :kwidth].reshape(seq_count, seq_len, KV_HEADS, HEAD_DIM)
    value_whole = kv_whole[:, :, kwidth:].reshape(seq_count, seq_len, KV_HEADS, HEAD_DIM)
    scores = masked_scores(query_rot, key_whole, allowed, score_scale)
    row_top = jnp.max(scores, axis=-1, keepdims=True)
    log_total = row_top + jnp.log(jnp.sum(jnp.exp(scores - row_top), axis=-1, keepdims=True))
    probs_low = jnp.exp(scores - log_total).astype(low)
    head_mix = jnp.einsum("skgql,slkd->sqkgd", probs_low, value_whole, preferred_element_type=wide)
    head_mix = head_mix.reshape(row_count, qwidth).astype(low)
    middle = residual + jnp.dot(head_mix, w_out, preferred_element_type=wide)
    inv_two, normed_two = norm_forward(middle, norm_two)
    normed_two = normed_two.astype(low)
    gate_pre = jnp.dot(normed_two, w_gate, preferred_element_type=wide)
    up_proj = jnp.dot(normed_two, w_up, preferred_element_type=wide)
    gate_sigmoid = jax.nn.sigmoid(gate_pre)
    active = (gate_pre * gate_sigmoid * up_proj).astype(low)
    block_rows = middle + jnp.dot(active, w_down, preferred_element_type=wide)
    one_cols, mix_cols, two_cols, active_cols = (
        lax.all_to_all(normed_one, "ctx", split_axis=1, concat_axis=0, tiled=True),
        lax.all_to_all(head_mix, "ctx", split_axis=1, concat_axis=0, tiled=True),
        lax.all_to_all(normed_two, "ctx", split_axis=1, concat_axis=0, tiled=True),
        lax.all_to_all(active, "ctx", split_axis=1, concat_axis=0, tiled=True),
    )
    cot_rows = cotangent.reshape(row_count, model_width)
    cot_low = cot_rows.astype(low)
    grad_active = jnp.dot(cot_low, w_down.T, preferred_element_type=wide)
    grad_gate = (
        grad_active * up_proj * gate_sigmoid * (1.0 + gate_pre * (1.0 - gate_sigmoid))
    ).astype(low)
    grad_up = (grad_active * gate_pre * gate_sigmoid).astype(low)
    grad_normed_two = jnp.dot(grad_gate, w_gate.T, preferred_element_type=wide) + jnp.dot(
        grad_up, w_up.T, preferred_element_type=wide
    )
    grad_middle, grad_gain_two = norm_backward(middle, inv_two, norm_two, grad_normed_two)
    grad_middle = cot_rows + grad_middle
    grad_mid_low = grad_middle.astype(low)
    grad_mix = jnp.dot(grad_mid_low, w_out.T, preferred_element_type=wide).astype(low)
    grad_mix = grad_mix.reshape(seq_count, local_len, KV_HEADS, groups, HEAD_DIM)
    attn_probs = jnp.exp(masked_scores(query_rot, key_whole, allowed, score_scale) - log_total)
    probs_low = attn_probs.astype(low)
    grad_probs = jnp.einsum("sqkgd,slkd->skgql", grad_mix, value_whole, preferred_element_type=wide)
    grad_value_all = jnp.einsum(
        "skgql,sqkgd->slkd", probs_low, grad_mix, preferred_element_type=wide
    )
    grad_scores = attn_probs * (
        grad_probs - jnp.sum(attn_probs * grad_probs, axis=-1, keepdims=True)
    )
    grad_scores_low = (grad_scores * score_scale).astype(low)
    grad_query = jnp.einsum(
        "skgql,slkd->sqkgd", grad_scores_low, key_whole, preferred_element_type=wide
    )
    grad_key_all = jnp.einsum(
        "skgql,sqkgd->slkd", grad_scores_low, query_rot, preferred_element_type=wide
    )
    kv_terms = jnp.concatenate(
        [
            grad_key_all.reshape(seq_count, seq_len, kwidth),
            grad_value_all.reshape(seq_count, seq_len, kwidth),
        ],
        axis=2,
    )
    kv_owned = lax.psum_scatter(
        kv_terms.astype(jnp.bfloat16), "ctx", scatter_dimension=1, tiled=True
    ).astype(jnp.float32)
    grad_key = kv_owned[:, :, :kwidth].reshape(row_count, KV_HEADS, HEAD_DIM)
    grad_value = kv_owned[:, :, kwidth:].reshape(row_count, kwidth).astype(low)
    grad_query = (
        unrotate(grad_query.reshape(row_count, HEADS, HEAD_DIM), cosine_table, sine_table)
        .reshape(row_count, qwidth)
        .astype(low)
    )
    grad_key = unrotate(grad_key, cosine_table, sine_table).reshape(row_count, kwidth).astype(low)
    grad_normed_one = (
        jnp.dot(grad_query, w_query.T, preferred_element_type=wide)
        + jnp.dot(grad_key, w_key.T, preferred_element_type=wide)
        + jnp.dot(grad_value, w_value.T, preferred_element_type=wide)
    )
    grad_resid, grad_gain_one = norm_backward(residual, inv_one, norm_one, grad_normed_one)
    grad_resid = grad_middle + grad_resid
    gathered = (
        lax.all_gather(grad_query, "ctx", axis=0, tiled=True),
        lax.all_gather(grad_key, "ctx", axis=0, tiled=True),
        lax.all_gather(grad_value, "ctx", axis=0, tiled=True),
        lax.all_gather(grad_mid_low, "ctx", axis=0, tiled=True),
        lax.all_gather(grad_gate, "ctx", axis=0, tiled=True),
        lax.all_gather(grad_up, "ctx", axis=0, tiled=True),
        lax.all_gather(cot_low, "ctx", axis=0, tiled=True),
    )
    all_query, all_key, all_value, all_mid, all_gate, all_up, all_cot = gathered
    attn_terms = jnp.concatenate(
        [
            left_dot(one_cols, all_query).reshape(-1),
            left_dot(one_cols, all_key).reshape(-1),
            left_dot(one_cols, all_value).reshape(-1),
            left_dot(mix_cols, all_mid).reshape(-1),
        ]
    ).reshape(-1, 128)
    mlp_terms = jnp.concatenate(
        [
            left_dot(two_cols, all_gate).reshape(-1),
            left_dot(two_cols, all_up).reshape(-1),
            left_dot(active_cols, all_cot).reshape(-1),
        ]
    ).reshape(-1, 128)
    attn_grad, mlp_grad = (
        lax.psum_scatter(
            attn_terms.astype(jnp.bfloat16), "dp", scatter_dimension=0, tiled=True
        ).astype(jnp.float32),
        lax.psum_scatter(
            mlp_terms.astype(jnp.bfloat16), "dp", scatter_dimension=0, tiled=True
        ).astype(jnp.float32),
    )
    gain_sums = lax.psum(jnp.stack([grad_gain_one, grad_gain_two]), ("dp", "ctx"))
    return (
        block_rows.reshape(seq_count, local_len, model_width),
        grad_resid.reshape(seq_count, local_len, model_width),
        attn_grad,
        mlp_grad,
        gain_sums[0],
        gain_sums[1],
    )


def gain_total(gain_rows):
    total = gain_rows
    for step in range(1, lax.axis_size("ctx")):
        total = total + lax.ppermute(gain_rows, "ctx", swap_pairs("ctx", step))
    step = 1
    while step < lax.axis_size("dp"):
        total = total + lax.ppermute(total, "dp", swap_pairs("dp", step))
        step = 2 * step
    return total


def swap_pairs(axis, step):
    return [(place, place ^ step) for place in range(lax.axis_size(axis))]


def spread(rows):
    return [rows] + [
        lax.ppermute(rows, "ctx", swap_pairs("ctx", step)) for step in range(1, lax.axis_size("ctx"))
    ]


def returned(terms):
    return [
        lax.ppermute(term, "ctx", swap_pairs("ctx", step + 1)) for step, term in enumerate(terms)
    ]


def trade(blocks):
    here = lax.axis_index("ctx")
    got = [lax.dynamic_index_in_dim(blocks, here, 0, False)]
    for step in range(1, lax.axis_size("ctx")):
        block = lax.dynamic_index_in_dim(blocks, here ^ step, 0, False)
        got.append(lax.ppermute(block, "ctx", swap_pairs("ctx", step)))
    return got


def in_order(pieces):
    here = lax.axis_index("ctx")
    step = 1
    while step < len(pieces):
        bit = (here & step) != 0
        pieces = [
            jnp.where(bit, pieces[place ^ step], pieces[place]) for place in range(len(pieces))
        ]
        step = 2 * step
    return jnp.stack(pieces)


def columns_apply(dp_count, ctx_count, rows):
    unit = FFN // 128
    return (
        rows % unit == 0
        and FFN % (128 * ctx_count) == 0
        and D % ctx_count == 0
        and ctx_count & (ctx_count - 1) == 0
        and dp_count & (dp_count - 1) == 0
        and rows % ctx_count == 0
        and (2 * (D // ctx_count) % (rows // unit)) * unit % ctx_count == 0
        and (rows - (2 * (D // ctx_count) % (rows // unit)) * unit) % (ctx_count * 2 * D // 128) == 0
        and rows % (2 * D // 128) == 0
    )


def mlp_sizes(rows, ctx_count):
    unit = FFN // 128
    held = rows // unit
    tall = 2 * (D // ctx_count)
    return unit, unit // ctx_count, held, tall // held, tall % held


def trade_mlp(flat):
    ctx_count = lax.axis_size("ctx")
    place = lax.axis_index("dp")
    rows = flat.shape[0]
    unit, part, held, edge, rest = mlp_sizes(rows, ctx_count)
    cut = rest * unit

    def by_column(block, count):
        return (
            block.reshape(count, ctx_count, part, 128)
            .transpose(1, 0, 2, 3)
            .reshape(ctx_count, count * part, 128)
        )

    full = by_column(flat, held)
    tail = flat[cut:].reshape(ctx_count, -1, 128)
    mixed = jnp.concatenate([by_column(flat[:cut], rest), tail], axis=1)
    got = in_order(trade(jnp.where(place < edge, full, mixed)))
    kept = jnp.concatenate([got[:, : rest * part], tail], axis=1)
    block = jnp.where(
        place < edge, got, jnp.where(place == edge, kept, flat.reshape(ctx_count, -1, 128))
    )
    return block.reshape(rows, 128)


def scatter_mlp(terms):
    ctx_count = lax.axis_size("ctx")
    place = lax.axis_index("dp")
    rows = terms.shape[0] // lax.axis_size("dp")
    unit, part, held, edge, rest = mlp_sizes(rows, ctx_count)
    own = lax.psum_scatter(terms, "dp", scatter_dimension=0, tiled=True)
    blocks = own.reshape(ctx_count, rows // ctx_count, 128)
    got = in_order(trade(blocks))

    def by_row(block, count):
        return block.reshape(ctx_count, count, part, 128).transpose(1, 0, 2, 3).reshape(-1, 128)

    full = by_row(got, held)
    mixed = jnp.concatenate(
        [by_row(got[:, : rest * part], rest), blocks[:, rest * part :].reshape(-1, 128)], axis=0
    )
    out = jnp.where(place < edge, full, jnp.where(place == edge, mixed, own))
    return out.astype(jnp.float32)


VMEM_BYTES = 56 * 1024 * 1024
LANES = 128
HALF = LANES // 2


def kernel_call(kernel, outs, scratch, *args):
    return pl.pallas_call(
        kernel,
        out_shape=[jax.ShapeDtypeStruct(shape, dtype) for shape, dtype in outs],
        scratch_shapes=[pltpu.VMEM(shape, dtype) for shape, dtype in scratch],
        compiler_params=pltpu.CompilerParams(vmem_limit_bytes=VMEM_BYTES),
    )(*args)


def low_lanes(rows):
    return lax.broadcasted_iota(jnp.int32, (rows, LANES), 1) < HALF


def dot_nt(left, right):
    return lax.dot_general(
        left, right, (((1,), (1,)), ((), ())), preferred_element_type=jnp.float32
    )


def dot_nn(left, right):
    return jnp.dot(left, right, preferred_element_type=jnp.float32)


def pair_rows(flat_ref, base, pairs, width, offset, put):
    halves = width // HALF
    tiles = [flat_ref[pl.ds(base + step, pairs, stride=halves), :] for step in range(halves)]
    rolled = {}
    mask = low_lanes(pairs)

    def roll(index):
        index = min(max(index, 0), halves - 1)
        if index not in rolled:
            rolled[index] = pltpu.roll(tiles[index], HALF, 1)
        return rolled[index]

    for parity in range(2):
        for tile in range((halves + offset + 1) // 2):
            first = parity * halves - offset + 2 * tile
            if first % 2 == 0:
                put(tile, parity, tiles[first // 2])
            else:
                put(tile, parity, jnp.where(mask, roll(first // 2), roll(first // 2 + 1)))


def flat_rows(get, flat_ref, base, pairs, width, offset):
    halves = width // HALF
    mask = low_lanes(pairs)
    blocks, rolled = {}, {}

    def half(index, want):
        parity, index = divmod(index, halves)
        tile, side = divmod(index + offset, 2)
        key = (tile, parity)
        if key not in blocks:
            blocks[key] = get(tile, parity)
        if side == want:
            return blocks[key]
        if key not in rolled:
            rolled[key] = pltpu.roll(blocks[key], HALF, 1)
        return rolled[key]

    for step in range(halves):
        left, right = half(2 * step, 0), half(2 * step + 1, 1)
        flat_ref[pl.ds(base + step, pairs, stride=halves), :] = (
            left if left is right else jnp.where(mask, left, right)
        )


def partner_lanes(block):
    quarter = HEAD_DIM // 2
    lane = lax.broadcasted_iota(jnp.int32, block.shape, 1)
    return jnp.where(
        (lane & quarter) == 0,
        pltpu.roll(block, LANES - quarter, 1),
        pltpu.roll(block, quarter, 1),
    )


def attn_pieces(rows, dp_count, ctx_count):
    runs = []
    begin = 0
    for height, width in (
        (D, HEADS * HEAD_DIM),
        (D, KV_HEADS * HEAD_DIM),
        (D, KV_HEADS * HEAD_DIM),
        (HEADS * HEAD_DIM, D),
    ):
        block = height // ctx_count
        span = block * width // LANES
        matrix = []
        for ctx in range(ctx_count):
            at = begin
            while at < begin + span:
                part, inside = divmod(at, rows)
                size = min(rows - inside, begin + span - at)
                matrix.append(
                    (
                        ctx * block + (at - begin) * LANES // width,
                        size * LANES // width,
                        (part * ctx_count + ctx) * rows + inside,
                        size,
                    )
                )
                at = at + size
        runs.append(matrix)
        begin = begin + span
    return runs


def attn_fits(rows, dp_count, ctx_count):
    widths = (HEADS * HEAD_DIM, KV_HEADS * HEAD_DIM, KV_HEADS * HEAD_DIM, D)
    return D % ctx_count == 0 and all(
        (2 * width) % LANES == 0
        and (width // HALF) % 2 == 1
        and size % (2 * width // LANES) == 0
        and row % 2 == 0
        for width, matrix in zip(widths, attn_pieces(rows, dp_count, ctx_count))
        for row, _, _, size in matrix
    )


def project(flat, residual, gain, cosine, sine, rows, dp_count, ctx_count):
    tokens = residual.shape[0]
    qwidth, kwidth = HEADS * HEAD_DIM, KV_HEADS * HEAD_DIM
    whole = qwidth + 2 * kwidth
    runs = attn_pieces(rows, dp_count, ctx_count)
    total = flat.shape[0]
    qtiles = -(-qwidth // LANES)
    ktile, koff = divmod(qwidth // HALF, 2)
    vtile, voff = divmod((qwidth + kwidth) // HALF, 2)
    ktiles = (kwidth // HALF + koff + 1) // 2
    vtiles = (kwidth // HALF + voff + 1) // 2

    def kernel(
        flat_ref, res_ref, gain_ref, cos_ref, sin_ref,
        normed_ref, query_ref, kv_ref, wide_ref, out_ref, long_ref, tile_ref,
    ):
        long_ref[...] = flat_ref[...].astype(jnp.float32)
        places = ((0, 0, 0), (qtiles, koff, ktile), (qtiles + ktiles, voff, vtile))
        for (slot, offset, _), matrix, width in zip(places, runs, (qwidth, kwidth, kwidth)):
            for row, count, base, size in matrix:
                def put(tile, parity, block, slot=slot, row=row, count=count):
                    tile_ref[slot + tile, pl.ds(row + parity, count // 2, stride=2), :] = block

                pair_rows(long_ref, base, count // 2, width, offset, put)
        mask = low_lanes(D)
        for tile in range(-(-whole // LANES)):
            held = [
                tile_ref[slot + tile - first]
                for (slot, _, first), count in zip(places, (qtiles, ktiles, vtiles))
                if first <= tile < first + count
            ]
            block = held[0] if len(held) == 1 else jnp.where(mask, held[0], held[1])
            width = min(LANES, whole - tile * LANES)
            wide_ref[:, tile * LANES : tile * LANES + width] = block[:, :width].astype(jnp.bfloat16)
        residual = res_ref[...]
        inverse = lax.rsqrt(jnp.mean(residual * residual, axis=-1, keepdims=True) + EPS)
        normed = (residual * inverse * gain_ref[...]).astype(jnp.bfloat16)
        normed_ref[...] = normed
        product = dot_nn(normed, wide_ref[...])
        turned = []
        for tile in range((qwidth + kwidth) // LANES):
            block = product[:, tile * LANES : (tile + 1) * LANES]
            turned.append(
                (block * cos_ref[...] + partner_lanes(block) * sin_ref[...]).astype(jnp.bfloat16)
            )
        turned = jnp.concatenate(turned, axis=1)
        query_ref[...] = turned[:, :qwidth]
        kv_ref[:, :kwidth] = turned[:, qwidth:]
        kv_ref[:, kwidth:] = product[:, qwidth + kwidth :].astype(jnp.bfloat16)
        for row, count, base, size in runs[3]:
            def put(tile, parity, block, row=row, count=count):
                tile_ref[tile, pl.ds(row + parity, count // 2, stride=2), :] = block

            pair_rows(long_ref, base, count // 2, D, 0, put)
        for tile in range(-(-D // LANES)):
            width = min(LANES, D - tile * LANES)
            out_ref[:, tile * LANES : tile * LANES + width] = tile_ref[tile][:, :width].astype(
                jnp.bfloat16
            )

    low = jnp.bfloat16
    return kernel_call(
        kernel,
        [
            ((tokens, D), low),
            ((tokens, qwidth), low),
            ((tokens, 2 * kwidth), low),
            ((D, whole), low),
            ((qwidth, D), low),
        ],
        [((total, LANES), jnp.float32), ((qtiles + ktiles + vtiles, D, LANES), jnp.float32)],
        flat, residual, gain, cosine, sine,
    )


def group_rows(ref, group, groups):
    first = group * groups * HEAD_DIM
    return jnp.concatenate(
        [ref[:, first + g * HEAD_DIM : first + (g + 1) * HEAD_DIM] for g in range(groups)], axis=0
    )


def group_allowed(seg_ref, near_ref, tokens, near_len, groups):
    query = lax.broadcasted_iota(jnp.int32, (tokens, near_len), 0)
    key = lax.broadcasted_iota(jnp.int32, (tokens, near_len), 1) - (near_len - tokens)
    allowed = (seg_ref[...] == near_ref[...]) & (key <= query)
    return allowed


def attend(query, kv_parts, seg_col, seg_near, residual, w_out, gain):
    tokens = query.shape[0]
    parts = len(kv_parts)
    near_len = parts * tokens
    groups = HEADS // KV_HEADS
    kwidth = KV_HEADS * HEAD_DIM
    scale = HEAD_DIM ** (-0.5)

    def kernel(*refs):
        query_ref = refs[0]
        kv_refs = refs[1 : 1 + parts]
        seg_ref, near_ref, res_ref, out_ref, gain_ref = refs[1 + parts : 6 + parts]
        near_kv_ref, mix_ref, log_ref, mid_ref, normed_ref = refs[6 + parts :]
        for part in range(parts):
            near_kv_ref[part * tokens : (part + 1) * tokens, :] = kv_refs[part][...]
        allowed = group_allowed(seg_ref, near_ref, tokens, near_len, groups)
        allowed = jnp.concatenate([allowed.astype(jnp.float32)] * groups, axis=0) > 0.5
        mixes, logs = [], []
        for group in range(KV_HEADS):
            at = group * HEAD_DIM
            key = near_kv_ref[:, at : at + HEAD_DIM]
            value = near_kv_ref[:, kwidth + at : kwidth + at + HEAD_DIM]
            scores = dot_nt(group_rows(query_ref, group, groups), key) * scale
            scores = jnp.where(allowed, scores, -jnp.inf)
            top = jnp.max(scores, axis=-1, keepdims=True)
            total = top + jnp.log(jnp.sum(jnp.exp(scores - top), axis=-1, keepdims=True))
            probs = jnp.exp(scores - total).astype(jnp.bfloat16)
            mix = dot_nn(probs, value).astype(jnp.bfloat16)
            for g in range(groups):
                mixes.append(mix[g * tokens : (g + 1) * tokens])
                logs.append(total[g * tokens : (g + 1) * tokens])
        for head in range(HEADS):
            log_ref[:, head : head + 1] = logs[head]
        head_mix = jnp.concatenate(mixes, axis=1)
        mix_ref[...] = head_mix
        middle = res_ref[...] + dot_nn(head_mix, out_ref[...])
        mid_ref[...] = middle
        inverse = lax.rsqrt(jnp.mean(middle * middle, axis=-1, keepdims=True) + EPS)
        normed_ref[...] = (middle * inverse * gain_ref[...]).astype(jnp.bfloat16)

    low, wide = jnp.bfloat16, jnp.float32
    return kernel_call(
        kernel,
        [
            ((near_len, 2 * kwidth), low),
            ((tokens, HEADS * HEAD_DIM), low),
            ((tokens, LANES), wide),
            ((tokens, D), wide),
            ((tokens, D), low),
        ],
        [],
        query, *kv_parts, seg_col, seg_near, residual, w_out, gain,
    )


def mlp_pieces(rows, dp_count, ctx_count):
    unit, part, held, edge, rest = mlp_sizes(rows, ctx_count)
    share = rows // ctx_count
    block = D // ctx_count
    gate, up, down = [], [], []
    for ctx in range(ctx_count):
        for dp in range(edge + (rest > 0)):
            count = held if dp < edge else rest
            row, stop = dp * held, dp * held + count
            base = (dp * ctx_count + ctx) * share
            for matrix, begin, end in ((gate, 0, block), (up, block, 2 * block)):
                low, high = max(row, begin), min(stop, end)
                if low < high:
                    matrix.append((ctx * block + low - begin, high - low, base + (low - row) * part))
    cut = rest * part
    at = 0
    for ctx in range(ctx_count):
        size = share - cut
        down.append((at * LANES // D, size * LANES // D, (edge * ctx_count + ctx) * share + cut))
        at = at + size
    for dp in range(edge + 1, dp_count):
        down.append((at * LANES // D, rows * LANES // D, dp * rows))
        at = at + rows
    return part, gate, up, down


def unpack_mlp(flat, cot_slots, rows, dp_count, ctx_count):
    part, gate, up, down = mlp_pieces(rows, dp_count, ctx_count)
    hidden = part * LANES
    tiles = -(-D // LANES)
    tokens = cot_slots[0].shape[0]
    count = len(cot_slots)

    def kernel(flat_ref, *refs):
        cot_refs = refs[:count]
        gate_ref, up_ref, down_ref, act_ref, long_ref, tile_ref, turn_ref = refs[count:]
        long_ref[...] = flat_ref[...].astype(jnp.float32)
        for row, size, base in down:
            def put(tile, parity, block, row=row, size=size):
                tile_ref[tile, pl.ds(row + parity, size // 2, stride=2), :] = block

            pair_rows(long_ref, base, size // 2, D, 0, put)
        for tile in range(tiles):
            width = min(LANES, D - tile * LANES)
            down_ref[:, tile * LANES : tile * LANES + width] = tile_ref[tile][:, :width].astype(
                jnp.bfloat16
            )
        for slot in range(count):
            act_ref[slot * tokens : (slot + 1) * tokens, :] = dot_nt(
                cot_refs[slot][...], down_ref[...]
            )
        for runs, ref in ((gate, gate_ref), (up, up_ref)):
            for row, size, base in runs:
                for step in range(part):
                    turn_ref[step, row : row + size, :] = long_ref[
                        pl.ds(base + step, size, stride=part), :
                    ]
            for step in range(part):
                ref[:, step * LANES : (step + 1) * LANES] = turn_ref[step].astype(jnp.bfloat16)

    low, wide = jnp.bfloat16, jnp.float32
    return kernel_call(
        kernel,
        [
            ((D, hidden), low),
            ((D, hidden), low),
            ((hidden, D), low),
            ((count * tokens, hidden), wide),
        ],
        [
            (flat.shape, wide),
            ((tiles, hidden, LANES), wide),
            ((part, D, LANES), wide),
        ],
        flat, *cot_slots,
    )


def feed_forward(two_slots, w_gate, w_up, grad_active):
    count = len(two_slots)
    tokens = two_slots[0].shape[0]
    hidden = w_gate.shape[1]

    def kernel(*refs):
        two_refs = refs[:count]
        gate_ref, up_ref, act_ref = refs[count : count + 3]
        active_ref, dgate_ref, dup_ref, own_ref = refs[count + 3 : count + 7]
        term_refs = refs[count + 7 :]
        for slot in list(range(1, count)) + [0]:
            rows = slice(slot * tokens, (slot + 1) * tokens)
            two = two_refs[slot][...]
            gate = dot_nn(two, gate_ref[...])
            up = dot_nn(two, up_ref[...])
            grad = act_ref[rows, :]
            sigmoid = jax.nn.sigmoid(gate)
            active_ref[rows, :] = (gate * sigmoid * up).astype(jnp.bfloat16)
            dgate = (grad * up * sigmoid * (1.0 + gate * (1.0 - sigmoid))).astype(jnp.bfloat16)
            dup = (grad * gate * sigmoid).astype(jnp.bfloat16)
            dgate_ref[rows, :] = dgate
            dup_ref[rows, :] = dup
            term = dot_nt(dgate, gate_ref[...]) + dot_nt(dup, up_ref[...])
            if slot:
                term_refs[slot - 1][...] = term.astype(jnp.bfloat16)
            else:
                own_ref[...] = term

    low, wide = jnp.bfloat16, jnp.float32
    return kernel_call(
        kernel,
        [((count * tokens, hidden), low)] * 3
        + [((tokens, D), wide)]
        + [((tokens, D), low)] * (count - 1),
        [],
        *two_slots, w_gate, w_up, grad_active,
    )


def mlp_grads(active, dgate, dup, two_slots, cot_slots, w_down, rows, dp_count, ctx_count):
    count = len(two_slots)
    tokens = two_slots[0].shape[0]
    part, gate_runs, up_runs, down_runs = mlp_pieces(rows, dp_count, ctx_count)
    tiles = -(-D // LANES)
    hidden = part * LANES

    def kernel(*refs):
        active_ref, dgate_ref, dup_ref = refs[:3]
        two_refs = refs[3 : 3 + count]
        cot_refs = refs[3 + count : 3 + 2 * count]
        down_ref = refs[3 + 2 * count]
        flat_ref, own_ref = refs[4 + 2 * count : 6 + 2 * count]
        term_refs = refs[6 + 2 * count : 5 + 3 * count]
        long_ref, tile_ref, turn_ref = refs[5 + 3 * count :]
        for slot in range(count):
            term = dot_nn(active_ref[slot * tokens : (slot + 1) * tokens, :], down_ref[...])
            if slot:
                term_refs[slot - 1][...] = term.astype(jnp.bfloat16)
            else:
                own_ref[...] = term
        two = jnp.concatenate([ref[...] for ref in two_refs], axis=0)
        for runs, grad_ref in ((gate_runs, dgate_ref), (up_runs, dup_ref)):
            value = left_dot(two, grad_ref[...])
            for step in range(part):
                turn_ref[step] = value[:, step * LANES : (step + 1) * LANES]
            for row, size, base in runs:
                for step in range(part):
                    long_ref[pl.ds(base + step, size, stride=part), :] = turn_ref[
                        step, row : row + size, :
                    ]
        cot = jnp.concatenate([ref[...] for ref in cot_refs], axis=0)
        value = left_dot(active_ref[...], cot)
        for tile in range(tiles):
            width = min(LANES, D - tile * LANES)
            tile_ref[tile, :, :width] = value[:, tile * LANES : tile * LANES + width]
        for row, size, base in down_runs:
            def get(tile, parity, row=row, size=size):
                return tile_ref[tile, pl.ds(row + parity, size // 2, stride=2), :]

            flat_rows(get, long_ref, base, size // 2, D, 0)
        flat_ref[...] = long_ref[...].astype(jnp.bfloat16)

    low, wide = jnp.bfloat16, jnp.float32
    total = rows * dp_count
    return kernel_call(
        kernel,
        [((total, LANES), low), ((tokens, D), wide)] + [((tokens, D), low)] * (count - 1),
        [((total, LANES), wide), ((tiles, hidden, LANES), wide), ((part, D, LANES), wide)],
        active, dgate, dup, *two_slots, *cot_slots, w_down,
    )


def middle_backward(own, others, middle, gain, cot_rows, w_out):
    tokens = own.shape[0]
    count = len(others)

    def kernel(own_ref, *refs):
        other_refs = refs[:count]
        mid_ref, gain_ref, cot_ref, out_ref = refs[count : count + 4]
        grad_ref, low_ref, mix_ref, sum_ref = refs[count + 4 :]
        grad = own_ref[...]
        for ref in other_refs:
            grad = grad + ref[...].astype(jnp.float32)
        middle = mid_ref[...]
        inverse = lax.rsqrt(jnp.mean(middle * middle, axis=-1, keepdims=True) + EPS)
        scaled = grad * gain_ref[...]
        cubed = inverse * inverse * inverse
        result = cot_ref[...] + (
            inverse * scaled - middle * cubed * jnp.mean(scaled * middle, axis=-1, keepdims=True)
        )
        grad_ref[...] = result
        low_ref[...] = result.astype(jnp.bfloat16)
        mix_ref[...] = dot_nt(low_ref[...], out_ref[...]).astype(jnp.bfloat16)
        sum_ref[...] = jnp.sum(grad * middle * inverse, axis=0, keepdims=True)

    low, wide = jnp.bfloat16, jnp.float32
    return kernel_call(
        kernel,
        [
            ((tokens, D), wide),
            ((tokens, D), low),
            ((tokens, HEADS * HEAD_DIM), low),
            ((1, D), wide),
        ],
        [],
        own, *others, middle, gain, cot_rows, w_out,
    )


def attend_backward(query, near_kv, grad_mix, logs, seg_col, seg_near, cosine, sine):
    tokens = query.shape[0]
    near_len = near_kv.shape[0]
    parts = near_len // tokens
    groups = HEADS // KV_HEADS
    qwidth, kwidth = HEADS * HEAD_DIM, KV_HEADS * HEAD_DIM
    scale = HEAD_DIM ** (-0.5)
    tiles = -(-qwidth // LANES)

    def kernel(
        query_ref, kv_ref, mix_ref, log_ref, seg_ref, near_ref, cos_ref, sin_ref, dquery_ref, own_ref,
        *rest,
    ):
        part_refs = rest[: parts - 1]
        turn_ref, term_ref = rest[parts - 1 :]
        allowed = group_allowed(seg_ref, near_ref, tokens, near_len, groups)
        allowed = jnp.concatenate([allowed.astype(jnp.float32)] * groups, axis=0) > 0.5
        if tiles * LANES > qwidth:
            turn_ref[:, qwidth:] = jnp.zeros((tokens, tiles * LANES - qwidth), jnp.float32)
        for group in range(KV_HEADS):
            at = group * HEAD_DIM
            key = kv_ref[:, at : at + HEAD_DIM]
            value = kv_ref[:, kwidth + at : kwidth + at + HEAD_DIM]
            queries = group_rows(query_ref, group, groups)
            mixes = group_rows(mix_ref, group, groups)
            total = jnp.concatenate(
                [log_ref[:, group * groups + g : group * groups + g + 1] for g in range(groups)],
                axis=0,
            )
            scores = dot_nt(queries, key) * scale
            probs = jnp.exp(jnp.where(allowed, scores, -jnp.inf) - total)
            grad_probs = dot_nt(mixes, value)
            grad_scores = probs * (grad_probs - jnp.sum(probs * grad_probs, axis=-1, keepdims=True))
            grad_scores = (grad_scores * scale).astype(jnp.bfloat16)
            dquery = dot_nn(grad_scores, key)
            for g in range(groups):
                first = (group * groups + g) * HEAD_DIM
                turn_ref[:, first : first + HEAD_DIM] = dquery[g * tokens : (g + 1) * tokens]
            term_ref[:, at : at + HEAD_DIM] = left_dot(grad_scores, queries)
            term_ref[:, kwidth + at : kwidth + at + HEAD_DIM] = left_dot(
                probs.astype(jnp.bfloat16), mixes
            )
        for part in range(parts - 1):
            part_refs[part][...] = term_ref[part * tokens : (part + 1) * tokens, :].astype(
                jnp.bfloat16
            )
        own_ref[...] = term_ref[near_len - tokens :, :]
        for tile in range(tiles):
            width = min(LANES, qwidth - tile * LANES)
            block = turn_ref[:, tile * LANES : (tile + 1) * LANES]
            block = block * cos_ref[...] - partner_lanes(block) * sin_ref[...]
            dquery_ref[:, tile * LANES : tile * LANES + width] = block[:, :width].astype(
                jnp.bfloat16
            )

    low, wide = jnp.bfloat16, jnp.float32
    return kernel_call(
        kernel,
        [((tokens, qwidth), low), ((tokens, 2 * kwidth), wide)]
        + [((tokens, 2 * kwidth), low)] * (parts - 1),
        [((tokens, tiles * LANES), wide), ((near_len, 2 * kwidth), wide)],
        query, near_kv, grad_mix, logs, seg_col, seg_near, cosine, sine,
    )


def own_kv(own, others, cosine, sine):
    tokens = own.shape[0]
    kwidth = KV_HEADS * HEAD_DIM

    def kernel(own_ref, *refs):
        other_refs, (cos_ref, sin_ref, out_ref) = refs[:-3], refs[-3:]
        total = own_ref[...]
        for ref in other_refs:
            total = total + ref[...].astype(jnp.float32)
        for tile in range(2 * kwidth // LANES):
            block = total[:, tile * LANES : (tile + 1) * LANES]
            if tile * LANES < kwidth:
                turned = block * cos_ref[...] - partner_lanes(block) * sin_ref[...]
                lane = lax.broadcasted_iota(jnp.int32, block.shape, 1)
                block = jnp.where(lane < kwidth - tile * LANES, turned, block)
            out_ref[:, tile * LANES : (tile + 1) * LANES] = block.astype(jnp.bfloat16)

    return kernel_call(
        kernel, [((tokens, 2 * kwidth), jnp.bfloat16)], [], own, *others, cosine, sine
    )[0]


def input_backward(grad_query, grad_kv, w_qkv, residual, gain, grad_middle):
    tokens = residual.shape[0]
    qwidth = HEADS * HEAD_DIM
    whole = w_qkv.shape[1]

    def kernel(query_ref, kv_ref, w_ref, res_ref, gain_ref, mid_ref, grad_ref, sum_ref, row_ref):
        row_ref[:, :qwidth] = query_ref[...]
        row_ref[:, qwidth:] = kv_ref[...]
        grad = dot_nt(row_ref[...], w_ref[...])
        residual = res_ref[...]
        inverse = lax.rsqrt(jnp.mean(residual * residual, axis=-1, keepdims=True) + EPS)
        scaled = grad * gain_ref[...]
        cubed = inverse * inverse * inverse
        grad_ref[...] = mid_ref[...] + (
            inverse * scaled
            - residual * cubed * jnp.mean(scaled * residual, axis=-1, keepdims=True)
        )
        sum_ref[...] = jnp.sum(grad * residual * inverse, axis=0, keepdims=True)

    return kernel_call(
        kernel,
        [((tokens, D), jnp.float32), ((1, D), jnp.float32)],
        [((tokens, whole), jnp.bfloat16)],
        grad_query, grad_kv, w_qkv, residual, gain, grad_middle,
    )


def attn_grads(one_slots, mix_slots, query_slots, kv_slots, mid_slots, rows, dp_count):
    count = len(one_slots)
    block = one_slots[0].shape[1]
    qwidth, kwidth = HEADS * HEAD_DIM, KV_HEADS * HEAD_DIM
    tiles = -(-max(qwidth, D) // LANES)
    total = rows * dp_count

    def kernel(*refs):
        ones, mixes, queries, kvs, mids = [
            jnp.concatenate([ref[...] for ref in refs[k * count : (k + 1) * count]], axis=0)
            for k in range(5)
        ]
        flat_ref, long_ref, tile_ref = refs[5 * count :]
        base = 0
        for left, right, parts in (
            (ones, queries, ((0, qwidth),)),
            (ones, kvs, ((0, kwidth), (kwidth, kwidth))),
            (mixes, mids, ((0, D),)),
        ):
            value = left_dot(left, right)
            span = value.shape[1]
            for tile in range(-(-span // LANES)):
                width = min(LANES, span - tile * LANES)
                tile_ref[tile, :, :width] = value[:, tile * LANES : tile * LANES + width]
            for first, width in parts:
                lead, offset = divmod(first // HALF, 2)

                def get(tile, parity, lead=lead):
                    return tile_ref[lead + tile, pl.ds(parity, block // 2, stride=2), :]

                flat_rows(get, long_ref, base, block // 2, width, offset)
                base = base + block * width // LANES
        flat_ref[...] = long_ref[...].astype(jnp.bfloat16)

    return kernel_call(
        kernel,
        [((total, LANES), jnp.bfloat16)],
        [((total, LANES), jnp.float32), ((tiles, block, LANES), jnp.float32)],
        *one_slots, *mix_slots, *query_slots, *kv_slots, *mid_slots,
    )[0]


def body(hidden_in, segments, attn_flat, mlp_flat, norm_one, norm_two, cotangent):
    dp_count, ctx_count = lax.axis_size("dp"), lax.axis_size("ctx")
    if not (
        hidden_in.shape[0] == 1
        and columns_apply(dp_count, ctx_count, mlp_flat.shape[0])
        and attn_fits(attn_flat.shape[0], dp_count, ctx_count)
    ):
        return body_rows(hidden_in, segments, attn_flat, mlp_flat, norm_one, norm_two, cotangent)
    return body_columns(hidden_in, segments, attn_flat, mlp_flat, norm_one, norm_two, cotangent)


def body_columns(hidden_in, segments, attn_flat, mlp_flat, norm_one, norm_two, cotangent):
    tokens = hidden_in.shape[1]
    seq_len = segments.shape[1]
    low = jnp.bfloat16
    dp_count = lax.axis_size("dp")
    ctx_count = lax.axis_size("ctx")
    attn_rows, mlp_rows = attn_flat.shape[0], mlp_flat.shape[0]
    back = -(-(seq_len // 2 - 1) // tokens)
    start_row = lax.axis_index("ctx") * tokens

    attn_near = in_order(spread(attn_flat)).reshape(-1, 128)
    mlp_near = trade_mlp(mlp_flat)
    attn_whole = lax.all_gather(attn_near, "dp", axis=0, tiled=True)
    mlp_near, attn_whole = lax.optimization_barrier((mlp_near, attn_whole))
    mlp_whole = lax.all_gather(mlp_near, "dp", axis=0, tiled=True)

    pos_local = lax.dynamic_slice_in_dim(positions_of(segments), start_row, tokens, 1)
    seg_col = lax.dynamic_slice_in_dim(segments, start_row, tokens, 1).reshape(tokens, 1)
    seg_near = lax.dynamic_slice_in_dim(
        jnp.pad(segments, ((0, 0), (back * tokens, 0)), constant_values=-1),
        start_row,
        (back + 1) * tokens,
        1,
    )
    cosine, sine = [table[:, 0] for table in rope_tables(pos_local.reshape(-1))]
    heads = 128 // HEAD_DIM
    cosine = jnp.concatenate([cosine, cosine] * heads, axis=1)
    sine = jnp.concatenate([-sine, sine] * heads, axis=1)
    gain_one, gain_two = norm_one.reshape(1, D), norm_two.reshape(1, D)

    residual = hidden_in.reshape(tokens, D)
    cot_rows = cotangent.reshape(tokens, D)
    cot_slots = spread(cot_rows.astype(low))

    def cols(rows):
        return trade(rows.reshape(tokens, ctx_count, -1).transpose(1, 0, 2))

    normed_one, query, kv_local, w_qkv, w_out = project(
        attn_whole, residual, gain_one, cosine, sine, attn_rows, dp_count, ctx_count
    )
    one_slots = cols(normed_one)
    up_pairs = [
        [(place, place + step) for place in range(ctx_count - step)] for step in range(back + 1)
    ]
    down_pairs = [[(right, left) for left, right in pairs] for pairs in up_pairs]
    kv_parts = [
        lax.ppermute(kv_local, "ctx", up_pairs[step]) for step in range(back, 0, -1)
    ] + [kv_local]
    near_kv, head_mix, logs, middle, normed_two = attend(
        query, kv_parts, seg_col, seg_near, residual, w_out, gain_two
    )
    two_slots = spread(normed_two)
    mix_slots = cols(head_mix)

    w_gate, w_up, w_down, grad_active = unpack_mlp(
        mlp_whole, cot_slots, mlp_rows, dp_count, ctx_count
    )
    active, grad_gate, grad_up, *two_terms = feed_forward(two_slots, w_gate, w_up, grad_active)
    two_others = returned(two_terms[1:])
    mlp_terms, block_own, *block_terms = mlp_grads(
        active, grad_gate, grad_up, two_slots, cot_slots, w_down, mlp_rows, dp_count, ctx_count
    )
    block_rows = middle + block_own
    for moved in returned(block_terms):
        block_rows = block_rows + moved.astype(jnp.float32)
    mlp_grad = scatter_mlp(mlp_terms)

    grad_middle, grad_mid_low, grad_mix, grad_gain_two = middle_backward(
        two_terms[0], two_others, middle, gain_two, cot_rows, w_out
    )
    mid_slots = spread(grad_mid_low)
    grad_query, kv_own, *kv_terms = attend_backward(
        query, near_kv, grad_mix, logs, seg_col, seg_near, cosine, sine
    )
    kv_others = [
        lax.ppermute(kv_terms[back - step], "ctx", down_pairs[step]) for step in range(1, back + 1)
    ]
    grad_kv = own_kv(kv_own, kv_others, cosine, sine)
    query_slots = spread(grad_query)
    kv_slots = spread(grad_kv)
    attn_terms = attn_grads(
        one_slots, mix_slots, query_slots, kv_slots, mid_slots, attn_rows, dp_count
    )
    attn_grad = lax.psum_scatter(attn_terms, "dp", scatter_dimension=0, tiled=True)
    grad_in, grad_gain_one = input_backward(
        grad_query, grad_kv, w_qkv, residual, gain_one, grad_middle
    )
    gain_sums = gain_total(jnp.concatenate([grad_gain_one, grad_gain_two], axis=0))
    return (
        block_rows.reshape(hidden_in.shape),
        grad_in.reshape(hidden_in.shape),
        attn_grad.astype(jnp.float32),
        mlp_grad,
        gain_sums[0],
        gain_sums[1],
    )


def solution(mesh):
    in_specs = (
        P("dp", "ctx", None),
        P("dp", None),
        P(("dp", "ctx"), None),
        P(("dp", "ctx"), None),
        P(),
        P(),
        P("dp", "ctx", None),
    )
    out_specs = (
        P("dp", "ctx", None),
        P("dp", "ctx", None),
        P(("dp", "ctx"), None),
        P(("dp", "ctx"), None),
        P(),
        P(),
    )
    return jax.shard_map(body, mesh=mesh, in_specs=in_specs, out_specs=out_specs, check_vma=False)
```

```python
import jax
import jax.numpy as jnp
from jax import lax
from jax.experimental import pallas as pl
from jax.experimental.pallas import tpu as pltpu
from jax.sharding import PartitionSpec as P

D = 960
HEADS = 15
KV_HEADS = 5
HEAD_DIM = 64
FFN = 2560


EPS = 1e-05
THETA = 100000.0


def positions_of(segment_ids):
    earlier = (segment_ids[..., None, :] < segment_ids[..., :, None]).astype(jnp.int32)
    total_len = segment_ids.shape[-1]
    return jnp.arange(total_len, dtype=jnp.int32) - jnp.sum(earlier, axis=-1)


def rope_tables(positions):
    half_dim = HEAD_DIM // 2
    frequency = THETA ** (-2.0 * jnp.arange(half_dim, dtype=jnp.float32) / HEAD_DIM)
    angles = positions.astype(jnp.float32)[:, None] * frequency[None, :]
    return (jnp.cos(angles)[:, None, :], jnp.sin(angles)[:, None, :])


def rotate(vectors, cosine_table, sine_table):
    half_dim = vectors.shape[-1] // 2
    lower_half = vectors[..., :half_dim]
    upper_half = vectors[..., half_dim:]
    return jnp.concatenate(
        [
            lower_half * cosine_table - upper_half * sine_table,
            upper_half * cosine_table + lower_half * sine_table,
        ],
        axis=-1,
    )


def unrotate(grad_rows, cosine_table, sine_table):
    half_dim = grad_rows.shape[-1] // 2
    lower_half = grad_rows[..., :half_dim]
    upper_half = grad_rows[..., half_dim:]
    return jnp.concatenate(
        [
            lower_half * cosine_table + upper_half * sine_table,
            upper_half * cosine_table - lower_half * sine_table,
        ],
        axis=-1,
    )


def unpack_blocks(flat_rows, shapes, dp_count, ctx_count):
    pieces = flat_rows.reshape(dp_count, ctx_count, -1).transpose(1, 0, 2).reshape(ctx_count, -1)
    matrices = []
    offset = 0
    for height, width_cols in shapes:
        length = height * width_cols // ctx_count
        matrices.append(pieces[:, offset : offset + length].reshape(height, width_cols))
        offset = offset + length
    return matrices


def norm_forward(residual, gain_vec):
    inverse = lax.rsqrt(jnp.mean(residual * residual, axis=-1, keepdims=True) + EPS)
    return (inverse, residual * inverse * gain_vec)


def norm_backward(residual, inverse, gain_vec, grad_normed):
    scaled = grad_normed * gain_vec
    cubed = inverse * inverse * inverse
    grad_resid = inverse * scaled - residual * cubed * jnp.mean(
        scaled * residual, axis=-1, keepdims=True
    )
    grad_gain = jnp.sum(grad_normed * residual * inverse, axis=0)
    return (grad_resid, grad_gain)


def masked_scores(query_rot, key_whole, allowed, score_scale):
    scores = (
        jnp.einsum("sqkgd,slkd->skgql", query_rot, key_whole, preferred_element_type=jnp.float32)
        * score_scale
    )
    return jnp.where(allowed, scores, -jnp.inf)


def left_dot(left_cols, right_rows):
    return lax.dot_general(
        left_cols, right_rows, (((0,), (0,)), ((), ())), preferred_element_type=jnp.float32
    )


def body_rows(hidden_in, segments, attn_flat, mlp_flat, norm_one, norm_two, cotangent):
    seq_count, local_len, model_width = hidden_in.shape
    seq_len = segments.shape[1]
    row_count = seq_count * local_len
    groups = HEADS // KV_HEADS
    qwidth = HEADS * HEAD_DIM
    kwidth = KV_HEADS * HEAD_DIM
    score_scale = HEAD_DIM ** (-0.5)
    low = jnp.bfloat16
    wide = jnp.float32
    dp_count = lax.axis_size("dp")
    ctx_count = lax.axis_size("ctx")
    attn_shapes = ((D, qwidth), (D, kwidth), (D, kwidth), (qwidth, D))
    mlp_shapes = ((D, FFN), (D, FFN), (FFN, D))
    start_row = lax.axis_index("ctx") * local_len
    attn_whole, mlp_whole = (
        lax.all_gather(attn_flat, ("dp", "ctx"), axis=0, tiled=True),
        lax.all_gather(mlp_flat, ("dp", "ctx"), axis=0, tiled=True),
    )
    w_query, w_key, w_value, w_out = unpack_blocks(attn_whole, attn_shapes, dp_count, ctx_count)
    w_gate, w_up, w_down = unpack_blocks(mlp_whole, mlp_shapes, dp_count, ctx_count)
    pos_all = positions_of(segments)
    pos_local = lax.dynamic_slice_in_dim(pos_all, start_row, local_len, 1)
    seg_local = lax.dynamic_slice_in_dim(segments, start_row, local_len, 1)
    cosine_table, sine_table = rope_tables(pos_local.reshape(-1))
    key_index = jnp.arange(seq_len, dtype=jnp.int32)
    query_index = start_row + jnp.arange(local_len, dtype=jnp.int32)
    allowed = (seg_local[:, :, None] == segments[:, None, :]) & (
        key_index[None, None, :] <= query_index[None, :, None]
    )
    allowed = allowed[:, None, None]
    residual = hidden_in.reshape(row_count, model_width)
    inv_one, normed_one = norm_forward(residual, norm_one)
    normed_one = normed_one.astype(low)
    query = jnp.dot(normed_one, w_query, preferred_element_type=wide).reshape(
        row_count, HEADS, HEAD_DIM
    )
    key_raw = jnp.dot(normed_one, w_key, preferred_element_type=wide).reshape(
        row_count, KV_HEADS, HEAD_DIM
    )
    value_low = jnp.dot(normed_one, w_value, preferred_element_type=wide).astype(low)
    query_rot = (
        rotate(query, cosine_table, sine_table)
        .astype(low)
        .reshape(seq_count, local_len, KV_HEADS, groups, HEAD_DIM)
    )
    key_rot = rotate(key_raw, cosine_table, sine_table).astype(low)
    kv_local = jnp.concatenate(
        [
            key_rot.reshape(seq_count, local_len, kwidth),
            value_low.reshape(seq_count, local_len, kwidth),
        ],
        axis=2,
    )
    kv_whole = lax.all_gather(kv_local, "ctx", axis=1, tiled=True)
    key_whole = kv_whole[:, :, :kwidth].reshape(seq_count, seq_len, KV_HEADS, HEAD_DIM)
    value_whole = kv_whole[:, :, kwidth:].reshape(seq_count, seq_len, KV_HEADS, HEAD_DIM)
    scores = masked_scores(query_rot, key_whole, allowed, score_scale)
    row_top = jnp.max(scores, axis=-1, keepdims=True)
    log_total = row_top + jnp.log(jnp.sum(jnp.exp(scores - row_top), axis=-1, keepdims=True))
    probs_low = jnp.exp(scores - log_total).astype(low)
    head_mix = jnp.einsum("skgql,slkd->sqkgd", probs_low, value_whole, preferred_element_type=wide)
    head_mix = head_mix.reshape(row_count, qwidth).astype(low)
    middle = residual + jnp.dot(head_mix, w_out, preferred_element_type=wide)
    inv_two, normed_two = norm_forward(middle, norm_two)
    normed_two = normed_two.astype(low)
    gate_pre = jnp.dot(normed_two, w_gate, preferred_element_type=wide)
    up_proj = jnp.dot(normed_two, w_up, preferred_element_type=wide)
    gate_sigmoid = jax.nn.sigmoid(gate_pre)
    active = (gate_pre * gate_sigmoid * up_proj).astype(low)
    block_rows = middle + jnp.dot(active, w_down, preferred_element_type=wide)
    one_cols, mix_cols, two_cols, active_cols = (
        lax.all_to_all(normed_one, "ctx", split_axis=1, concat_axis=0, tiled=True),
        lax.all_to_all(head_mix, "ctx", split_axis=1, concat_axis=0, tiled=True),
        lax.all_to_all(normed_two, "ctx", split_axis=1, concat_axis=0, tiled=True),
        lax.all_to_all(active, "ctx", split_axis=1, concat_axis=0, tiled=True),
    )
    cot_rows = cotangent.reshape(row_count, model_width)
    cot_low = cot_rows.astype(low)
    grad_active = jnp.dot(cot_low, w_down.T, preferred_element_type=wide)
    grad_gate = (
        grad_active * up_proj * gate_sigmoid * (1.0 + gate_pre * (1.0 - gate_sigmoid))
    ).astype(low)
    grad_up = (grad_active * gate_pre * gate_sigmoid).astype(low)
    grad_normed_two = jnp.dot(grad_gate, w_gate.T, preferred_element_type=wide) + jnp.dot(
        grad_up, w_up.T, preferred_element_type=wide
    )
    grad_middle, grad_gain_two = norm_backward(middle, inv_two, norm_two, grad_normed_two)
    grad_middle = cot_rows + grad_middle
    grad_mid_low = grad_middle.astype(low)
    grad_mix = jnp.dot(grad_mid_low, w_out.T, preferred_element_type=wide).astype(low)
    grad_mix = grad_mix.reshape(seq_count, local_len, KV_HEADS, groups, HEAD_DIM)
    attn_probs = jnp.exp(masked_scores(query_rot, key_whole, allowed, score_scale) - log_total)
    probs_low = attn_probs.astype(low)
    grad_probs = jnp.einsum("sqkgd,slkd->skgql", grad_mix, value_whole, preferred_element_type=wide)
    grad_value_all = jnp.einsum(
        "skgql,sqkgd->slkd", probs_low, grad_mix, preferred_element_type=wide
    )
    grad_scores = attn_probs * (
        grad_probs - jnp.sum(attn_probs * grad_probs, axis=-1, keepdims=True)
    )
    grad_scores_low = (grad_scores * score_scale).astype(low)
    grad_query = jnp.einsum(
        "skgql,slkd->sqkgd", grad_scores_low, key_whole, preferred_element_type=wide
    )
    grad_key_all = jnp.einsum(
        "skgql,sqkgd->slkd", grad_scores_low, query_rot, preferred_element_type=wide
    )
    kv_terms = jnp.concatenate(
        [
            grad_key_all.reshape(seq_count, seq_len, kwidth),
            grad_value_all.reshape(seq_count, seq_len, kwidth),
        ],
        axis=2,
    )
    kv_owned = lax.psum_scatter(
        kv_terms.astype(jnp.bfloat16), "ctx", scatter_dimension=1, tiled=True
    ).astype(jnp.float32)
    grad_key = kv_owned[:, :, :kwidth].reshape(row_count, KV_HEADS, HEAD_DIM)
    grad_value = kv_owned[:, :, kwidth:].reshape(row_count, kwidth).astype(low)
    grad_query = (
        unrotate(grad_query.reshape(row_count, HEADS, HEAD_DIM), cosine_table, sine_table)
        .reshape(row_count, qwidth)
        .astype(low)
    )
    grad_key = unrotate(grad_key, cosine_table, sine_table).reshape(row_count, kwidth).astype(low)
    grad_normed_one = (
        jnp.dot(grad_query, w_query.T, preferred_element_type=wide)
        + jnp.dot(grad_key, w_key.T, preferred_element_type=wide)
        + jnp.dot(grad_value, w_value.T, preferred_element_type=wide)
    )
    grad_resid, grad_gain_one = norm_backward(residual, inv_one, norm_one, grad_normed_one)
    grad_resid = grad_middle + grad_resid
    gathered = (
        lax.all_gather(grad_query, "ctx", axis=0, tiled=True),
        lax.all_gather(grad_key, "ctx", axis=0, tiled=True),
        lax.all_gather(grad_value, "ctx", axis=0, tiled=True),
        lax.all_gather(grad_mid_low, "ctx", axis=0, tiled=True),
        lax.all_gather(grad_gate, "ctx", axis=0, tiled=True),
        lax.all_gather(grad_up, "ctx", axis=0, tiled=True),
        lax.all_gather(cot_low, "ctx", axis=0, tiled=True),
    )
    all_query, all_key, all_value, all_mid, all_gate, all_up, all_cot = gathered
    attn_terms = jnp.concatenate(
        [
            left_dot(one_cols, all_query).reshape(-1),
            left_dot(one_cols, all_key).reshape(-1),
            left_dot(one_cols, all_value).reshape(-1),
            left_dot(mix_cols, all_mid).reshape(-1),
        ]
    ).reshape(-1, 128)
    mlp_terms = jnp.concatenate(
        [
            left_dot(two_cols, all_gate).reshape(-1),
            left_dot(two_cols, all_up).reshape(-1),
            left_dot(active_cols, all_cot).reshape(-1),
        ]
    ).reshape(-1, 128)
    attn_grad, mlp_grad = (
        lax.psum_scatter(
            attn_terms.astype(jnp.bfloat16), "dp", scatter_dimension=0, tiled=True
        ).astype(jnp.float32),
        lax.psum_scatter(
            mlp_terms.astype(jnp.bfloat16), "dp", scatter_dimension=0, tiled=True
        ).astype(jnp.float32),
    )
    gain_sums = lax.psum(jnp.stack([grad_gain_one, grad_gain_two]), ("dp", "ctx"))
    return (
        block_rows.reshape(seq_count, local_len, model_width),
        grad_resid.reshape(seq_count, local_len, model_width),
        attn_grad,
        mlp_grad,
        gain_sums[0],
        gain_sums[1],
    )


def add_swapped(rows, axis, masks):
    total = rows
    for mask in masks:
        total = total + lax.ppermute(rows, axis, swap_pairs(axis, mask))
    return total


def swap_pairs(axis, step):
    return [(place, place ^ step) for place in range(lax.axis_size(axis))]


def spread(rows):
    return [rows] + [
        lax.ppermute(rows, "ctx", swap_pairs("ctx", step)) for step in range(1, lax.axis_size("ctx"))
    ]


def returned(terms):
    return [
        lax.ppermute(term, "ctx", swap_pairs("ctx", step + 1)) for step, term in enumerate(terms)
    ]


def trade(blocks, *before):
    here = lax.axis_index("ctx")
    got = [lax.dynamic_index_in_dim(blocks, here, 0, False)]
    for step in range(1, lax.axis_size("ctx")):
        block = lax.dynamic_index_in_dim(blocks, here ^ step, 0, False)
        block = after(block, *before)
        got.append(lax.ppermute(block, "ctx", swap_pairs("ctx", step)))
    return got


def in_order(pieces):
    here = lax.axis_index("ctx")
    step = 1
    while step < len(pieces):
        bit = (here & step) != 0
        pieces = [
            jnp.where(bit, pieces[place ^ step], pieces[place]) for place in range(len(pieces))
        ]
        step = 2 * step
    return jnp.stack(pieces)


def columns_apply(dp_count, ctx_count, rows):
    unit = FFN // 128
    return (
        rows % unit == 0
        and FFN % (128 * ctx_count) == 0
        and D % ctx_count == 0
        and ctx_count & (ctx_count - 1) == 0
        and dp_count & (dp_count - 1) == 0
        and rows % ctx_count == 0
        and (2 * (D // ctx_count) % (rows // unit)) * unit % ctx_count == 0
        and (rows - (2 * (D // ctx_count) % (rows // unit)) * unit) % (ctx_count * 2 * D // 128) == 0
        and rows % (2 * D // 128) == 0
    )


def mlp_sizes(rows, ctx_count):
    unit = FFN // 128
    held = rows // unit
    tall = 2 * (D // ctx_count)
    return unit, unit // ctx_count, held, tall // held, tall % held


def trade_mlp(flat, *before):
    ctx_count = lax.axis_size("ctx")
    place = lax.axis_index("dp")
    rows = flat.shape[0]
    unit, part, held, edge, rest = mlp_sizes(rows, ctx_count)
    cut = rest * unit

    def by_column(block, count):
        return (
            block.reshape(count, ctx_count, part, 128)
            .transpose(1, 0, 2, 3)
            .reshape(ctx_count, count * part, 128)
        )

    full = by_column(flat, held)
    tail = flat[cut:].reshape(ctx_count, -1, 128)
    mixed = jnp.concatenate([by_column(flat[:cut], rest), tail], axis=1)
    got = in_order(trade(jnp.where(place < edge, full, mixed), *before))
    kept = jnp.concatenate([got[:, : rest * part], tail], axis=1)
    block = jnp.where(
        place < edge, got, jnp.where(place == edge, kept, flat.reshape(ctx_count, -1, 128))
    )
    return block.reshape(rows, 128)


def scatter_mlp(own):
    ctx_count = lax.axis_size("ctx")
    place = lax.axis_index("dp")
    rows = own.shape[0]
    unit, part, held, edge, rest = mlp_sizes(rows, ctx_count)
    blocks = own.reshape(ctx_count, rows // ctx_count, 128)
    got = in_order(trade(blocks))

    def by_row(block, count):
        return block.reshape(ctx_count, count, part, 128).transpose(1, 0, 2, 3).reshape(-1, 128)

    full = by_row(got, held)
    mixed = jnp.concatenate(
        [by_row(got[:, : rest * part], rest), blocks[:, rest * part :].reshape(-1, 128)], axis=0
    )
    out = jnp.where(place < edge, full, jnp.where(place == edge, mixed, own))
    return out.astype(jnp.float32)


VMEM_BYTES = 56 * 1024 * 1024
LANES = 128
HALF = LANES // 2
GRAIN = 160


def kernel_call(kernel, outs, scratch, *args, places=None):
    specs = [pl.BlockSpec(memory_space=pltpu.VMEM) for _ in args]
    if places is not None:
        specs = [pl.BlockSpec(memory_space=pltpu.SMEM)] + specs
        args = (places,) + args
    return pl.pallas_call(
        kernel,
        in_specs=specs,
        out_shape=[jax.ShapeDtypeStruct(shape, dtype) for shape, dtype in outs],
        scratch_shapes=[pltpu.VMEM(shape, dtype) for shape, dtype in scratch],
        compiler_params=pltpu.CompilerParams(vmem_limit_bytes=VMEM_BYTES),
    )(*args)


def low_lanes(rows):
    return lax.broadcasted_iota(jnp.int32, (rows, LANES), 1) < HALF


def dot_nt(left, right):
    return lax.dot_general(
        left, right, (((1,), (1,)), ((), ())), preferred_element_type=jnp.float32
    )


def dot_nn(left, right):
    return jnp.dot(left, right, preferred_element_type=jnp.float32)


def pair_rows(flat_ref, base, pairs, width, offset, put):
    halves = width // HALF
    tiles = [flat_ref[pl.ds(base + step, pairs, stride=halves), :] for step in range(halves)]
    rolled = {}
    mask = low_lanes(pairs)

    def roll(index):
        index = min(max(index, 0), halves - 1)
        if index not in rolled:
            rolled[index] = pltpu.roll(tiles[index], HALF, 1)
        return rolled[index]

    for parity in range(2):
        for tile in range((halves + offset + 1) // 2):
            first = parity * halves - offset + 2 * tile
            if first % 2 == 0:
                put(tile, parity, tiles[first // 2])
            else:
                put(tile, parity, jnp.where(mask, roll(first // 2), roll(first // 2 + 1)))


def flat_rows(get, flat_ref, base, pairs, width, offset):
    halves = width // HALF
    mask = low_lanes(pairs)
    blocks, rolled = {}, {}

    def half(index, want):
        parity, index = divmod(index, halves)
        tile, side = divmod(index + offset, 2)
        key = (tile, parity)
        if key not in blocks:
            blocks[key] = get(tile, parity)
        if side == want:
            return blocks[key]
        if key not in rolled:
            rolled[key] = pltpu.roll(blocks[key], HALF, 1)
        return rolled[key]

    for step in range(halves):
        left, right = half(2 * step, 0), half(2 * step + 1, 1)
        flat_ref[pl.ds(base + step, pairs, stride=halves), :] = (
            left if left is right else jnp.where(mask, left, right)
        )


def partner_lanes(block):
    quarter = HEAD_DIM // 2
    lane = lax.broadcasted_iota(jnp.int32, block.shape, 1)
    return jnp.where(
        (lane & quarter) == 0,
        pltpu.roll(block, LANES - quarter, 1),
        pltpu.roll(block, quarter, 1),
    )


def attn_pieces(rows, dp_count, ctx_count, stride=None):
    runs = []
    begin = 0
    for height, width in (
        (D, HEADS * HEAD_DIM),
        (D, KV_HEADS * HEAD_DIM),
        (D, KV_HEADS * HEAD_DIM),
        (HEADS * HEAD_DIM, D),
    ):
        block = height // ctx_count
        span = block * width // LANES
        matrix = []
        for ctx in range(ctx_count):
            at = begin
            while at < begin + span:
                part, inside = divmod(at, rows)
                size = min(rows - inside, begin + span - at)
                matrix.append(
                    (
                        ctx * block + (at - begin) * LANES // width,
                        size * LANES // width,
                        (part * ctx_count + ctx) * (stride or rows) + inside,
                        size,
                    )
                )
                at = at + size
        runs.append(matrix)
        begin = begin + span
    return runs


def attn_fits(rows, dp_count, ctx_count):
    widths = (HEADS * HEAD_DIM, KV_HEADS * HEAD_DIM, KV_HEADS * HEAD_DIM, D)
    return D % ctx_count == 0 and all(
        (2 * width) % LANES == 0
        and (width // HALF) % 2 == 1
        and size % (2 * width // LANES) == 0
        and row % 2 == 0
        and (rows * ctx_count) % GRAIN == 0
        for width, matrix in zip(widths, attn_pieces(rows, dp_count, ctx_count))
        for row, _, _, size in matrix
    )


def project(places, held, normed_parts, cosine, sine, used, rows, dp_count, ctx_count):
    parts = len(normed_parts)
    tokens = normed_parts[-1].shape[0]
    near_len = parts * tokens
    qwidth, kwidth = HEADS * HEAD_DIM, KV_HEADS * HEAD_DIM
    whole = qwidth + 2 * kwidth
    runs = attn_pieces(used, dp_count, ctx_count, rows)
    total = rows * dp_count * ctx_count
    qtiles = -(-qwidth // LANES)
    ktile, koff = divmod(qwidth // HALF, 2)
    vtile, voff = divmod((qwidth + kwidth) // HALF, 2)
    ktiles = (kwidth // HALF + koff + 1) // 2
    vtiles = (kwidth // HALF + voff + 1) // 2

    def kernel(place_ref, *refs):
        held_refs = refs[: len(held)]
        normed_refs = refs[len(held) : len(held) + parts]
        cos_ref, sin_ref = refs[len(held) + parts : len(held) + parts + 2]
        query_ref, kv_ref, wide_ref, out_ref, long_ref, tile_ref = refs[len(held) + parts + 2 :]
        for (dp_mask, ctx_masks, _), ref in zip(held, held_refs):
            def move(step, carry, dp_mask=dp_mask, lead=ctx_masks[0], ref=ref):
                block = (place_ref[0] ^ dp_mask) * ctx_count + (place_ref[1] ^ (lead + step // 2))
                first = pl.multiple_of(block * rows + (step % 2) * (rows // 2), 16)
                long_ref[pl.ds(first, rows // 2), :] = ref[
                    pl.ds(pl.multiple_of(step * (rows // 2), 16), rows // 2), :
                ].astype(jnp.float32)
                return carry

            lax.fori_loop(0, 2 * len(ctx_masks), move, 0)
        slots = ((0, 0, 0), (qtiles, koff, ktile), (qtiles + ktiles, voff, vtile))
        for (slot, offset, _), matrix, width in zip(slots, runs, (qwidth, kwidth, kwidth)):
            for row, count, base, size in matrix:
                def put(tile, parity, block, slot=slot, row=row, count=count):
                    tile_ref[slot + tile, pl.ds(row + parity, count // 2, stride=2), :] = block

                pair_rows(long_ref, base, count // 2, width, offset, put)
        mask = low_lanes(D)
        for tile in range(-(-whole // LANES)):
            found = [
                tile_ref[slot + tile - first]
                for (slot, _, first), count in zip(slots, (qtiles, ktiles, vtiles))
                if first <= tile < first + count
            ]
            block = found[0] if len(found) == 1 else jnp.where(mask, found[0], found[1])
            width = min(LANES, whole - tile * LANES)
            wide_ref[:, tile * LANES : tile * LANES + width] = block[:, :width].astype(jnp.bfloat16)
        product = dot_nn(normed_refs[-1][...], wide_ref[:, : qtiles * LANES])
        here = slice(near_len - tokens, near_len)
        for tile in range(qtiles):
            width = min(LANES, qwidth - tile * LANES)
            block = product[:, tile * LANES : (tile + 1) * LANES]
            block = block * cos_ref[here, :] + partner_lanes(block) * sin_ref[here, :]
            query_ref[:, tile * LANES : tile * LANES + width] = block[:, :width].astype(jnp.bfloat16)
        near = jnp.concatenate([ref[...] for ref in normed_refs], axis=0)
        product = dot_nn(near, wide_ref[:, ktile * LANES :])
        lead = qwidth - ktile * LANES
        turned = []
        for tile in range((lead + kwidth) // LANES):
            block = product[:, tile * LANES : (tile + 1) * LANES]
            turned.append(
                (block * cos_ref[...] + partner_lanes(block) * sin_ref[...]).astype(jnp.bfloat16)
            )
        kv_ref[:, :kwidth] = jnp.concatenate(turned, axis=1)[:, lead:]
        kv_ref[:, kwidth:] = product[:, lead + kwidth :].astype(jnp.bfloat16)
        for row, count, base, size in runs[3]:
            def put(tile, parity, block, row=row, count=count):
                tile_ref[tile, pl.ds(row + parity, count // 2, stride=2), :] = block

            pair_rows(long_ref, base, count // 2, D, 0, put)
        for tile in range(-(-D // LANES)):
            width = min(LANES, D - tile * LANES)
            out_ref[:, tile * LANES : tile * LANES + width] = tile_ref[tile][:, :width].astype(
                jnp.bfloat16
            )

    low = jnp.bfloat16
    return kernel_call(
        kernel,
        [
            ((tokens, qwidth), low),
            ((near_len, 2 * kwidth), low),
            ((D, whole), low),
            ((qwidth, D), low),
        ],
        [((total, LANES), jnp.float32), ((qtiles + ktiles + vtiles, D, LANES), jnp.float32)],
        *[array for _, _, array in held], *normed_parts, cosine, sine,
        places=places,
    )


def group_rows(ref, group, groups):
    first = group * groups * HEAD_DIM
    return jnp.concatenate(
        [ref[:, first + g * HEAD_DIM : first + (g + 1) * HEAD_DIM] for g in range(groups)], axis=0
    )


def group_allowed(seg_ref, near_ref, tokens, near_len, groups):
    query = lax.broadcasted_iota(jnp.int32, (tokens, near_len), 0)
    key = lax.broadcasted_iota(jnp.int32, (tokens, near_len), 1) - (near_len - tokens)
    allowed = (seg_ref[...] == near_ref[...]) & (key <= query)
    return allowed


def attend(query, near_kv, seg_col, seg_near, residual, w_out, gain):
    tokens = query.shape[0]
    near_len = near_kv.shape[0]
    groups = HEADS // KV_HEADS
    kwidth = KV_HEADS * HEAD_DIM
    scale = HEAD_DIM ** (-0.5)

    def kernel(
        query_ref, near_kv_ref, seg_ref, near_ref, res_ref, out_ref, gain_ref,
        mix_ref, log_ref, mid_ref, normed_ref,
    ):
        allowed = group_allowed(seg_ref, near_ref, tokens, near_len, groups)
        allowed = jnp.concatenate([allowed.astype(jnp.float32)] * groups, axis=0) > 0.5
        mixes, logs = [], []
        for group in range(KV_HEADS):
            at = group * HEAD_DIM
            key = near_kv_ref[:, at : at + HEAD_DIM]
            value = near_kv_ref[:, kwidth + at : kwidth + at + HEAD_DIM]
            scores = dot_nt(group_rows(query_ref, group, groups), key) * scale
            scores = jnp.where(allowed, scores, -jnp.inf)
            top = jnp.max(scores, axis=-1, keepdims=True)
            total = top + jnp.log(jnp.sum(jnp.exp(scores - top), axis=-1, keepdims=True))
            probs = jnp.exp(scores - total).astype(jnp.bfloat16)
            mix = dot_nn(probs, value).astype(jnp.bfloat16)
            for g in range(groups):
                mixes.append(mix[g * tokens : (g + 1) * tokens])
                logs.append(total[g * tokens : (g + 1) * tokens])
        for head in range(HEADS):
            log_ref[:, head : head + 1] = logs[head]
        head_mix = jnp.concatenate(mixes, axis=1)
        mix_ref[...] = head_mix
        middle = res_ref[...] + dot_nn(head_mix, out_ref[...])
        mid_ref[...] = middle
        inverse = lax.rsqrt(jnp.mean(middle * middle, axis=-1, keepdims=True) + EPS)
        normed_ref[...] = (middle * inverse * gain_ref[...]).astype(jnp.bfloat16)

    low, wide = jnp.bfloat16, jnp.float32
    return kernel_call(
        kernel,
        [
            ((tokens, HEADS * HEAD_DIM), low),
            ((tokens, LANES), wide),
            ((tokens, D), wide),
            ((tokens, D), low),
        ],
        [],
        query, near_kv, seg_col, seg_near, residual, w_out, gain,
    )


def mlp_pieces(rows, dp_count, ctx_count):
    unit, part, held, edge, rest = mlp_sizes(rows, ctx_count)
    share = rows // ctx_count
    block = D // ctx_count
    gate, up, down = [], [], []
    for ctx in range(ctx_count):
        for dp in range(edge + (rest > 0)):
            count = held if dp < edge else rest
            row, stop = dp * held, dp * held + count
            base = (dp * ctx_count + ctx) * share
            for matrix, begin, end in ((gate, 0, block), (up, block, 2 * block)):
                low, high = max(row, begin), min(stop, end)
                if low < high:
                    matrix.append((ctx * block + low - begin, high - low, base + (low - row) * part))
    cut = rest * part
    at = 0
    for ctx in range(ctx_count):
        size = share - cut
        down.append((at * LANES // D, size * LANES // D, (edge * ctx_count + ctx) * share + cut))
        at = at + size
    for dp in range(edge + 1, dp_count):
        down.append((at * LANES // D, rows * LANES // D, dp * rows))
        at = at + rows
    return part, gate, up, down


def unpack_mlp(flat, cot_slots, rows, dp_count, ctx_count):
    part, gate, up, down = mlp_pieces(rows, dp_count, ctx_count)
    hidden = part * LANES
    tiles = -(-D // LANES)
    tokens = cot_slots[0].shape[0]
    count = len(cot_slots)

    def kernel(flat_ref, *refs):
        cot_refs = refs[:count]
        gate_ref, up_ref, down_ref, act_ref, long_ref, tile_ref, turn_ref = refs[count:]
        long_ref[...] = flat_ref[...].astype(jnp.float32)
        for row, size, base in down:
            def put(tile, parity, block, row=row, size=size):
                tile_ref[tile, pl.ds(row + parity, size // 2, stride=2), :] = block

            pair_rows(long_ref, base, size // 2, D, 0, put)
        for tile in range(tiles):
            width = min(LANES, D - tile * LANES)
            down_ref[:, tile * LANES : tile * LANES + width] = tile_ref[tile][:, :width].astype(
                jnp.bfloat16
            )
        for slot in range(count):
            act_ref[slot * tokens : (slot + 1) * tokens, :] = dot_nt(
                cot_refs[slot][...], down_ref[...]
            )
        for runs, ref in ((gate, gate_ref), (up, up_ref)):
            for row, size, base in runs:
                for step in range(part):
                    turn_ref[step, row : row + size, :] = long_ref[
                        pl.ds(base + step, size, stride=part), :
                    ]
            for step in range(part):
                ref[:, step * LANES : (step + 1) * LANES] = turn_ref[step].astype(jnp.bfloat16)

    low, wide = jnp.bfloat16, jnp.float32
    return kernel_call(
        kernel,
        [
            ((D, hidden), low),
            ((D, hidden), low),
            ((hidden, D), low),
            ((count * tokens, hidden), wide),
        ],
        [
            (flat.shape, wide),
            ((tiles, hidden, LANES), wide),
            ((part, D, LANES), wide),
        ],
        flat, *cot_slots,
    )


def feed_forward(two_slots, w_gate, w_up, grad_active):
    count = len(two_slots)
    tokens = two_slots[0].shape[0]
    hidden = w_gate.shape[1]

    def kernel(*refs):
        two_refs = refs[:count]
        gate_ref, up_ref, act_ref = refs[count : count + 3]
        active_ref, dgate_ref, dup_ref, own_ref = refs[count + 3 : count + 7]
        term_refs = refs[count + 7 :]
        for slot in list(range(1, count)) + [0]:
            rows = slice(slot * tokens, (slot + 1) * tokens)
            two = two_refs[slot][...]
            gate = dot_nn(two, gate_ref[...])
            up = dot_nn(two, up_ref[...])
            grad = act_ref[rows, :]
            sigmoid = jax.nn.sigmoid(gate)
            active_ref[rows, :] = (gate * sigmoid * up).astype(jnp.bfloat16)
            dgate = (grad * up * sigmoid * (1.0 + gate * (1.0 - sigmoid))).astype(jnp.bfloat16)
            dup = (grad * gate * sigmoid).astype(jnp.bfloat16)
            dgate_ref[rows, :] = dgate
            dup_ref[rows, :] = dup
            term = dot_nt(dgate, gate_ref[...]) + dot_nt(dup, up_ref[...])
            if slot:
                term_refs[slot - 1][...] = term.astype(jnp.bfloat16)
            else:
                own_ref[...] = term

    low, wide = jnp.bfloat16, jnp.float32
    return kernel_call(
        kernel,
        [((count * tokens, hidden), low)] * 3
        + [((tokens, D), wide)]
        + [((tokens, D), low)] * (count - 1),
        [],
        *two_slots, w_gate, w_up, grad_active,
    )


def mlp_grads(active, dgate, dup, two_slots, cot_slots, w_down, rows, dp_count, ctx_count):
    count = len(two_slots)
    tokens = two_slots[0].shape[0]
    part, gate_runs, up_runs, down_runs = mlp_pieces(rows, dp_count, ctx_count)
    tiles = -(-D // LANES)
    hidden = part * LANES

    def kernel(*refs):
        active_ref, dgate_ref, dup_ref = refs[:3]
        two_refs = refs[3 : 3 + count]
        cot_refs = refs[3 + count : 3 + 2 * count]
        down_ref = refs[3 + 2 * count]
        flat_ref, own_ref = refs[4 + 2 * count : 6 + 2 * count]
        term_refs = refs[6 + 2 * count : 5 + 3 * count]
        long_ref, tile_ref, turn_ref = refs[5 + 3 * count :]
        for slot in range(count):
            term = dot_nn(active_ref[slot * tokens : (slot + 1) * tokens, :], down_ref[...])
            if slot:
                term_refs[slot - 1][...] = term.astype(jnp.bfloat16)
            else:
                own_ref[...] = term
        two = jnp.concatenate([ref[...] for ref in two_refs], axis=0)
        for runs, grad_ref in ((gate_runs, dgate_ref), (up_runs, dup_ref)):
            value = left_dot(two, grad_ref[...])
            for step in range(part):
                turn_ref[step] = value[:, step * LANES : (step + 1) * LANES]
            for row, size, base in runs:
                for step in range(part):
                    long_ref[pl.ds(base + step, size, stride=part), :] = turn_ref[
                        step, row : row + size, :
                    ]
        cot = jnp.concatenate([ref[...] for ref in cot_refs], axis=0)
        value = left_dot(active_ref[...], cot)
        for tile in range(tiles):
            width = min(LANES, D - tile * LANES)
            tile_ref[tile, :, :width] = value[:, tile * LANES : tile * LANES + width]
        for row, size, base in down_runs:
            def get(tile, parity, row=row, size=size):
                return tile_ref[tile, pl.ds(row + parity, size // 2, stride=2), :]

            flat_rows(get, long_ref, base, size // 2, D, 0)
        flat_ref[...] = long_ref[...].astype(jnp.bfloat16)

    low, wide = jnp.bfloat16, jnp.float32
    total = rows * dp_count
    return kernel_call(
        kernel,
        [((total, LANES), low), ((tokens, D), wide)] + [((tokens, D), low)] * (count - 1),
        [((total, LANES), wide), ((tiles, hidden, LANES), wide), ((part, D, LANES), wide)],
        active, dgate, dup, *two_slots, *cot_slots, w_down,
    )


def middle_backward(own, others, middle, gain, cot_rows, w_out):
    tokens = own.shape[0]
    count = len(others)

    def kernel(own_ref, *refs):
        other_refs = refs[:count]
        mid_ref, gain_ref, cot_ref, out_ref = refs[count : count + 4]
        grad_ref, low_ref, mix_ref, sum_ref = refs[count + 4 :]
        grad = own_ref[...]
        for ref in other_refs:
            grad = grad + ref[...].astype(jnp.float32)
        middle = mid_ref[...]
        inverse = lax.rsqrt(jnp.mean(middle * middle, axis=-1, keepdims=True) + EPS)
        scaled = grad * gain_ref[...]
        cubed = inverse * inverse * inverse
        result = cot_ref[...] + (
            inverse * scaled - middle * cubed * jnp.mean(scaled * middle, axis=-1, keepdims=True)
        )
        grad_ref[...] = result
        low_ref[...] = result.astype(jnp.bfloat16)
        mix_ref[...] = dot_nt(low_ref[...], out_ref[...]).astype(jnp.bfloat16)
        sum_ref[...] = jnp.sum(grad * middle * inverse, axis=0, keepdims=True)

    low, wide = jnp.bfloat16, jnp.float32
    return kernel_call(
        kernel,
        [
            ((tokens, D), wide),
            ((tokens, D), low),
            ((tokens, HEADS * HEAD_DIM), low),
            ((1, D), wide),
        ],
        [],
        own, *others, middle, gain, cot_rows, w_out,
    )


def turn_back(block, tile, cosine, sine):
    width = KV_HEADS * HEAD_DIM - tile * LANES
    if width <= 0:
        return block
    turned = block * cosine - partner_lanes(block) * sine
    if width >= LANES:
        return turned
    lane = lax.broadcasted_iota(jnp.int32, block.shape, 1)
    return jnp.where(lane < width, turned, block)


def attend_backward(query, near_kv, grad_mix, logs, seg_col, seg_near, cosine, sine):
    tokens = query.shape[0]
    near_len = near_kv.shape[0]
    parts = near_len // tokens
    groups = HEADS // KV_HEADS
    qwidth, kwidth = HEADS * HEAD_DIM, KV_HEADS * HEAD_DIM
    scale = HEAD_DIM ** (-0.5)
    tiles = -(-qwidth // LANES)

    def kernel(
        query_ref, kv_ref, mix_ref, log_ref, seg_ref, near_ref, cos_ref, sin_ref, dquery_ref,
        near_out_ref, own_ref, *rest,
    ):
        part_refs = rest[: parts - 1]
        turn_ref, term_ref = rest[parts - 1 :]
        allowed = group_allowed(seg_ref, near_ref, tokens, near_len, groups)
        allowed = jnp.concatenate([allowed.astype(jnp.float32)] * groups, axis=0) > 0.5
        if tiles * LANES > qwidth:
            turn_ref[:, qwidth:] = jnp.zeros((tokens, tiles * LANES - qwidth), jnp.float32)
        for group in range(KV_HEADS):
            at = group * HEAD_DIM
            key = kv_ref[:, at : at + HEAD_DIM]
            value = kv_ref[:, kwidth + at : kwidth + at + HEAD_DIM]
            queries = group_rows(query_ref, group, groups)
            mixes = group_rows(mix_ref, group, groups)
            total = jnp.concatenate(
                [log_ref[:, group * groups + g : group * groups + g + 1] for g in range(groups)],
                axis=0,
            )
            scores = dot_nt(queries, key) * scale
            probs = jnp.exp(jnp.where(allowed, scores, -jnp.inf) - total)
            grad_probs = dot_nt(mixes, value)
            grad_scores = probs * (grad_probs - jnp.sum(probs * grad_probs, axis=-1, keepdims=True))
            grad_scores = (grad_scores * scale).astype(jnp.bfloat16)
            dquery = dot_nn(grad_scores, key)
            for g in range(groups):
                first = (group * groups + g) * HEAD_DIM
                turn_ref[:, first : first + HEAD_DIM] = dquery[g * tokens : (g + 1) * tokens]
            term_ref[:, at : at + HEAD_DIM] = left_dot(grad_scores, queries)
            term_ref[:, kwidth + at : kwidth + at + HEAD_DIM] = left_dot(
                probs.astype(jnp.bfloat16), mixes
            )
        for part in range(parts - 1):
            part_refs[part][...] = term_ref[part * tokens : (part + 1) * tokens, :].astype(
                jnp.bfloat16
            )
        own_ref[...] = term_ref[near_len - tokens :, :]
        for tile in range(2 * kwidth // LANES):
            span = slice(tile * LANES, (tile + 1) * LANES)
            near_out_ref[:, span] = turn_back(
                term_ref[:, span], tile, cos_ref[...], sin_ref[...]
            ).astype(jnp.bfloat16)
        for tile in range(tiles):
            width = min(LANES, qwidth - tile * LANES)
            block = turn_ref[:, tile * LANES : (tile + 1) * LANES]
            here = slice(near_len - tokens, near_len)
            block = block * cos_ref[here, :] - partner_lanes(block) * sin_ref[here, :]
            dquery_ref[:, tile * LANES : tile * LANES + width] = block[:, :width].astype(
                jnp.bfloat16
            )

    low, wide = jnp.bfloat16, jnp.float32
    return kernel_call(
        kernel,
        [((tokens, qwidth), low), ((near_len, 2 * kwidth), low), ((tokens, 2 * kwidth), wide)]
        + [((tokens, 2 * kwidth), low)] * (parts - 1),
        [((tokens, tiles * LANES), wide), ((near_len, 2 * kwidth), wide)],
        query, near_kv, grad_mix, logs, seg_col, seg_near, cosine, sine,
    )


def own_kv(own, others, cosine, sine):
    tokens = own.shape[0]
    kwidth = KV_HEADS * HEAD_DIM

    def kernel(own_ref, *refs):
        other_refs, (cos_ref, sin_ref, out_ref) = refs[:-3], refs[-3:]
        total = own_ref[...]
        for ref in other_refs:
            total = total + ref[...].astype(jnp.float32)
        for tile in range(2 * kwidth // LANES):
            block = total[:, tile * LANES : (tile + 1) * LANES]
            block = turn_back(block, tile, cos_ref[...], sin_ref[...])
            out_ref[:, tile * LANES : (tile + 1) * LANES] = block.astype(jnp.bfloat16)

    return kernel_call(
        kernel, [((tokens, 2 * kwidth), jnp.bfloat16)], [], own, *others, cosine, sine
    )[0]


def input_backward(grad_query, grad_kv, w_qkv, residual, gain, grad_middle):
    tokens = residual.shape[0]
    qwidth = HEADS * HEAD_DIM
    whole = w_qkv.shape[1]

    def kernel(query_ref, kv_ref, w_ref, res_ref, gain_ref, mid_ref, grad_ref, sum_ref, row_ref):
        row_ref[:, :qwidth] = query_ref[...]
        row_ref[:, qwidth:] = kv_ref[...]
        grad = dot_nt(row_ref[...], w_ref[...])
        residual = res_ref[...]
        inverse = lax.rsqrt(jnp.mean(residual * residual, axis=-1, keepdims=True) + EPS)
        scaled = grad * gain_ref[...]
        cubed = inverse * inverse * inverse
        grad_ref[...] = mid_ref[...] + (
            inverse * scaled
            - residual * cubed * jnp.mean(scaled * residual, axis=-1, keepdims=True)
        )
        sum_ref[...] = jnp.sum(grad * residual * inverse, axis=0, keepdims=True)

    return kernel_call(
        kernel,
        [((tokens, D), jnp.float32), ((1, D), jnp.float32)],
        [((tokens, whole), jnp.bfloat16)],
        grad_query, grad_kv, w_qkv, residual, gain, grad_middle,
    )


def attn_grads(
    places, normed_parts, head_mix, grad_query, near_kv, grad_mid, rows, dp_count, ctx_count
):
    parts = len(normed_parts)
    qwidth, kwidth = HEADS * HEAD_DIM, KV_HEADS * HEAD_DIM
    tiles = -(-max(qwidth, D) // LANES)
    runs = attn_pieces(rows, dp_count, ctx_count)
    share = rows * ctx_count

    def kernel(place_ref, *refs):
        normed_refs = refs[:parts]
        mix_ref, query_ref, kv_ref, mid_ref = refs[parts : parts + 4]
        even_ref, odd_ref, long_ref, tile_ref = refs[parts + 4 :]
        near = jnp.concatenate([ref[...] for ref in normed_refs], axis=0)
        for value, matrices in (
            (left_dot(normed_refs[-1][...], query_ref[...]), ((0, qwidth, runs[0]),)),
            (
                left_dot(near, kv_ref[...]),
                ((0, kwidth, runs[1]), (kwidth, kwidth, runs[2])),
            ),
            (left_dot(mix_ref[...], mid_ref[...]), ((0, D, runs[3]),)),
        ):
            span = value.shape[1]
            for tile in range(-(-span // LANES)):
                width = min(LANES, span - tile * LANES)
                tile_ref[tile, :, :width] = value[:, tile * LANES : tile * LANES + width]
            for first, width, matrix in matrices:
                lead, offset = divmod(first // HALF, 2)
                for row, count, base, _ in matrix:
                    def get(tile, parity, lead=lead, row=row, count=count):
                        return tile_ref[lead + tile, pl.ds(row + parity, count // 2, stride=2), :]

                    flat_rows(get, long_ref, base, count // 2, width, offset)
        for mask in range(dp_count):
            ref = odd_ref if mask % 2 else even_ref
            first = pl.multiple_of((place_ref[0] ^ mask) * share, 8)
            chunk = GRAIN

            def move(step, carry, ref=ref, mask=mask, first=first):
                at = pl.multiple_of(step * chunk, 8)
                ref[mask // 2, pl.ds(at, chunk), :] = long_ref[pl.ds(first + at, chunk), :].astype(
                    jnp.bfloat16
                )
                return carry

            lax.fori_loop(0, share // chunk, move, 0)

    half = (dp_count // 2, share, LANES)
    return kernel_call(
        kernel,
        [(half, jnp.bfloat16)] * 2,
        [((dp_count * share, LANES), jnp.float32), ((tiles, D, LANES), jnp.float32)],
        *normed_parts, head_mix, grad_query, near_kv, grad_mid,
        places=places,
    )


def after(value, *others):
    return lax.optimization_barrier((value,) + others)[0]


def from_chips(rows):
    return [(0, rows)] + [
        (mask, lax.ppermute(rows, "dp", swap_pairs("dp", mask)))
        for mask in range(2, lax.axis_size("dp"), 2)
    ]


def with_cores(held):
    return held + [
        (mask + 1, lax.ppermute(array, "dp", swap_pairs("dp", 1))) for mask, array in held
    ]


def reduce_cores(even, odd):
    wide = jnp.float32
    moved = lax.ppermute(odd, "dp", swap_pairs("dp", 1))
    return [
        (even[at].astype(wide) + moved[at].astype(wide)).astype(jnp.bfloat16)
        for at in range(even.shape[0])
    ]


def reduce_chips(sums):
    total = sums[0].astype(jnp.float32)
    for at in range(1, len(sums)):
        moved = lax.ppermute(sums[at], "dp", swap_pairs("dp", 2 * at))
        total = total + moved.astype(jnp.float32)
    return total.astype(jnp.bfloat16)


def body(hidden_in, segments, attn_flat, mlp_flat, norm_one, norm_two, cotangent):
    dp_count, ctx_count = lax.axis_size("dp"), lax.axis_size("ctx")
    if not (
        hidden_in.shape[0] == 1
        and columns_apply(dp_count, ctx_count, mlp_flat.shape[0])
        and attn_fits(attn_flat.shape[0], dp_count, ctx_count)
    ):
        return body_rows(hidden_in, segments, attn_flat, mlp_flat, norm_one, norm_two, cotangent)
    return body_columns(hidden_in, segments, attn_flat, mlp_flat, norm_one, norm_two, cotangent)


def body_columns(hidden_in, segments, attn_flat, mlp_flat, norm_one, norm_two, cotangent):
    tokens = hidden_in.shape[1]
    seq_len = segments.shape[1]
    low = jnp.bfloat16
    dp_count = lax.axis_size("dp")
    ctx_count = lax.axis_size("ctx")
    attn_rows, mlp_rows = attn_flat.shape[0], mlp_flat.shape[0]
    back = -(-(seq_len // 2 - 1) // tokens)
    start_row = lax.axis_index("ctx") * tokens

    places = jnp.stack([lax.axis_index("dp"), lax.axis_index("ctx")]).astype(jnp.int32)
    up_pairs = [
        [(place, place + step) for place in range(ctx_count - step)] for step in range(back + 1)
    ]
    down_pairs = [[(right, left) for left, right in pairs] for pairs in up_pairs]
    residual = hidden_in.reshape(tokens, D)
    cot_rows = cotangent.reshape(tokens, D)
    normed_one = norm_forward(residual, norm_one)[1].astype(low)

    padded = -(-attn_rows // 32) * 32
    flat = jnp.pad(attn_flat, ((0, padded - attn_rows), (0, 0)))
    own_blocks = from_chips(flat)
    others = jnp.concatenate(spread(flat)[1:], axis=0)
    others, window, *arrays = lax.optimization_barrier(
        (others, normed_one, *[array for _, array in own_blocks])
    )
    own_blocks = with_cores([(mask, array) for (mask, _), array in zip(own_blocks, arrays)])
    normed_parts = [
        lax.ppermute(window, "ctx", up_pairs[step]) for step in range(back, 0, -1)
    ] + [normed_one]
    mlp_near = trade_mlp(mlp_flat, others)
    other_blocks = from_chips(others)
    cot_low, *arrays = lax.optimization_barrier(
        (cot_rows.astype(low), *[array for _, array in other_blocks], *normed_parts[:-1], mlp_near)
    )
    other_blocks = with_cores([(mask, array) for (mask, _), array in zip(other_blocks, arrays)])
    cot_slots = spread(cot_low)
    held = [(mask, (0,), array) for mask, array in own_blocks]
    held += [(mask, tuple(range(1, ctx_count)), array) for mask, array in other_blocks]

    pos_near = lax.dynamic_slice_in_dim(
        jnp.pad(positions_of(segments), ((0, 0), (back * tokens, 0))),
        start_row,
        (back + 1) * tokens,
        1,
    )
    seg_col = lax.dynamic_slice_in_dim(segments, start_row, tokens, 1).reshape(tokens, 1)
    seg_near = lax.dynamic_slice_in_dim(
        jnp.pad(segments, ((0, 0), (back * tokens, 0)), constant_values=-1),
        start_row,
        (back + 1) * tokens,
        1,
    )
    cosine, sine = [table[:, 0] for table in rope_tables(pos_near.reshape(-1))]
    heads = 128 // HEAD_DIM
    cosine = jnp.concatenate([cosine, cosine] * heads, axis=1)
    sine = jnp.concatenate([-sine, sine] * heads, axis=1)
    gain_one, gain_two = norm_one.reshape(1, D), norm_two.reshape(1, D)

    query, near_kv, w_qkv, w_out = project(
        places, held, normed_parts, cosine, sine, attn_rows, padded, dp_count, ctx_count
    )
    mlp_near = after(mlp_near, *[array for _, _, array in held])
    mlp_whole = lax.all_gather(mlp_near, "dp", axis=0, tiled=True)
    head_mix, logs, middle, normed_two = attend(
        query, near_kv, seg_col, seg_near, residual, w_out, gain_two
    )
    two_slots = spread(normed_two)

    w_gate, w_up, w_down, grad_active = unpack_mlp(
        mlp_whole, cot_slots, mlp_rows, dp_count, ctx_count
    )
    active, grad_gate, grad_up, *two_terms = feed_forward(two_slots, w_gate, w_up, grad_active)
    two_others = returned(two_terms[1:])
    mlp_terms, block_own, *block_terms = mlp_grads(
        active, grad_gate, grad_up, two_slots, cot_slots, w_down, mlp_rows, dp_count, ctx_count
    )
    mlp_own = lax.psum_scatter(after(mlp_terms, *two_others), "dp", scatter_dimension=0, tiled=True)
    grad_middle, grad_mid_low, grad_mix, grad_gain_two = middle_backward(
        after(two_terms[0], mlp_terms), two_others, middle, gain_two, cot_rows, w_out
    )
    grad_query, near_grads, kv_own, *kv_terms = attend_backward(
        query, near_kv, grad_mix, logs, seg_col, seg_near, cosine, sine
    )
    kv_others = [
        lax.ppermute(kv_terms[back - step], "ctx", down_pairs[step]) for step in range(1, back + 1)
    ]
    even, odd = attn_grads(
        places, normed_parts, head_mix, grad_query, near_grads, grad_mid_low,
        attn_rows, dp_count, ctx_count,
    )
    sums = reduce_cores(even, odd)
    first, *block_terms = lax.optimization_barrier((sums[0], *block_terms))
    block_others = returned(block_terms)
    total = reduce_chips([after(first, *block_others)] + sums[1:])
    block_rows = middle + block_own
    for moved in block_others:
        block_rows = block_rows + moved.astype(jnp.float32)
    total, kv_own, own = lax.optimization_barrier((total, kv_own, mlp_own))
    attn_blocks = trade(total.reshape(ctx_count, -1, 128))
    grad_kv = own_kv(kv_own, kv_others, cosine[-tokens:], sine[-tokens:])
    grad_in, grad_gain_one = input_backward(
        grad_query, grad_kv, w_qkv, residual, gain_one, grad_middle
    )
    gains = jnp.concatenate([grad_gain_one, grad_gain_two], axis=0)
    gains = add_swapped(gains, "dp", (1,))
    gains = add_swapped(gains, "dp", range(2, dp_count, 2))
    gain_sums = add_swapped(gains, "ctx", range(1, ctx_count))
    mlp_grad = scatter_mlp(own)
    attn_grad = 0.0
    for block in attn_blocks:
        attn_grad = attn_grad + block.astype(jnp.float32)
    return (
        block_rows.reshape(hidden_in.shape),
        grad_in.reshape(hidden_in.shape),
        attn_grad,
        mlp_grad,
        gain_sums[0],
        gain_sums[1],
    )


def solution(mesh):
    in_specs = (
        P("dp", "ctx", None),
        P("dp", None),
        P(("dp", "ctx"), None),
        P(("dp", "ctx"), None),
        P(),
        P(),
        P("dp", "ctx", None),
    )
    out_specs = (
        P("dp", "ctx", None),
        P("dp", "ctx", None),
        P(("dp", "ctx"), None),
        P(("dp", "ctx"), None),
        P(),
        P(),
    )
    return jax.shard_map(body, mesh=mesh, in_specs=in_specs, out_specs=out_specs, check_vma=False)
```

```python
import jax
import jax.numpy as jnp
from jax import lax
from jax.experimental import pallas as pl
from jax.experimental.pallas import tpu as pltpu
from jax.sharding import PartitionSpec as P

D = 960
HEADS = 15
KV_HEADS = 5
HEAD_DIM = 64
FFN = 2560


EPS = 1e-05
THETA = 100000.0


def positions_of(segment_ids):
    earlier = (segment_ids[..., None, :] < segment_ids[..., :, None]).astype(jnp.int32)
    total_len = segment_ids.shape[-1]
    return jnp.arange(total_len, dtype=jnp.int32) - jnp.sum(earlier, axis=-1)


def rope_tables(positions):
    half_dim = HEAD_DIM // 2
    frequency = THETA ** (-2.0 * jnp.arange(half_dim, dtype=jnp.float32) / HEAD_DIM)
    angles = positions.astype(jnp.float32)[:, None] * frequency[None, :]
    return (jnp.cos(angles)[:, None, :], jnp.sin(angles)[:, None, :])


def rotate(vectors, cosine_table, sine_table):
    half_dim = vectors.shape[-1] // 2
    lower_half = vectors[..., :half_dim]
    upper_half = vectors[..., half_dim:]
    return jnp.concatenate(
        [
            lower_half * cosine_table - upper_half * sine_table,
            upper_half * cosine_table + lower_half * sine_table,
        ],
        axis=-1,
    )


def unrotate(grad_rows, cosine_table, sine_table):
    half_dim = grad_rows.shape[-1] // 2
    lower_half = grad_rows[..., :half_dim]
    upper_half = grad_rows[..., half_dim:]
    return jnp.concatenate(
        [
            lower_half * cosine_table + upper_half * sine_table,
            upper_half * cosine_table - lower_half * sine_table,
        ],
        axis=-1,
    )


def unpack_blocks(flat_rows, shapes, dp_count, ctx_count):
    pieces = flat_rows.reshape(dp_count, ctx_count, -1).transpose(1, 0, 2).reshape(ctx_count, -1)
    matrices = []
    offset = 0
    for height, width_cols in shapes:
        length = height * width_cols // ctx_count
        matrices.append(pieces[:, offset : offset + length].reshape(height, width_cols))
        offset = offset + length
    return matrices


def norm_forward(residual, gain_vec):
    inverse = lax.rsqrt(jnp.mean(residual * residual, axis=-1, keepdims=True) + EPS)
    return (inverse, residual * inverse * gain_vec)


def norm_backward(residual, inverse, gain_vec, grad_normed):
    scaled = grad_normed * gain_vec
    cubed = inverse * inverse * inverse
    grad_resid = inverse * scaled - residual * cubed * jnp.mean(
        scaled * residual, axis=-1, keepdims=True
    )
    grad_gain = jnp.sum(grad_normed * residual * inverse, axis=0)
    return (grad_resid, grad_gain)


def masked_scores(query_rot, key_whole, allowed, score_scale):
    scores = (
        jnp.einsum("sqkgd,slkd->skgql", query_rot, key_whole, preferred_element_type=jnp.float32)
        * score_scale
    )
    return jnp.where(allowed, scores, -jnp.inf)


def left_dot(left_cols, right_rows):
    return lax.dot_general(
        left_cols, right_rows, (((0,), (0,)), ((), ())), preferred_element_type=jnp.float32
    )


def body_rows(hidden_in, segments, attn_flat, mlp_flat, norm_one, norm_two, cotangent):
    seq_count, local_len, model_width = hidden_in.shape
    seq_len = segments.shape[1]
    row_count = seq_count * local_len
    groups = HEADS // KV_HEADS
    qwidth = HEADS * HEAD_DIM
    kwidth = KV_HEADS * HEAD_DIM
    score_scale = HEAD_DIM ** (-0.5)
    low = jnp.bfloat16
    wide = jnp.float32
    dp_count = lax.axis_size("dp")
    ctx_count = lax.axis_size("ctx")
    attn_shapes = ((D, qwidth), (D, kwidth), (D, kwidth), (qwidth, D))
    mlp_shapes = ((D, FFN), (D, FFN), (FFN, D))
    start_row = lax.axis_index("ctx") * local_len
    attn_whole, mlp_whole = (
        lax.all_gather(attn_flat, ("dp", "ctx"), axis=0, tiled=True),
        lax.all_gather(mlp_flat, ("dp", "ctx"), axis=0, tiled=True),
    )
    w_query, w_key, w_value, w_out = unpack_blocks(attn_whole, attn_shapes, dp_count, ctx_count)
    w_gate, w_up, w_down = unpack_blocks(mlp_whole, mlp_shapes, dp_count, ctx_count)
    pos_all = positions_of(segments)
    pos_local = lax.dynamic_slice_in_dim(pos_all, start_row, local_len, 1)
    seg_local = lax.dynamic_slice_in_dim(segments, start_row, local_len, 1)
    cosine_table, sine_table = rope_tables(pos_local.reshape(-1))
    key_index = jnp.arange(seq_len, dtype=jnp.int32)
    query_index = start_row + jnp.arange(local_len, dtype=jnp.int32)
    allowed = (seg_local[:, :, None] == segments[:, None, :]) & (
        key_index[None, None, :] <= query_index[None, :, None]
    )
    allowed = allowed[:, None, None]
    residual = hidden_in.reshape(row_count, model_width)
    inv_one, normed_one = norm_forward(residual, norm_one)
    normed_one = normed_one.astype(low)
    query = jnp.dot(normed_one, w_query, preferred_element_type=wide).reshape(
        row_count, HEADS, HEAD_DIM
    )
    key_raw = jnp.dot(normed_one, w_key, preferred_element_type=wide).reshape(
        row_count, KV_HEADS, HEAD_DIM
    )
    value_low = jnp.dot(normed_one, w_value, preferred_element_type=wide).astype(low)
    query_rot = (
        rotate(query, cosine_table, sine_table)
        .astype(low)
        .reshape(seq_count, local_len, KV_HEADS, groups, HEAD_DIM)
    )
    key_rot = rotate(key_raw, cosine_table, sine_table).astype(low)
    kv_local = jnp.concatenate(
        [
            key_rot.reshape(seq_count, local_len, kwidth),
            value_low.reshape(seq_count, local_len, kwidth),
        ],
        axis=2,
    )
    kv_whole = lax.all_gather(kv_local, "ctx", axis=1, tiled=True)
    key_whole = kv_whole[:, :, :kwidth].reshape(seq_count, seq_len, KV_HEADS, HEAD_DIM)
    value_whole = kv_whole[:, :, kwidth:].reshape(seq_count, seq_len, KV_HEADS, HEAD_DIM)
    scores = masked_scores(query_rot, key_whole, allowed, score_scale)
    row_top = jnp.max(scores, axis=-1, keepdims=True)
    log_total = row_top + jnp.log(jnp.sum(jnp.exp(scores - row_top), axis=-1, keepdims=True))
    probs_low = jnp.exp(scores - log_total).astype(low)
    head_mix = jnp.einsum("skgql,slkd->sqkgd", probs_low, value_whole, preferred_element_type=wide)
    head_mix = head_mix.reshape(row_count, qwidth).astype(low)
    middle = residual + jnp.dot(head_mix, w_out, preferred_element_type=wide)
    inv_two, normed_two = norm_forward(middle, norm_two)
    normed_two = normed_two.astype(low)
    gate_pre = jnp.dot(normed_two, w_gate, preferred_element_type=wide)
    up_proj = jnp.dot(normed_two, w_up, preferred_element_type=wide)
    gate_sigmoid = jax.nn.sigmoid(gate_pre)
    active = (gate_pre * gate_sigmoid * up_proj).astype(low)
    block_rows = middle + jnp.dot(active, w_down, preferred_element_type=wide)
    one_cols, mix_cols, two_cols, active_cols = (
        lax.all_to_all(normed_one, "ctx", split_axis=1, concat_axis=0, tiled=True),
        lax.all_to_all(head_mix, "ctx", split_axis=1, concat_axis=0, tiled=True),
        lax.all_to_all(normed_two, "ctx", split_axis=1, concat_axis=0, tiled=True),
        lax.all_to_all(active, "ctx", split_axis=1, concat_axis=0, tiled=True),
    )
    cot_rows = cotangent.reshape(row_count, model_width)
    cot_low = cot_rows.astype(low)
    grad_active = jnp.dot(cot_low, w_down.T, preferred_element_type=wide)
    grad_gate = (
        grad_active * up_proj * gate_sigmoid * (1.0 + gate_pre * (1.0 - gate_sigmoid))
    ).astype(low)
    grad_up = (grad_active * gate_pre * gate_sigmoid).astype(low)
    grad_normed_two = jnp.dot(grad_gate, w_gate.T, preferred_element_type=wide) + jnp.dot(
        grad_up, w_up.T, preferred_element_type=wide
    )
    grad_middle, grad_gain_two = norm_backward(middle, inv_two, norm_two, grad_normed_two)
    grad_middle = cot_rows + grad_middle
    grad_mid_low = grad_middle.astype(low)
    grad_mix = jnp.dot(grad_mid_low, w_out.T, preferred_element_type=wide).astype(low)
    grad_mix = grad_mix.reshape(seq_count, local_len, KV_HEADS, groups, HEAD_DIM)
    attn_probs = jnp.exp(masked_scores(query_rot, key_whole, allowed, score_scale) - log_total)
    probs_low = attn_probs.astype(low)
    grad_probs = jnp.einsum("sqkgd,slkd->skgql", grad_mix, value_whole, preferred_element_type=wide)
    grad_value_all = jnp.einsum(
        "skgql,sqkgd->slkd", probs_low, grad_mix, preferred_element_type=wide
    )
    grad_scores = attn_probs * (
        grad_probs - jnp.sum(attn_probs * grad_probs, axis=-1, keepdims=True)
    )
    grad_scores_low = (grad_scores * score_scale).astype(low)
    grad_query = jnp.einsum(
        "skgql,slkd->sqkgd", grad_scores_low, key_whole, preferred_element_type=wide
    )
    grad_key_all = jnp.einsum(
        "skgql,sqkgd->slkd", grad_scores_low, query_rot, preferred_element_type=wide
    )
    kv_terms = jnp.concatenate(
        [
            grad_key_all.reshape(seq_count, seq_len, kwidth),
            grad_value_all.reshape(seq_count, seq_len, kwidth),
        ],
        axis=2,
    )
    kv_owned = lax.psum_scatter(
        kv_terms.astype(jnp.bfloat16), "ctx", scatter_dimension=1, tiled=True
    ).astype(jnp.float32)
    grad_key = kv_owned[:, :, :kwidth].reshape(row_count, KV_HEADS, HEAD_DIM)
    grad_value = kv_owned[:, :, kwidth:].reshape(row_count, kwidth).astype(low)
    grad_query = (
        unrotate(grad_query.reshape(row_count, HEADS, HEAD_DIM), cosine_table, sine_table)
        .reshape(row_count, qwidth)
        .astype(low)
    )
    grad_key = unrotate(grad_key, cosine_table, sine_table).reshape(row_count, kwidth).astype(low)
    grad_normed_one = (
        jnp.dot(grad_query, w_query.T, preferred_element_type=wide)
        + jnp.dot(grad_key, w_key.T, preferred_element_type=wide)
        + jnp.dot(grad_value, w_value.T, preferred_element_type=wide)
    )
    grad_resid, grad_gain_one = norm_backward(residual, inv_one, norm_one, grad_normed_one)
    grad_resid = grad_middle + grad_resid
    gathered = (
        lax.all_gather(grad_query, "ctx", axis=0, tiled=True),
        lax.all_gather(grad_key, "ctx", axis=0, tiled=True),
        lax.all_gather(grad_value, "ctx", axis=0, tiled=True),
        lax.all_gather(grad_mid_low, "ctx", axis=0, tiled=True),
        lax.all_gather(grad_gate, "ctx", axis=0, tiled=True),
        lax.all_gather(grad_up, "ctx", axis=0, tiled=True),
        lax.all_gather(cot_low, "ctx", axis=0, tiled=True),
    )
    all_query, all_key, all_value, all_mid, all_gate, all_up, all_cot = gathered
    attn_terms = jnp.concatenate(
        [
            left_dot(one_cols, all_query).reshape(-1),
            left_dot(one_cols, all_key).reshape(-1),
            left_dot(one_cols, all_value).reshape(-1),
            left_dot(mix_cols, all_mid).reshape(-1),
        ]
    ).reshape(-1, 128)
    mlp_terms = jnp.concatenate(
        [
            left_dot(two_cols, all_gate).reshape(-1),
            left_dot(two_cols, all_up).reshape(-1),
            left_dot(active_cols, all_cot).reshape(-1),
        ]
    ).reshape(-1, 128)
    attn_grad, mlp_grad = (
        lax.psum_scatter(
            attn_terms.astype(jnp.bfloat16), "dp", scatter_dimension=0, tiled=True
        ).astype(jnp.float32),
        lax.psum_scatter(
            mlp_terms.astype(jnp.bfloat16), "dp", scatter_dimension=0, tiled=True
        ).astype(jnp.float32),
    )
    gain_sums = lax.psum(jnp.stack([grad_gain_one, grad_gain_two]), ("dp", "ctx"))
    return (
        block_rows.reshape(seq_count, local_len, model_width),
        grad_resid.reshape(seq_count, local_len, model_width),
        attn_grad,
        mlp_grad,
        gain_sums[0],
        gain_sums[1],
    )


def add_swapped(rows, axis, masks):
    total = rows
    for mask in masks:
        total = total + lax.ppermute(rows, axis, swap_pairs(axis, mask))
    return total


def swap_pairs(axis, step):
    return [(place, place ^ step) for place in range(lax.axis_size(axis))]


def spread(rows):
    return [rows] + [
        lax.ppermute(rows, "ctx", swap_pairs("ctx", step)) for step in range(1, lax.axis_size("ctx"))
    ]


def returned(terms):
    return [
        lax.ppermute(term, "ctx", swap_pairs("ctx", step + 1)) for step, term in enumerate(terms)
    ]


def trade(blocks, *before):
    here = lax.axis_index("ctx")
    got = [lax.dynamic_index_in_dim(blocks, here, 0, False)]
    for step in range(1, lax.axis_size("ctx")):
        block = lax.dynamic_index_in_dim(blocks, here ^ step, 0, False)
        block = after(block, *before)
        got.append(lax.ppermute(block, "ctx", swap_pairs("ctx", step)))
    return got


def in_order(pieces):
    here = lax.axis_index("ctx")
    step = 1
    while step < len(pieces):
        bit = (here & step) != 0
        pieces = [
            jnp.where(bit, pieces[place ^ step], pieces[place]) for place in range(len(pieces))
        ]
        step = 2 * step
    return jnp.stack(pieces)


def columns_apply(dp_count, ctx_count, rows):
    unit = FFN // 128
    return (
        rows % unit == 0
        and FFN % (128 * ctx_count) == 0
        and D % ctx_count == 0
        and ctx_count & (ctx_count - 1) == 0
        and dp_count & (dp_count - 1) == 0
        and rows % ctx_count == 0
        and (2 * (D // ctx_count) % (rows // unit)) * unit % ctx_count == 0
        and (rows - (2 * (D // ctx_count) % (rows // unit)) * unit) % (ctx_count * 2 * D // 128) == 0
        and rows % (2 * D // 128) == 0
    )


def mlp_sizes(rows, ctx_count):
    unit = FFN // 128
    held = rows // unit
    tall = 2 * (D // ctx_count)
    return unit, unit // ctx_count, held, tall // held, tall % held


def trade_mlp(flat, *before):
    ctx_count = lax.axis_size("ctx")
    place = lax.axis_index("dp")
    rows = flat.shape[0]
    unit, part, held, edge, rest = mlp_sizes(rows, ctx_count)
    cut = rest * unit

    def by_column(block, count):
        return (
            block.reshape(count, ctx_count, part, 128)
            .transpose(1, 0, 2, 3)
            .reshape(ctx_count, count * part, 128)
        )

    full = by_column(flat, held)
    tail = flat[cut:].reshape(ctx_count, -1, 128)
    mixed = jnp.concatenate([by_column(flat[:cut], rest), tail], axis=1)
    got = in_order(trade(jnp.where(place < edge, full, mixed), *before))
    kept = jnp.concatenate([got[:, : rest * part], tail], axis=1)
    block = jnp.where(
        place < edge, got, jnp.where(place == edge, kept, flat.reshape(ctx_count, -1, 128))
    )
    return block.reshape(rows, 128)


def scatter_mlp(own):
    ctx_count = lax.axis_size("ctx")
    place = lax.axis_index("dp")
    rows = own.shape[0]
    unit, part, held, edge, rest = mlp_sizes(rows, ctx_count)
    blocks = own.reshape(ctx_count, rows // ctx_count, 128)
    got = in_order(trade(blocks))

    def by_row(block, count):
        return block.reshape(ctx_count, count, part, 128).transpose(1, 0, 2, 3).reshape(-1, 128)

    full = by_row(got, held)
    mixed = jnp.concatenate(
        [by_row(got[:, : rest * part], rest), blocks[:, rest * part :].reshape(-1, 128)], axis=0
    )
    out = jnp.where(place < edge, full, jnp.where(place == edge, mixed, own))
    return out.astype(jnp.float32)


VMEM_BYTES = 56 * 1024 * 1024
LANES = 128
HALF = LANES // 2
GRAIN = 160


def kernel_call(kernel, outs, scratch, *args, places=None):
    specs = [pl.BlockSpec(memory_space=pltpu.VMEM) for _ in args]
    if places is not None:
        specs = [pl.BlockSpec(memory_space=pltpu.SMEM)] + specs
        args = (places,) + args
    return pl.pallas_call(
        kernel,
        in_specs=specs,
        out_shape=[jax.ShapeDtypeStruct(shape, dtype) for shape, dtype in outs],
        scratch_shapes=[pltpu.VMEM(shape, dtype) for shape, dtype in scratch],
        compiler_params=pltpu.CompilerParams(vmem_limit_bytes=VMEM_BYTES),
    )(*args)


def low_lanes(rows):
    return lax.broadcasted_iota(jnp.int32, (rows, LANES), 1) < HALF


def dot_nt(left, right):
    return lax.dot_general(
        left, right, (((1,), (1,)), ((), ())), preferred_element_type=jnp.float32
    )


def dot_nn(left, right):
    return jnp.dot(left, right, preferred_element_type=jnp.float32)


def pair_rows(flat_ref, base, pairs, width, offset, put):
    halves = width // HALF
    tiles = [flat_ref[pl.ds(base + step, pairs, stride=halves), :] for step in range(halves)]
    rolled = {}
    mask = low_lanes(pairs)

    def roll(index):
        index = min(max(index, 0), halves - 1)
        if index not in rolled:
            rolled[index] = pltpu.roll(tiles[index], HALF, 1)
        return rolled[index]

    for parity in range(2):
        for tile in range((halves + offset + 1) // 2):
            first = parity * halves - offset + 2 * tile
            if first % 2 == 0:
                put(tile, parity, tiles[first // 2])
            else:
                put(tile, parity, jnp.where(mask, roll(first // 2), roll(first // 2 + 1)))


def flat_rows(get, flat_ref, base, pairs, width, offset):
    halves = width // HALF
    mask = low_lanes(pairs)
    blocks, rolled = {}, {}

    def half(index, want):
        parity, index = divmod(index, halves)
        tile, side = divmod(index + offset, 2)
        key = (tile, parity)
        if key not in blocks:
            blocks[key] = get(tile, parity)
        if side == want:
            return blocks[key]
        if key not in rolled:
            rolled[key] = pltpu.roll(blocks[key], HALF, 1)
        return rolled[key]

    for step in range(halves):
        left, right = half(2 * step, 0), half(2 * step + 1, 1)
        flat_ref[pl.ds(base + step, pairs, stride=halves), :] = (
            left if left is right else jnp.where(mask, left, right)
        )


def partner_lanes(block):
    quarter = HEAD_DIM // 2
    lane = lax.broadcasted_iota(jnp.int32, block.shape, 1)
    return jnp.where(
        (lane & quarter) == 0,
        pltpu.roll(block, LANES - quarter, 1),
        pltpu.roll(block, quarter, 1),
    )


def attn_pieces(rows, dp_count, ctx_count, stride=None):
    runs = []
    begin = 0
    for height, width in (
        (D, HEADS * HEAD_DIM),
        (D, KV_HEADS * HEAD_DIM),
        (D, KV_HEADS * HEAD_DIM),
        (HEADS * HEAD_DIM, D),
    ):
        block = height // ctx_count
        span = block * width // LANES
        matrix = []
        for ctx in range(ctx_count):
            at = begin
            while at < begin + span:
                part, inside = divmod(at, rows)
                size = min(rows - inside, begin + span - at)
                matrix.append(
                    (
                        ctx * block + (at - begin) * LANES // width,
                        size * LANES // width,
                        (part * ctx_count + ctx) * (stride or rows) + inside,
                        size,
                    )
                )
                at = at + size
        runs.append(matrix)
        begin = begin + span
    return runs


def attn_fits(rows, dp_count, ctx_count):
    widths = (HEADS * HEAD_DIM, KV_HEADS * HEAD_DIM, KV_HEADS * HEAD_DIM, D)
    return D % ctx_count == 0 and all(
        (2 * width) % LANES == 0
        and (width // HALF) % 2 == 1
        and size % (2 * width // LANES) == 0
        and row % 2 == 0
        and (rows * ctx_count) % GRAIN == 0
        for width, matrix in zip(widths, attn_pieces(rows, dp_count, ctx_count))
        for row, _, _, size in matrix
    )


def project(places, held, normed_parts, cosine, sine, used, rows, dp_count, ctx_count):
    parts = len(normed_parts)
    tokens = normed_parts[-1].shape[0]
    near_len = parts * tokens
    qwidth, kwidth = HEADS * HEAD_DIM, KV_HEADS * HEAD_DIM
    whole = qwidth + 2 * kwidth
    runs = attn_pieces(used, dp_count, ctx_count, rows)
    total = rows * dp_count * ctx_count
    qtiles = -(-qwidth // LANES)
    ktile, koff = divmod(qwidth // HALF, 2)
    vtile, voff = divmod((qwidth + kwidth) // HALF, 2)
    ktiles = (kwidth // HALF + koff + 1) // 2
    vtiles = (kwidth // HALF + voff + 1) // 2

    def kernel(place_ref, *refs):
        held_refs = refs[: len(held)]
        normed_refs = refs[len(held) : len(held) + parts]
        cos_ref, sin_ref = refs[len(held) + parts : len(held) + parts + 2]
        query_ref, kv_ref, wide_ref, out_ref, long_ref, tile_ref = refs[len(held) + parts + 2 :]
        for (dp_mask, ctx_masks, _), ref in zip(held, held_refs):
            def move(step, carry, dp_mask=dp_mask, lead=ctx_masks[0], ref=ref):
                block = (place_ref[0] ^ dp_mask) * ctx_count + (place_ref[1] ^ (lead + step // 2))
                first = pl.multiple_of(block * rows + (step % 2) * (rows // 2), 16)
                long_ref[pl.ds(first, rows // 2), :] = ref[
                    pl.ds(pl.multiple_of(step * (rows // 2), 16), rows // 2), :
                ].astype(jnp.float32)
                return carry

            lax.fori_loop(0, 2 * len(ctx_masks), move, 0)
        slots = ((0, 0, 0), (qtiles, koff, ktile), (qtiles + ktiles, voff, vtile))
        for (slot, offset, _), matrix, width in zip(slots, runs, (qwidth, kwidth, kwidth)):
            for row, count, base, size in matrix:
                def put(tile, parity, block, slot=slot, row=row, count=count):
                    tile_ref[slot + tile, pl.ds(row + parity, count // 2, stride=2), :] = block

                pair_rows(long_ref, base, count // 2, width, offset, put)
        mask = low_lanes(D)
        for tile in range(-(-whole // LANES)):
            found = [
                tile_ref[slot + tile - first]
                for (slot, _, first), count in zip(slots, (qtiles, ktiles, vtiles))
                if first <= tile < first + count
            ]
            block = found[0] if len(found) == 1 else jnp.where(mask, found[0], found[1])
            width = min(LANES, whole - tile * LANES)
            wide_ref[:, tile * LANES : tile * LANES + width] = block[:, :width].astype(jnp.bfloat16)
        product = dot_nn(normed_refs[-1][...], wide_ref[:, : qtiles * LANES])
        here = slice(near_len - tokens, near_len)
        for tile in range(qtiles):
            width = min(LANES, qwidth - tile * LANES)
            block = product[:, tile * LANES : (tile + 1) * LANES]
            block = block * cos_ref[here, :] + partner_lanes(block) * sin_ref[here, :]
            query_ref[:, tile * LANES : tile * LANES + width] = block[:, :width].astype(jnp.bfloat16)
        near = jnp.concatenate([ref[...] for ref in normed_refs], axis=0)
        product = dot_nn(near, wide_ref[:, ktile * LANES :])
        lead = qwidth - ktile * LANES
        turned = []
        for tile in range((lead + kwidth) // LANES):
            block = product[:, tile * LANES : (tile + 1) * LANES]
            turned.append(
                (block * cos_ref[...] + partner_lanes(block) * sin_ref[...]).astype(jnp.bfloat16)
            )
        kv_ref[:, :kwidth] = jnp.concatenate(turned, axis=1)[:, lead:]
        kv_ref[:, kwidth:] = product[:, lead + kwidth :].astype(jnp.bfloat16)
        for row, count, base, size in runs[3]:
            def put(tile, parity, block, row=row, count=count):
                tile_ref[tile, pl.ds(row + parity, count // 2, stride=2), :] = block

            pair_rows(long_ref, base, count // 2, D, 0, put)
        for tile in range(-(-D // LANES)):
            width = min(LANES, D - tile * LANES)
            out_ref[:, tile * LANES : tile * LANES + width] = tile_ref[tile][:, :width].astype(
                jnp.bfloat16
            )

    low = jnp.bfloat16
    return kernel_call(
        kernel,
        [
            ((tokens, qwidth), low),
            ((near_len, 2 * kwidth), low),
            ((D, whole), low),
            ((qwidth, D), low),
        ],
        [((total, LANES), jnp.float32), ((qtiles + ktiles + vtiles, D, LANES), jnp.float32)],
        *[array for _, _, array in held], *normed_parts, cosine, sine,
        places=places,
    )


def group_rows(ref, group, groups):
    first = group * groups * HEAD_DIM
    return jnp.concatenate(
        [ref[:, first + g * HEAD_DIM : first + (g + 1) * HEAD_DIM] for g in range(groups)], axis=0
    )


def group_allowed(seg_ref, near_ref, tokens, near_len, groups):
    query = lax.broadcasted_iota(jnp.int32, (tokens, near_len), 0)
    key = lax.broadcasted_iota(jnp.int32, (tokens, near_len), 1) - (near_len - tokens)
    allowed = (seg_ref[...] == near_ref[...]) & (key <= query)
    return allowed


def attend(query, near_kv, seg_col, seg_near, residual, w_out, gain):
    tokens = query.shape[0]
    near_len = near_kv.shape[0]
    groups = HEADS // KV_HEADS
    kwidth = KV_HEADS * HEAD_DIM
    scale = HEAD_DIM ** (-0.5)

    def kernel(
        query_ref, near_kv_ref, seg_ref, near_ref, res_ref, out_ref, gain_ref,
        mix_ref, log_ref, mid_ref, normed_ref,
    ):
        allowed = group_allowed(seg_ref, near_ref, tokens, near_len, groups)
        allowed = jnp.concatenate([allowed.astype(jnp.float32)] * groups, axis=0) > 0.5
        mixes, logs = [], []
        for group in range(KV_HEADS):
            at = group * HEAD_DIM
            key = near_kv_ref[:, at : at + HEAD_DIM]
            value = near_kv_ref[:, kwidth + at : kwidth + at + HEAD_DIM]
            scores = dot_nt(group_rows(query_ref, group, groups), key) * scale
            scores = jnp.where(allowed, scores, -jnp.inf)
            top = jnp.max(scores, axis=-1, keepdims=True)
            total = top + jnp.log(jnp.sum(jnp.exp(scores - top), axis=-1, keepdims=True))
            probs = jnp.exp(scores - total).astype(jnp.bfloat16)
            mix = dot_nn(probs, value).astype(jnp.bfloat16)
            for g in range(groups):
                mixes.append(mix[g * tokens : (g + 1) * tokens])
                logs.append(total[g * tokens : (g + 1) * tokens])
        for head in range(HEADS):
            log_ref[:, head : head + 1] = logs[head]
        head_mix = jnp.concatenate(mixes, axis=1)
        mix_ref[...] = head_mix
        middle = res_ref[...] + dot_nn(head_mix, out_ref[...])
        mid_ref[...] = middle
        inverse = lax.rsqrt(jnp.mean(middle * middle, axis=-1, keepdims=True) + EPS)
        normed_ref[...] = (middle * inverse * gain_ref[...]).astype(jnp.bfloat16)

    low, wide = jnp.bfloat16, jnp.float32
    return kernel_call(
        kernel,
        [
            ((tokens, HEADS * HEAD_DIM), low),
            ((tokens, LANES), wide),
            ((tokens, D), wide),
            ((tokens, D), low),
        ],
        [],
        query, near_kv, seg_col, seg_near, residual, w_out, gain,
    )


def mlp_pieces(rows, dp_count, ctx_count):
    unit, part, held, edge, rest = mlp_sizes(rows, ctx_count)
    share = rows // ctx_count
    block = D // ctx_count
    gate, up, down = [], [], []
    for ctx in range(ctx_count):
        for dp in range(edge + (rest > 0)):
            count = held if dp < edge else rest
            row, stop = dp * held, dp * held + count
            base = (dp * ctx_count + ctx) * share
            for matrix, begin, end in ((gate, 0, block), (up, block, 2 * block)):
                low, high = max(row, begin), min(stop, end)
                if low < high:
                    matrix.append((ctx * block + low - begin, high - low, base + (low - row) * part))
    cut = rest * part
    at = 0
    for ctx in range(ctx_count):
        size = share - cut
        down.append((at * LANES // D, size * LANES // D, (edge * ctx_count + ctx) * share + cut))
        at = at + size
    for dp in range(edge + 1, dp_count):
        down.append((at * LANES // D, rows * LANES // D, dp * rows))
        at = at + rows
    return part, gate, up, down


def unpack_mlp(flat, cot_slots, rows, dp_count, ctx_count):
    part, gate, up, down = mlp_pieces(rows, dp_count, ctx_count)
    hidden = part * LANES
    tiles = -(-D // LANES)
    tokens = cot_slots[0].shape[0]
    count = len(cot_slots)

    def kernel(flat_ref, *refs):
        cot_refs = refs[:count]
        gate_ref, up_ref, down_ref, act_ref, long_ref, tile_ref, turn_ref = refs[count:]
        long_ref[...] = flat_ref[...].astype(jnp.float32)
        for row, size, base in down:
            def put(tile, parity, block, row=row, size=size):
                tile_ref[tile, pl.ds(row + parity, size // 2, stride=2), :] = block

            pair_rows(long_ref, base, size // 2, D, 0, put)
        for tile in range(tiles):
            width = min(LANES, D - tile * LANES)
            down_ref[:, tile * LANES : tile * LANES + width] = tile_ref[tile][:, :width].astype(
                jnp.bfloat16
            )
        for slot in range(count):
            act_ref[slot * tokens : (slot + 1) * tokens, :] = dot_nt(
                cot_refs[slot][...], down_ref[...]
            )
        for runs, ref in ((gate, gate_ref), (up, up_ref)):
            for row, size, base in runs:
                for step in range(part):
                    turn_ref[step, row : row + size, :] = long_ref[
                        pl.ds(base + step, size, stride=part), :
                    ]
            for step in range(part):
                ref[:, step * LANES : (step + 1) * LANES] = turn_ref[step].astype(jnp.bfloat16)

    low, wide = jnp.bfloat16, jnp.float32
    return kernel_call(
        kernel,
        [
            ((D, hidden), low),
            ((D, hidden), low),
            ((hidden, D), low),
            ((count * tokens, hidden), wide),
        ],
        [
            (flat.shape, wide),
            ((tiles, hidden, LANES), wide),
            ((part, D, LANES), wide),
        ],
        flat, *cot_slots,
    )


def feed_forward(two_slots, w_gate, w_up, grad_active):
    count = len(two_slots)
    tokens = two_slots[0].shape[0]
    hidden = w_gate.shape[1]

    def kernel(*refs):
        two_refs = refs[:count]
        gate_ref, up_ref, act_ref = refs[count : count + 3]
        active_ref, dgate_ref, dup_ref, own_ref = refs[count + 3 : count + 7]
        term_refs = refs[count + 7 :]
        for slot in list(range(1, count)) + [0]:
            rows = slice(slot * tokens, (slot + 1) * tokens)
            two = two_refs[slot][...]
            gate = dot_nn(two, gate_ref[...])
            up = dot_nn(two, up_ref[...])
            grad = act_ref[rows, :]
            sigmoid = jax.nn.sigmoid(gate)
            active_ref[rows, :] = (gate * sigmoid * up).astype(jnp.bfloat16)
            dgate = (grad * up * sigmoid * (1.0 + gate * (1.0 - sigmoid))).astype(jnp.bfloat16)
            dup = (grad * gate * sigmoid).astype(jnp.bfloat16)
            dgate_ref[rows, :] = dgate
            dup_ref[rows, :] = dup
            term = dot_nt(dgate, gate_ref[...]) + dot_nt(dup, up_ref[...])
            if slot:
                term_refs[slot - 1][...] = term.astype(jnp.bfloat16)
            else:
                own_ref[...] = term

    low, wide = jnp.bfloat16, jnp.float32
    return kernel_call(
        kernel,
        [((count * tokens, hidden), low)] * 3
        + [((tokens, D), wide)]
        + [((tokens, D), low)] * (count - 1),
        [],
        *two_slots, w_gate, w_up, grad_active,
    )


def mlp_grads(places, active, dgate, dup, two_slots, cot_slots, w_down, rows, dp_count, ctx_count):
    count = len(two_slots)
    tokens = two_slots[0].shape[0]
    part, gate_runs, up_runs, down_runs = mlp_pieces(rows, dp_count, ctx_count)
    tiles = -(-D // LANES)
    hidden = part * LANES

    def kernel(place_ref, *refs):
        active_ref, dgate_ref, dup_ref = refs[:3]
        two_refs = refs[3 : 3 + count]
        cot_refs = refs[3 + count : 3 + 2 * count]
        down_ref = refs[3 + 2 * count]
        even_ref, odd_ref, own_ref = refs[4 + 2 * count : 7 + 2 * count]
        term_refs = refs[7 + 2 * count : 6 + 3 * count]
        long_ref, tile_ref, turn_ref = refs[6 + 3 * count :]
        for slot in range(count):
            term = dot_nn(active_ref[slot * tokens : (slot + 1) * tokens, :], down_ref[...])
            if slot:
                term_refs[slot - 1][...] = term.astype(jnp.bfloat16)
            else:
                own_ref[...] = term
        two = jnp.concatenate([ref[...] for ref in two_refs], axis=0)
        for runs, grad_ref in ((gate_runs, dgate_ref), (up_runs, dup_ref)):
            value = left_dot(two, grad_ref[...])
            for step in range(part):
                turn_ref[step] = value[:, step * LANES : (step + 1) * LANES]
            for row, size, base in runs:
                for step in range(part):
                    long_ref[pl.ds(base + step, size, stride=part), :] = turn_ref[
                        step, row : row + size, :
                    ]
        cot = jnp.concatenate([ref[...] for ref in cot_refs], axis=0)
        value = left_dot(active_ref[...], cot)
        for tile in range(tiles):
            width = min(LANES, D - tile * LANES)
            tile_ref[tile, :, :width] = value[:, tile * LANES : tile * LANES + width]
        for row, size, base in down_runs:
            def get(tile, parity, row=row, size=size):
                return tile_ref[tile, pl.ds(row + parity, size // 2, stride=2), :]

            flat_rows(get, long_ref, base, size // 2, D, 0)
        for odd, ref in enumerate((even_ref, odd_ref)):
            def move(step, carry, odd=odd, ref=ref):
                first = pl.multiple_of((place_ref[0] ^ (2 * step + odd)) * rows, 8)
                ref[step] = long_ref[pl.ds(first, rows), :].astype(jnp.bfloat16)
                return carry

            lax.fori_loop(0, dp_count // 2, move, 0)

    low, wide = jnp.bfloat16, jnp.float32
    total = rows * dp_count
    return kernel_call(
        kernel,
        [((dp_count // 2, rows, LANES), low)] * 2
        + [((tokens, D), wide)]
        + [((tokens, D), low)] * (count - 1),
        [((total, LANES), wide), ((tiles, hidden, LANES), wide), ((part, D, LANES), wide)],
        active, dgate, dup, *two_slots, *cot_slots, w_down,
        places=places,
    )


def middle_backward(own, others, middle, gain, cot_rows, w_out):
    tokens = own.shape[0]
    count = len(others)

    def kernel(own_ref, *refs):
        other_refs = refs[:count]
        mid_ref, gain_ref, cot_ref, out_ref = refs[count : count + 4]
        grad_ref, low_ref, mix_ref, sum_ref = refs[count + 4 :]
        grad = own_ref[...]
        for ref in other_refs:
            grad = grad + ref[...].astype(jnp.float32)
        middle = mid_ref[...]
        inverse = lax.rsqrt(jnp.mean(middle * middle, axis=-1, keepdims=True) + EPS)
        scaled = grad * gain_ref[...]
        cubed = inverse * inverse * inverse
        result = cot_ref[...] + (
            inverse * scaled - middle * cubed * jnp.mean(scaled * middle, axis=-1, keepdims=True)
        )
        grad_ref[...] = result
        low_ref[...] = result.astype(jnp.bfloat16)
        mix_ref[...] = dot_nt(low_ref[...], out_ref[...]).astype(jnp.bfloat16)
        sum_ref[...] = jnp.sum(grad * middle * inverse, axis=0, keepdims=True)

    low, wide = jnp.bfloat16, jnp.float32
    return kernel_call(
        kernel,
        [
            ((tokens, D), wide),
            ((tokens, D), low),
            ((tokens, HEADS * HEAD_DIM), low),
            ((1, D), wide),
        ],
        [],
        own, *others, middle, gain, cot_rows, w_out,
    )


def turn_back(block, tile, cosine, sine):
    width = KV_HEADS * HEAD_DIM - tile * LANES
    if width <= 0:
        return block
    turned = block * cosine - partner_lanes(block) * sine
    if width >= LANES:
        return turned
    lane = lax.broadcasted_iota(jnp.int32, block.shape, 1)
    return jnp.where(lane < width, turned, block)


def attend_backward(query, near_kv, grad_mix, logs, seg_col, seg_near, cosine, sine):
    tokens = query.shape[0]
    near_len = near_kv.shape[0]
    parts = near_len // tokens
    groups = HEADS // KV_HEADS
    qwidth, kwidth = HEADS * HEAD_DIM, KV_HEADS * HEAD_DIM
    scale = HEAD_DIM ** (-0.5)
    tiles = -(-qwidth // LANES)

    def kernel(
        query_ref, kv_ref, mix_ref, log_ref, seg_ref, near_ref, cos_ref, sin_ref, dquery_ref,
        near_out_ref, own_ref, *rest,
    ):
        part_refs = rest[: parts - 1]
        turn_ref, term_ref = rest[parts - 1 :]
        allowed = group_allowed(seg_ref, near_ref, tokens, near_len, groups)
        allowed = jnp.concatenate([allowed.astype(jnp.float32)] * groups, axis=0) > 0.5
        if tiles * LANES > qwidth:
            turn_ref[:, qwidth:] = jnp.zeros((tokens, tiles * LANES - qwidth), jnp.float32)
        for group in range(KV_HEADS):
            at = group * HEAD_DIM
            key = kv_ref[:, at : at + HEAD_DIM]
            value = kv_ref[:, kwidth + at : kwidth + at + HEAD_DIM]
            queries = group_rows(query_ref, group, groups)
            mixes = group_rows(mix_ref, group, groups)
            total = jnp.concatenate(
                [log_ref[:, group * groups + g : group * groups + g + 1] for g in range(groups)],
                axis=0,
            )
            scores = dot_nt(queries, key) * scale
            probs = jnp.exp(jnp.where(allowed, scores, -jnp.inf) - total)
            grad_probs = dot_nt(mixes, value)
            grad_scores = probs * (grad_probs - jnp.sum(probs * grad_probs, axis=-1, keepdims=True))
            grad_scores = (grad_scores * scale).astype(jnp.bfloat16)
            dquery = dot_nn(grad_scores, key)
            for g in range(groups):
                first = (group * groups + g) * HEAD_DIM
                turn_ref[:, first : first + HEAD_DIM] = dquery[g * tokens : (g + 1) * tokens]
            term_ref[:, at : at + HEAD_DIM] = left_dot(grad_scores, queries)
            term_ref[:, kwidth + at : kwidth + at + HEAD_DIM] = left_dot(
                probs.astype(jnp.bfloat16), mixes
            )
        for part in range(parts - 1):
            part_refs[part][...] = term_ref[part * tokens : (part + 1) * tokens, :].astype(
                jnp.bfloat16
            )
        own_ref[...] = term_ref[near_len - tokens :, :]
        for tile in range(2 * kwidth // LANES):
            span = slice(tile * LANES, (tile + 1) * LANES)
            near_out_ref[:, span] = turn_back(
                term_ref[:, span], tile, cos_ref[...], sin_ref[...]
            ).astype(jnp.bfloat16)
        for tile in range(tiles):
            width = min(LANES, qwidth - tile * LANES)
            block = turn_ref[:, tile * LANES : (tile + 1) * LANES]
            here = slice(near_len - tokens, near_len)
            block = block * cos_ref[here, :] - partner_lanes(block) * sin_ref[here, :]
            dquery_ref[:, tile * LANES : tile * LANES + width] = block[:, :width].astype(
                jnp.bfloat16
            )

    low, wide = jnp.bfloat16, jnp.float32
    return kernel_call(
        kernel,
        [((tokens, qwidth), low), ((near_len, 2 * kwidth), low), ((tokens, 2 * kwidth), wide)]
        + [((tokens, 2 * kwidth), low)] * (parts - 1),
        [((tokens, tiles * LANES), wide), ((near_len, 2 * kwidth), wide)],
        query, near_kv, grad_mix, logs, seg_col, seg_near, cosine, sine,
    )


def own_kv(own, others, cosine, sine):
    tokens = own.shape[0]
    kwidth = KV_HEADS * HEAD_DIM

    def kernel(own_ref, *refs):
        other_refs, (cos_ref, sin_ref, out_ref) = refs[:-3], refs[-3:]
        total = own_ref[...]
        for ref in other_refs:
            total = total + ref[...].astype(jnp.float32)
        for tile in range(2 * kwidth // LANES):
            block = total[:, tile * LANES : (tile + 1) * LANES]
            block = turn_back(block, tile, cos_ref[...], sin_ref[...])
            out_ref[:, tile * LANES : (tile + 1) * LANES] = block.astype(jnp.bfloat16)

    return kernel_call(
        kernel, [((tokens, 2 * kwidth), jnp.bfloat16)], [], own, *others, cosine, sine
    )[0]


def input_backward(grad_query, grad_kv, w_qkv, residual, gain, grad_middle):
    tokens = residual.shape[0]
    qwidth = HEADS * HEAD_DIM
    whole = w_qkv.shape[1]

    def kernel(query_ref, kv_ref, w_ref, res_ref, gain_ref, mid_ref, grad_ref, sum_ref, row_ref):
        row_ref[:, :qwidth] = query_ref[...]
        row_ref[:, qwidth:] = kv_ref[...]
        grad = dot_nt(row_ref[...], w_ref[...])
        residual = res_ref[...]
        inverse = lax.rsqrt(jnp.mean(residual * residual, axis=-1, keepdims=True) + EPS)
        scaled = grad * gain_ref[...]
        cubed = inverse * inverse * inverse
        grad_ref[...] = mid_ref[...] + (
            inverse * scaled
            - residual * cubed * jnp.mean(scaled * residual, axis=-1, keepdims=True)
        )
        sum_ref[...] = jnp.sum(grad * residual * inverse, axis=0, keepdims=True)

    return kernel_call(
        kernel,
        [((tokens, D), jnp.float32), ((1, D), jnp.float32)],
        [((tokens, whole), jnp.bfloat16)],
        grad_query, grad_kv, w_qkv, residual, gain, grad_middle,
    )


def attn_grads(
    places, normed_parts, head_mix, grad_query, near_kv, grad_mid, rows, dp_count, ctx_count
):
    parts = len(normed_parts)
    qwidth, kwidth = HEADS * HEAD_DIM, KV_HEADS * HEAD_DIM
    tiles = -(-max(qwidth, D) // LANES)
    runs = attn_pieces(rows, dp_count, ctx_count)
    share = rows * ctx_count

    def kernel(place_ref, *refs):
        normed_refs = refs[:parts]
        mix_ref, query_ref, kv_ref, mid_ref = refs[parts : parts + 4]
        even_ref, odd_ref, long_ref, tile_ref = refs[parts + 4 :]
        near = jnp.concatenate([ref[...] for ref in normed_refs], axis=0)
        for value, matrices in (
            (left_dot(normed_refs[-1][...], query_ref[...]), ((0, qwidth, runs[0]),)),
            (
                left_dot(near, kv_ref[...]),
                ((0, kwidth, runs[1]), (kwidth, kwidth, runs[2])),
            ),
            (left_dot(mix_ref[...], mid_ref[...]), ((0, D, runs[3]),)),
        ):
            span = value.shape[1]
            for tile in range(-(-span // LANES)):
                width = min(LANES, span - tile * LANES)
                tile_ref[tile, :, :width] = value[:, tile * LANES : tile * LANES + width]
            for first, width, matrix in matrices:
                lead, offset = divmod(first // HALF, 2)
                for row, count, base, _ in matrix:
                    def get(tile, parity, lead=lead, row=row, count=count):
                        return tile_ref[lead + tile, pl.ds(row + parity, count // 2, stride=2), :]

                    flat_rows(get, long_ref, base, count // 2, width, offset)
        for mask in range(dp_count):
            ref = odd_ref if mask % 2 else even_ref
            first = pl.multiple_of((place_ref[0] ^ mask) * share, 8)
            chunk = GRAIN

            def move(step, carry, ref=ref, mask=mask, first=first):
                at = pl.multiple_of(step * chunk, 8)
                ref[mask // 2, pl.ds(at, chunk), :] = long_ref[pl.ds(first + at, chunk), :].astype(
                    jnp.bfloat16
                )
                return carry

            lax.fori_loop(0, share // chunk, move, 0)

    half = (dp_count // 2, share, LANES)
    return kernel_call(
        kernel,
        [(half, jnp.bfloat16)] * 2,
        [((dp_count * share, LANES), jnp.float32), ((tiles, D, LANES), jnp.float32)],
        *normed_parts, head_mix, grad_query, near_kv, grad_mid,
        places=places,
    )


def after(value, *others):
    return lax.optimization_barrier((value,) + others)[0]


def from_chips(rows):
    return [(0, rows)] + [
        (mask, lax.ppermute(rows, "dp", swap_pairs("dp", mask)))
        for mask in range(2, lax.axis_size("dp"), 2)
    ]


def with_cores(held):
    return held + [
        (mask + 1, lax.ppermute(array, "dp", swap_pairs("dp", 1))) for mask, array in held
    ]


def reduce_cores(even, odd):
    wide = jnp.float32
    moved = lax.ppermute(odd, "dp", swap_pairs("dp", 1))
    return [
        (even[at].astype(wide) + moved[at].astype(wide)).astype(jnp.bfloat16)
        for at in range(even.shape[0])
    ]


def reduce_chips(sums):
    total = sums[0].astype(jnp.float32)
    for at in range(1, len(sums)):
        moved = lax.ppermute(sums[at], "dp", swap_pairs("dp", 2 * at))
        total = total + moved.astype(jnp.float32)
    return total.astype(jnp.bfloat16)


def body(hidden_in, segments, attn_flat, mlp_flat, norm_one, norm_two, cotangent):
    dp_count, ctx_count = lax.axis_size("dp"), lax.axis_size("ctx")
    if not (
        hidden_in.shape[0] == 1
        and columns_apply(dp_count, ctx_count, mlp_flat.shape[0])
        and attn_fits(attn_flat.shape[0], dp_count, ctx_count)
    ):
        return body_rows(hidden_in, segments, attn_flat, mlp_flat, norm_one, norm_two, cotangent)
    return body_columns(hidden_in, segments, attn_flat, mlp_flat, norm_one, norm_two, cotangent)


def body_columns(hidden_in, segments, attn_flat, mlp_flat, norm_one, norm_two, cotangent):
    tokens = hidden_in.shape[1]
    seq_len = segments.shape[1]
    low = jnp.bfloat16
    dp_count = lax.axis_size("dp")
    ctx_count = lax.axis_size("ctx")
    attn_rows, mlp_rows = attn_flat.shape[0], mlp_flat.shape[0]
    back = -(-(seq_len // 2 - 1) // tokens)
    start_row = lax.axis_index("ctx") * tokens

    places = jnp.stack([lax.axis_index("dp"), lax.axis_index("ctx")]).astype(jnp.int32)
    up_pairs = [
        [(place, place + step) for place in range(ctx_count - step)] for step in range(back + 1)
    ]
    down_pairs = [[(right, left) for left, right in pairs] for pairs in up_pairs]
    residual = hidden_in.reshape(tokens, D)
    cot_rows = cotangent.reshape(tokens, D)
    normed_one = norm_forward(residual, norm_one)[1].astype(low)

    pos_near = lax.dynamic_slice_in_dim(
        jnp.pad(positions_of(segments), ((0, 0), (back * tokens, 0))),
        start_row,
        (back + 1) * tokens,
        1,
    )
    seg_col = lax.dynamic_slice_in_dim(segments, start_row, tokens, 1).reshape(tokens, 1)
    seg_near = lax.dynamic_slice_in_dim(
        jnp.pad(segments, ((0, 0), (back * tokens, 0)), constant_values=-1),
        start_row,
        (back + 1) * tokens,
        1,
    )
    cosine, sine = [table[:, 0] for table in rope_tables(pos_near.reshape(-1))]
    heads = 128 // HEAD_DIM
    cosine = jnp.concatenate([cosine, cosine] * heads, axis=1)
    sine = jnp.concatenate([-sine, sine] * heads, axis=1)
    gain_one, gain_two = norm_one.reshape(1, D), norm_two.reshape(1, D)

    padded = -(-attn_rows // 32) * 32
    flat = jnp.pad(attn_flat, ((0, padded - attn_rows), (0, 0)))
    own_blocks = from_chips(flat)
    others = jnp.concatenate(spread(flat)[1:], axis=0)
    others, window, *arrays = lax.optimization_barrier(
        (others, normed_one, *[array for _, array in own_blocks])
    )
    own_blocks = with_cores([(mask, array) for (mask, _), array in zip(own_blocks, arrays)])
    normed_parts = [
        lax.ppermute(window, "ctx", up_pairs[step]) for step in range(back, 0, -1)
    ] + [normed_one]
    mlp_near = trade_mlp(mlp_flat, others)
    other_blocks = from_chips(others)
    cot_low, cosine, sine, *arrays = lax.optimization_barrier(
        (cot_rows.astype(low), cosine, sine, *[array for _, array in other_blocks], *normed_parts[:-1], mlp_near)
    )
    other_blocks = with_cores([(mask, array) for (mask, _), array in zip(other_blocks, arrays)])
    cot_slots = spread(cot_low)
    held = [(mask, (0,), array) for mask, array in own_blocks]
    held += [(mask, tuple(range(1, ctx_count)), array) for mask, array in other_blocks]

    query, near_kv, w_qkv, w_out = project(
        places, held, normed_parts, cosine, sine, attn_rows, padded, dp_count, ctx_count
    )
    mlp_near = after(mlp_near, *[array for _, _, array in held])
    mlp_whole = lax.all_gather(mlp_near, "dp", axis=0, tiled=True)
    head_mix, logs, middle, normed_two = attend(
        query, near_kv, seg_col, seg_near, residual, w_out, gain_two
    )
    two_slots = spread(normed_two)

    w_gate, w_up, w_down, grad_active = unpack_mlp(
        mlp_whole, cot_slots, mlp_rows, dp_count, ctx_count
    )
    active, grad_gate, grad_up, *two_terms = feed_forward(two_slots, w_gate, w_up, grad_active)
    two_others = returned(two_terms[1:])
    mlp_even, mlp_odd, block_own, *block_terms = mlp_grads(
        places, active, grad_gate, grad_up, two_slots, cot_slots, w_down, mlp_rows, dp_count, ctx_count
    )
    mlp_sums = reduce_cores(mlp_even, after(mlp_odd, *two_others))
    block_others = returned([after(term, *two_others) for term in block_terms])
    grad_middle, grad_mid_low, grad_mix, grad_gain_two = middle_backward(
        after(two_terms[0], mlp_even), two_others, middle, gain_two, cot_rows, w_out
    )
    grad_query, near_grads, kv_own, *kv_terms = attend_backward(
        query, near_kv, after(grad_mix, *mlp_sums), logs, seg_col, seg_near, cosine, sine
    )
    kv_others = [
        lax.ppermute(kv_terms[back - step], "ctx", down_pairs[step]) for step in range(1, back + 1)
    ]
    even, odd = attn_grads(
        places, normed_parts, head_mix, grad_query, near_grads, grad_mid_low,
        attn_rows, dp_count, ctx_count,
    )
    mlp_own = reduce_chips([after(mlp_sums[0], odd)] + mlp_sums[1:])
    sums = reduce_cores(even, after(odd, mlp_own, *block_others[:-1]))
    block_rows = middle + block_own
    for moved in block_others:
        block_rows = block_rows + moved.astype(jnp.float32)
    mlp_grad = scatter_mlp(after(mlp_own, *sums))
    total = reduce_chips([after(sums[0], *kv_others, block_others[-1])] + sums[1:])
    attn_blocks = trade(total.reshape(ctx_count, -1, 128))
    kv_own = after(kv_own, *attn_blocks[1:])
    grad_kv = own_kv(kv_own, kv_others, cosine[-tokens:], sine[-tokens:])
    grad_in, grad_gain_one = input_backward(
        grad_query, grad_kv, w_qkv, residual, gain_one, grad_middle
    )
    gains = jnp.concatenate([grad_gain_one, grad_gain_two], axis=0)
    gains = add_swapped(gains, "dp", (1,))
    gains = add_swapped(gains, "dp", range(2, dp_count, 2))
    gain_sums = add_swapped(gains, "ctx", range(1, ctx_count))
    attn_grad = 0.0
    for block in attn_blocks:
        attn_grad = attn_grad + block.astype(jnp.float32)
    return (
        block_rows.reshape(hidden_in.shape),
        grad_in.reshape(hidden_in.shape),
        attn_grad,
        mlp_grad,
        gain_sums[0],
        gain_sums[1],
    )


def solution(mesh):
    in_specs = (
        P("dp", "ctx", None),
        P("dp", None),
        P(("dp", "ctx"), None),
        P(("dp", "ctx"), None),
        P(),
        P(),
        P("dp", "ctx", None),
    )
    out_specs = (
        P("dp", "ctx", None),
        P("dp", "ctx", None),
        P(("dp", "ctx"), None),
        P(("dp", "ctx"), None),
        P(),
        P(),
    )
    return jax.shard_map(body, mesh=mesh, in_specs=in_specs, out_specs=out_specs, check_vma=False)
```

```python
import jax
import jax.numpy as jnp
from jax import lax
from jax.experimental import pallas as pl
from jax.experimental.pallas import tpu as pltpu
from jax.sharding import PartitionSpec as P

D = 960
HEADS = 15
KV_HEADS = 5
HEAD_DIM = 64
FFN = 2560


EPS = 1e-05
THETA = 100000.0


def positions_of(segment_ids):
    earlier = (segment_ids[..., None, :] < segment_ids[..., :, None]).astype(jnp.int32)
    total_len = segment_ids.shape[-1]
    return jnp.arange(total_len, dtype=jnp.int32) - jnp.sum(earlier, axis=-1)


def rope_tables(positions):
    half_dim = HEAD_DIM // 2
    frequency = THETA ** (-2.0 * jnp.arange(half_dim, dtype=jnp.float32) / HEAD_DIM)
    angles = positions.astype(jnp.float32)[:, None] * frequency[None, :]
    return (jnp.cos(angles)[:, None, :], jnp.sin(angles)[:, None, :])


def rotate(vectors, cosine_table, sine_table):
    half_dim = vectors.shape[-1] // 2
    lower_half = vectors[..., :half_dim]
    upper_half = vectors[..., half_dim:]
    return jnp.concatenate(
        [
            lower_half * cosine_table - upper_half * sine_table,
            upper_half * cosine_table + lower_half * sine_table,
        ],
        axis=-1,
    )


def unrotate(grad_rows, cosine_table, sine_table):
    half_dim = grad_rows.shape[-1] // 2
    lower_half = grad_rows[..., :half_dim]
    upper_half = grad_rows[..., half_dim:]
    return jnp.concatenate(
        [
            lower_half * cosine_table + upper_half * sine_table,
            upper_half * cosine_table - lower_half * sine_table,
        ],
        axis=-1,
    )


def unpack_blocks(flat_rows, shapes, dp_count, ctx_count):
    pieces = flat_rows.reshape(dp_count, ctx_count, -1).transpose(1, 0, 2).reshape(ctx_count, -1)
    matrices = []
    offset = 0
    for height, width_cols in shapes:
        length = height * width_cols // ctx_count
        matrices.append(pieces[:, offset : offset + length].reshape(height, width_cols))
        offset = offset + length
    return matrices


def norm_forward(residual, gain_vec):
    inverse = lax.rsqrt(jnp.mean(residual * residual, axis=-1, keepdims=True) + EPS)
    return (inverse, residual * inverse * gain_vec)


def norm_backward(residual, inverse, gain_vec, grad_normed):
    scaled = grad_normed * gain_vec
    cubed = inverse * inverse * inverse
    grad_resid = inverse * scaled - residual * cubed * jnp.mean(
        scaled * residual, axis=-1, keepdims=True
    )
    grad_gain = jnp.sum(grad_normed * residual * inverse, axis=0)
    return (grad_resid, grad_gain)


def masked_scores(query_rot, key_whole, allowed, score_scale):
    scores = (
        jnp.einsum("sqkgd,slkd->skgql", query_rot, key_whole, preferred_element_type=jnp.float32)
        * score_scale
    )
    return jnp.where(allowed, scores, -jnp.inf)


def left_dot(left_cols, right_rows):
    return lax.dot_general(
        left_cols, right_rows, (((0,), (0,)), ((), ())), preferred_element_type=jnp.float32
    )


def body_rows(hidden_in, segments, attn_flat, mlp_flat, norm_one, norm_two, cotangent):
    seq_count, local_len, model_width = hidden_in.shape
    seq_len = segments.shape[1]
    row_count = seq_count * local_len
    groups = HEADS // KV_HEADS
    qwidth = HEADS * HEAD_DIM
    kwidth = KV_HEADS * HEAD_DIM
    score_scale = HEAD_DIM ** (-0.5)
    low = jnp.bfloat16
    wide = jnp.float32
    dp_count = lax.axis_size("dp")
    ctx_count = lax.axis_size("ctx")
    attn_shapes = ((D, qwidth), (D, kwidth), (D, kwidth), (qwidth, D))
    mlp_shapes = ((D, FFN), (D, FFN), (FFN, D))
    start_row = lax.axis_index("ctx") * local_len
    attn_whole, mlp_whole = (
        lax.all_gather(attn_flat, ("dp", "ctx"), axis=0, tiled=True),
        lax.all_gather(mlp_flat, ("dp", "ctx"), axis=0, tiled=True),
    )
    w_query, w_key, w_value, w_out = unpack_blocks(attn_whole, attn_shapes, dp_count, ctx_count)
    w_gate, w_up, w_down = unpack_blocks(mlp_whole, mlp_shapes, dp_count, ctx_count)
    pos_all = positions_of(segments)
    pos_local = lax.dynamic_slice_in_dim(pos_all, start_row, local_len, 1)
    seg_local = lax.dynamic_slice_in_dim(segments, start_row, local_len, 1)
    cosine_table, sine_table = rope_tables(pos_local.reshape(-1))
    key_index = jnp.arange(seq_len, dtype=jnp.int32)
    query_index = start_row + jnp.arange(local_len, dtype=jnp.int32)
    allowed = (seg_local[:, :, None] == segments[:, None, :]) & (
        key_index[None, None, :] <= query_index[None, :, None]
    )
    allowed = allowed[:, None, None]
    residual = hidden_in.reshape(row_count, model_width)
    inv_one, normed_one = norm_forward(residual, norm_one)
    normed_one = normed_one.astype(low)
    query = jnp.dot(normed_one, w_query, preferred_element_type=wide).reshape(
        row_count, HEADS, HEAD_DIM
    )
    key_raw = jnp.dot(normed_one, w_key, preferred_element_type=wide).reshape(
        row_count, KV_HEADS, HEAD_DIM
    )
    value_low = jnp.dot(normed_one, w_value, preferred_element_type=wide).astype(low)
    query_rot = (
        rotate(query, cosine_table, sine_table)
        .astype(low)
        .reshape(seq_count, local_len, KV_HEADS, groups, HEAD_DIM)
    )
    key_rot = rotate(key_raw, cosine_table, sine_table).astype(low)
    kv_local = jnp.concatenate(
        [
            key_rot.reshape(seq_count, local_len, kwidth),
            value_low.reshape(seq_count, local_len, kwidth),
        ],
        axis=2,
    )
    kv_whole = lax.all_gather(kv_local, "ctx", axis=1, tiled=True)
    key_whole = kv_whole[:, :, :kwidth].reshape(seq_count, seq_len, KV_HEADS, HEAD_DIM)
    value_whole = kv_whole[:, :, kwidth:].reshape(seq_count, seq_len, KV_HEADS, HEAD_DIM)
    scores = masked_scores(query_rot, key_whole, allowed, score_scale)
    row_top = jnp.max(scores, axis=-1, keepdims=True)
    log_total = row_top + jnp.log(jnp.sum(jnp.exp(scores - row_top), axis=-1, keepdims=True))
    probs_low = jnp.exp(scores - log_total).astype(low)
    head_mix = jnp.einsum("skgql,slkd->sqkgd", probs_low, value_whole, preferred_element_type=wide)
    head_mix = head_mix.reshape(row_count, qwidth).astype(low)
    middle = residual + jnp.dot(head_mix, w_out, preferred_element_type=wide)
    inv_two, normed_two = norm_forward(middle, norm_two)
    normed_two = normed_two.astype(low)
    gate_pre = jnp.dot(normed_two, w_gate, preferred_element_type=wide)
    up_proj = jnp.dot(normed_two, w_up, preferred_element_type=wide)
    gate_sigmoid = jax.nn.sigmoid(gate_pre)
    active = (gate_pre * gate_sigmoid * up_proj).astype(low)
    block_rows = middle + jnp.dot(active, w_down, preferred_element_type=wide)
    one_cols, mix_cols, two_cols, active_cols = (
        lax.all_to_all(normed_one, "ctx", split_axis=1, concat_axis=0, tiled=True),
        lax.all_to_all(head_mix, "ctx", split_axis=1, concat_axis=0, tiled=True),
        lax.all_to_all(normed_two, "ctx", split_axis=1, concat_axis=0, tiled=True),
        lax.all_to_all(active, "ctx", split_axis=1, concat_axis=0, tiled=True),
    )
    cot_rows = cotangent.reshape(row_count, model_width)
    cot_low = cot_rows.astype(low)
    grad_active = jnp.dot(cot_low, w_down.T, preferred_element_type=wide)
    grad_gate = (
        grad_active * up_proj * gate_sigmoid * (1.0 + gate_pre * (1.0 - gate_sigmoid))
    ).astype(low)
    grad_up = (grad_active * gate_pre * gate_sigmoid).astype(low)
    grad_normed_two = jnp.dot(grad_gate, w_gate.T, preferred_element_type=wide) + jnp.dot(
        grad_up, w_up.T, preferred_element_type=wide
    )
    grad_middle, grad_gain_two = norm_backward(middle, inv_two, norm_two, grad_normed_two)
    grad_middle = cot_rows + grad_middle
    grad_mid_low = grad_middle.astype(low)
    grad_mix = jnp.dot(grad_mid_low, w_out.T, preferred_element_type=wide).astype(low)
    grad_mix = grad_mix.reshape(seq_count, local_len, KV_HEADS, groups, HEAD_DIM)
    attn_probs = jnp.exp(masked_scores(query_rot, key_whole, allowed, score_scale) - log_total)
    probs_low = attn_probs.astype(low)
    grad_probs = jnp.einsum("sqkgd,slkd->skgql", grad_mix, value_whole, preferred_element_type=wide)
    grad_value_all = jnp.einsum(
        "skgql,sqkgd->slkd", probs_low, grad_mix, preferred_element_type=wide
    )
    grad_scores = attn_probs * (
        grad_probs - jnp.sum(attn_probs * grad_probs, axis=-1, keepdims=True)
    )
    grad_scores_low = (grad_scores * score_scale).astype(low)
    grad_query = jnp.einsum(
        "skgql,slkd->sqkgd", grad_scores_low, key_whole, preferred_element_type=wide
    )
    grad_key_all = jnp.einsum(
        "skgql,sqkgd->slkd", grad_scores_low, query_rot, preferred_element_type=wide
    )
    kv_terms = jnp.concatenate(
        [
            grad_key_all.reshape(seq_count, seq_len, kwidth),
            grad_value_all.reshape(seq_count, seq_len, kwidth),
        ],
        axis=2,
    )
    kv_owned = lax.psum_scatter(
        kv_terms.astype(jnp.bfloat16), "ctx", scatter_dimension=1, tiled=True
    ).astype(jnp.float32)
    grad_key = kv_owned[:, :, :kwidth].reshape(row_count, KV_HEADS, HEAD_DIM)
    grad_value = kv_owned[:, :, kwidth:].reshape(row_count, kwidth).astype(low)
    grad_query = (
        unrotate(grad_query.reshape(row_count, HEADS, HEAD_DIM), cosine_table, sine_table)
        .reshape(row_count, qwidth)
        .astype(low)
    )
    grad_key = unrotate(grad_key, cosine_table, sine_table).reshape(row_count, kwidth).astype(low)
    grad_normed_one = (
        jnp.dot(grad_query, w_query.T, preferred_element_type=wide)
        + jnp.dot(grad_key, w_key.T, preferred_element_type=wide)
        + jnp.dot(grad_value, w_value.T, preferred_element_type=wide)
    )
    grad_resid, grad_gain_one = norm_backward(residual, inv_one, norm_one, grad_normed_one)
    grad_resid = grad_middle + grad_resid
    gathered = (
        lax.all_gather(grad_query, "ctx", axis=0, tiled=True),
        lax.all_gather(grad_key, "ctx", axis=0, tiled=True),
        lax.all_gather(grad_value, "ctx", axis=0, tiled=True),
        lax.all_gather(grad_mid_low, "ctx", axis=0, tiled=True),
        lax.all_gather(grad_gate, "ctx", axis=0, tiled=True),
        lax.all_gather(grad_up, "ctx", axis=0, tiled=True),
        lax.all_gather(cot_low, "ctx", axis=0, tiled=True),
    )
    all_query, all_key, all_value, all_mid, all_gate, all_up, all_cot = gathered
    attn_terms = jnp.concatenate(
        [
            left_dot(one_cols, all_query).reshape(-1),
            left_dot(one_cols, all_key).reshape(-1),
            left_dot(one_cols, all_value).reshape(-1),
            left_dot(mix_cols, all_mid).reshape(-1),
        ]
    ).reshape(-1, 128)
    mlp_terms = jnp.concatenate(
        [
            left_dot(two_cols, all_gate).reshape(-1),
            left_dot(two_cols, all_up).reshape(-1),
            left_dot(active_cols, all_cot).reshape(-1),
        ]
    ).reshape(-1, 128)
    attn_grad, mlp_grad = (
        lax.psum_scatter(
            attn_terms.astype(jnp.bfloat16), "dp", scatter_dimension=0, tiled=True
        ).astype(jnp.float32),
        lax.psum_scatter(
            mlp_terms.astype(jnp.bfloat16), "dp", scatter_dimension=0, tiled=True
        ).astype(jnp.float32),
    )
    gain_sums = lax.psum(jnp.stack([grad_gain_one, grad_gain_two]), ("dp", "ctx"))
    return (
        block_rows.reshape(seq_count, local_len, model_width),
        grad_resid.reshape(seq_count, local_len, model_width),
        attn_grad,
        mlp_grad,
        gain_sums[0],
        gain_sums[1],
    )


def add_swapped(rows, axis, masks):
    total = rows
    for mask in masks:
        total = total + lax.ppermute(rows, axis, swap_pairs(axis, mask))
    return total


def swap_pairs(axis, step):
    return [(place, place ^ step) for place in range(lax.axis_size(axis))]


def spread(rows):
    return [rows] + [
        lax.ppermute(rows, "ctx", swap_pairs("ctx", step)) for step in range(1, lax.axis_size("ctx"))
    ]


def returned(terms):
    return [
        lax.ppermute(term, "ctx", swap_pairs("ctx", step + 1)) for step, term in enumerate(terms)
    ]


def trade(blocks, *before):
    here = lax.axis_index("ctx")
    got = [lax.dynamic_index_in_dim(blocks, here, 0, False)]
    for step in range(1, lax.axis_size("ctx")):
        block = lax.dynamic_index_in_dim(blocks, here ^ step, 0, False)
        block = after(block, *before)
        got.append(lax.ppermute(block, "ctx", swap_pairs("ctx", step)))
    return got


def in_order(pieces):
    here = lax.axis_index("ctx")
    step = 1
    while step < len(pieces):
        bit = (here & step) != 0
        pieces = [
            jnp.where(bit, pieces[place ^ step], pieces[place]) for place in range(len(pieces))
        ]
        step = 2 * step
    return jnp.stack(pieces)


def columns_apply(dp_count, ctx_count, rows):
    unit = FFN // 128
    return (
        rows % unit == 0
        and FFN % (128 * ctx_count) == 0
        and D % ctx_count == 0
        and ctx_count & (ctx_count - 1) == 0
        and dp_count & (dp_count - 1) == 0
        and rows % ctx_count == 0
        and (2 * (D // ctx_count) % (rows // unit)) * unit % ctx_count == 0
        and (rows - (2 * (D // ctx_count) % (rows // unit)) * unit) % (ctx_count * 2 * D // 128) == 0
        and rows % (2 * D // 128) == 0
    )


def mlp_sizes(rows, ctx_count):
    unit = FFN // 128
    held = rows // unit
    tall = 2 * (D // ctx_count)
    return unit, unit // ctx_count, held, tall // held, tall % held


def trade_mlp(flat, *before):
    ctx_count = lax.axis_size("ctx")
    place = lax.axis_index("dp")
    rows = flat.shape[0]
    unit, part, held, edge, rest = mlp_sizes(rows, ctx_count)
    cut = rest * unit

    def by_column(block, count):
        return (
            block.reshape(count, ctx_count, part, 128)
            .transpose(1, 0, 2, 3)
            .reshape(ctx_count, count * part, 128)
        )

    full = by_column(flat, held)
    tail = flat[cut:].reshape(ctx_count, -1, 128)
    mixed = jnp.concatenate([by_column(flat[:cut], rest), tail], axis=1)
    got = in_order(trade(jnp.where(place < edge, full, mixed), *before))
    kept = jnp.concatenate([got[:, : rest * part], tail], axis=1)
    block = jnp.where(
        place < edge, got, jnp.where(place == edge, kept, flat.reshape(ctx_count, -1, 128))
    )
    return block.reshape(rows, 128)


def scatter_mlp(own):
    ctx_count = lax.axis_size("ctx")
    place = lax.axis_index("dp")
    rows = own.shape[0]
    unit, part, held, edge, rest = mlp_sizes(rows, ctx_count)
    blocks = own.reshape(ctx_count, rows // ctx_count, 128)
    got = in_order(trade(blocks))

    def by_row(block, count):
        return block.reshape(ctx_count, count, part, 128).transpose(1, 0, 2, 3).reshape(-1, 128)

    full = by_row(got, held)
    mixed = jnp.concatenate(
        [by_row(got[:, : rest * part], rest), blocks[:, rest * part :].reshape(-1, 128)], axis=0
    )
    out = jnp.where(place < edge, full, jnp.where(place == edge, mixed, own))
    return out.astype(jnp.float32)


VMEM_BYTES = 56 * 1024 * 1024
LANES = 128
HALF = LANES // 2
GRAIN = 160


def kernel_call(kernel, outs, scratch, *args, places=None):
    specs = [pl.BlockSpec(memory_space=pltpu.VMEM) for _ in args]
    if places is not None:
        specs = [pl.BlockSpec(memory_space=pltpu.SMEM)] + specs
        args = (places,) + args
    return pl.pallas_call(
        kernel,
        in_specs=specs,
        out_shape=[jax.ShapeDtypeStruct(shape, dtype) for shape, dtype in outs],
        scratch_shapes=[pltpu.VMEM(shape, dtype) for shape, dtype in scratch],
        compiler_params=pltpu.CompilerParams(vmem_limit_bytes=VMEM_BYTES),
    )(*args)


def low_lanes(rows):
    return lax.broadcasted_iota(jnp.int32, (rows, LANES), 1) < HALF


def dot_nt(left, right):
    return lax.dot_general(
        left, right, (((1,), (1,)), ((), ())), preferred_element_type=jnp.float32
    )


def dot_nn(left, right):
    return jnp.dot(left, right, preferred_element_type=jnp.float32)


def pair_rows(flat_ref, base, pairs, width, offset, put):
    halves = width // HALF
    tiles = [flat_ref[pl.ds(base + step, pairs, stride=halves), :] for step in range(halves)]
    rolled = {}
    mask = low_lanes(pairs)

    def roll(index):
        index = min(max(index, 0), halves - 1)
        if index not in rolled:
            rolled[index] = pltpu.roll(tiles[index], HALF, 1)
        return rolled[index]

    for parity in range(2):
        for tile in range((halves + offset + 1) // 2):
            first = parity * halves - offset + 2 * tile
            if first % 2 == 0:
                put(tile, parity, tiles[first // 2])
            else:
                put(tile, parity, jnp.where(mask, roll(first // 2), roll(first // 2 + 1)))


def flat_rows(get, flat_ref, base, pairs, width, offset):
    halves = width // HALF
    mask = low_lanes(pairs)
    blocks, rolled = {}, {}

    def half(index, want):
        parity, index = divmod(index, halves)
        tile, side = divmod(index + offset, 2)
        key = (tile, parity)
        if key not in blocks:
            blocks[key] = get(tile, parity)
        if side == want:
            return blocks[key]
        if key not in rolled:
            rolled[key] = pltpu.roll(blocks[key], HALF, 1)
        return rolled[key]

    for step in range(halves):
        left, right = half(2 * step, 0), half(2 * step + 1, 1)
        flat_ref[pl.ds(base + step, pairs, stride=halves), :] = (
            left if left is right else jnp.where(mask, left, right)
        )


def partner_lanes(block):
    quarter = HEAD_DIM // 2
    lane = lax.broadcasted_iota(jnp.int32, block.shape, 1)
    return jnp.where(
        (lane & quarter) == 0,
        pltpu.roll(block, LANES - quarter, 1),
        pltpu.roll(block, quarter, 1),
    )


def attn_pieces(rows, dp_count, ctx_count, stride=None):
    runs = []
    begin = 0
    for height, width in (
        (D, HEADS * HEAD_DIM),
        (D, KV_HEADS * HEAD_DIM),
        (D, KV_HEADS * HEAD_DIM),
        (HEADS * HEAD_DIM, D),
    ):
        block = height // ctx_count
        span = block * width // LANES
        matrix = []
        for ctx in range(ctx_count):
            at = begin
            while at < begin + span:
                part, inside = divmod(at, rows)
                size = min(rows - inside, begin + span - at)
                matrix.append(
                    (
                        ctx * block + (at - begin) * LANES // width,
                        size * LANES // width,
                        (part * ctx_count + ctx) * (stride or rows) + inside,
                        size,
                    )
                )
                at = at + size
        runs.append(matrix)
        begin = begin + span
    return runs


def attn_fits(rows, dp_count, ctx_count):
    widths = (HEADS * HEAD_DIM, KV_HEADS * HEAD_DIM, KV_HEADS * HEAD_DIM, D)
    return D % ctx_count == 0 and all(
        (2 * width) % LANES == 0
        and (width // HALF) % 2 == 1
        and size % (2 * width // LANES) == 0
        and row % 2 == 0
        and (rows * ctx_count) % GRAIN == 0
        for width, matrix in zip(widths, attn_pieces(rows, dp_count, ctx_count))
        for row, _, _, size in matrix
    )


def project(places, held, normed_parts, cosine, sine, used, rows, dp_count, ctx_count):
    parts = len(normed_parts)
    tokens = normed_parts[-1].shape[0]
    near_len = parts * tokens
    qwidth, kwidth = HEADS * HEAD_DIM, KV_HEADS * HEAD_DIM
    whole = qwidth + 2 * kwidth
    runs = attn_pieces(used, dp_count, ctx_count, rows)
    total = rows * dp_count * ctx_count
    qtiles = -(-qwidth // LANES)
    ktile, koff = divmod(qwidth // HALF, 2)
    vtile, voff = divmod((qwidth + kwidth) // HALF, 2)
    ktiles = (kwidth // HALF + koff + 1) // 2
    vtiles = (kwidth // HALF + voff + 1) // 2

    def kernel(place_ref, *refs):
        held_refs = refs[: len(held)]
        normed_refs = refs[len(held) : len(held) + parts]
        cos_ref, sin_ref = refs[len(held) + parts : len(held) + parts + 2]
        query_ref, kv_ref, wide_ref, out_ref, long_ref, tile_ref = refs[len(held) + parts + 2 :]
        for (dp_mask, ctx_masks, _), ref in zip(held, held_refs):
            def move(step, carry, dp_mask=dp_mask, lead=ctx_masks[0], ref=ref):
                block = (place_ref[0] ^ dp_mask) * ctx_count + (place_ref[1] ^ (lead + step // 2))
                first = pl.multiple_of(block * rows + (step % 2) * (rows // 2), 16)
                long_ref[pl.ds(first, rows // 2), :] = ref[
                    pl.ds(pl.multiple_of(step * (rows // 2), 16), rows // 2), :
                ].astype(jnp.float32)
                return carry

            lax.fori_loop(0, 2 * len(ctx_masks), move, 0)
        slots = ((0, 0, 0), (qtiles, koff, ktile), (qtiles + ktiles, voff, vtile))
        for (slot, offset, _), matrix, width in zip(slots, runs, (qwidth, kwidth, kwidth)):
            for row, count, base, size in matrix:
                def put(tile, parity, block, slot=slot, row=row, count=count):
                    tile_ref[slot + tile, pl.ds(row + parity, count // 2, stride=2), :] = block

                pair_rows(long_ref, base, count // 2, width, offset, put)
        mask = low_lanes(D)
        for tile in range(-(-whole // LANES)):
            found = [
                tile_ref[slot + tile - first]
                for (slot, _, first), count in zip(slots, (qtiles, ktiles, vtiles))
                if first <= tile < first + count
            ]
            block = found[0] if len(found) == 1 else jnp.where(mask, found[0], found[1])
            width = min(LANES, whole - tile * LANES)
            wide_ref[:, tile * LANES : tile * LANES + width] = block[:, :width].astype(jnp.bfloat16)
        product = dot_nn(normed_refs[-1][...], wide_ref[:, : qtiles * LANES])
        here = slice(near_len - tokens, near_len)
        for tile in range(qtiles):
            width = min(LANES, qwidth - tile * LANES)
            block = product[:, tile * LANES : (tile + 1) * LANES]
            block = block * cos_ref[here, :] + partner_lanes(block) * sin_ref[here, :]
            query_ref[:, tile * LANES : tile * LANES + width] = block[:, :width].astype(jnp.bfloat16)
        near = jnp.concatenate([ref[...] for ref in normed_refs], axis=0)
        product = dot_nn(near, wide_ref[:, ktile * LANES :])
        lead = qwidth - ktile * LANES
        turned = []
        for tile in range((lead + kwidth) // LANES):
            block = product[:, tile * LANES : (tile + 1) * LANES]
            turned.append(
                (block * cos_ref[...] + partner_lanes(block) * sin_ref[...]).astype(jnp.bfloat16)
            )
        kv_ref[:, :kwidth] = jnp.concatenate(turned, axis=1)[:, lead:]
        kv_ref[:, kwidth:] = product[:, lead + kwidth :].astype(jnp.bfloat16)
        for row, count, base, size in runs[3]:
            def put(tile, parity, block, row=row, count=count):
                tile_ref[tile, pl.ds(row + parity, count // 2, stride=2), :] = block

            pair_rows(long_ref, base, count // 2, D, 0, put)
        for tile in range(-(-D // LANES)):
            width = min(LANES, D - tile * LANES)
            out_ref[:, tile * LANES : tile * LANES + width] = tile_ref[tile][:, :width].astype(
                jnp.bfloat16
            )

    low = jnp.bfloat16
    return kernel_call(
        kernel,
        [
            ((tokens, qwidth), low),
            ((near_len, 2 * kwidth), low),
            ((D, whole), low),
            ((qwidth, D), low),
        ],
        [((total, LANES), jnp.float32), ((qtiles + ktiles + vtiles, D, LANES), jnp.float32)],
        *[array for _, _, array in held], *normed_parts, cosine, sine,
        places=places,
    )


def group_rows(ref, group, groups):
    first = group * groups * HEAD_DIM
    return jnp.concatenate(
        [ref[:, first + g * HEAD_DIM : first + (g + 1) * HEAD_DIM] for g in range(groups)], axis=0
    )


def group_allowed(seg_ref, near_ref, tokens, near_len, groups):
    query = lax.broadcasted_iota(jnp.int32, (tokens, near_len), 0)
    key = lax.broadcasted_iota(jnp.int32, (tokens, near_len), 1) - (near_len - tokens)
    allowed = (seg_ref[...] == near_ref[...]) & (key <= query)
    return allowed


def attend(query, near_kv, seg_col, seg_near, residual, w_out, gain):
    tokens = query.shape[0]
    near_len = near_kv.shape[0]
    groups = HEADS // KV_HEADS
    kwidth = KV_HEADS * HEAD_DIM
    scale = HEAD_DIM ** (-0.5)

    def kernel(
        query_ref, near_kv_ref, seg_ref, near_ref, res_ref, out_ref, gain_ref,
        mix_ref, log_ref, mid_ref, normed_ref,
    ):
        allowed = group_allowed(seg_ref, near_ref, tokens, near_len, groups)
        allowed = jnp.concatenate([allowed.astype(jnp.float32)] * groups, axis=0) > 0.5
        mixes, logs = [], []
        for group in range(KV_HEADS):
            at = group * HEAD_DIM
            key = near_kv_ref[:, at : at + HEAD_DIM]
            value = near_kv_ref[:, kwidth + at : kwidth + at + HEAD_DIM]
            scores = dot_nt(group_rows(query_ref, group, groups), key) * scale
            scores = jnp.where(allowed, scores, -jnp.inf)
            top = jnp.max(scores, axis=-1, keepdims=True)
            total = top + jnp.log(jnp.sum(jnp.exp(scores - top), axis=-1, keepdims=True))
            probs = jnp.exp(scores - total).astype(jnp.bfloat16)
            mix = dot_nn(probs, value).astype(jnp.bfloat16)
            for g in range(groups):
                mixes.append(mix[g * tokens : (g + 1) * tokens])
                logs.append(total[g * tokens : (g + 1) * tokens])
        for head in range(HEADS):
            log_ref[:, head : head + 1] = logs[head]
        head_mix = jnp.concatenate(mixes, axis=1)
        mix_ref[...] = head_mix
        middle = res_ref[...] + dot_nn(head_mix, out_ref[...])
        mid_ref[...] = middle
        inverse = lax.rsqrt(jnp.mean(middle * middle, axis=-1, keepdims=True) + EPS)
        normed_ref[...] = (middle * inverse * gain_ref[...]).astype(jnp.bfloat16)

    low, wide = jnp.bfloat16, jnp.float32
    return kernel_call(
        kernel,
        [
            ((tokens, HEADS * HEAD_DIM), low),
            ((tokens, LANES), wide),
            ((tokens, D), wide),
            ((tokens, D), low),
        ],
        [],
        query, near_kv, seg_col, seg_near, residual, w_out, gain,
    )


def mlp_pieces(rows, dp_count, ctx_count):
    unit, part, held, edge, rest = mlp_sizes(rows, ctx_count)
    share = rows // ctx_count
    block = D // ctx_count
    gate, up, down = [], [], []
    for ctx in range(ctx_count):
        for dp in range(edge + (rest > 0)):
            count = held if dp < edge else rest
            row, stop = dp * held, dp * held + count
            base = (dp * ctx_count + ctx) * share
            for matrix, begin, end in ((gate, 0, block), (up, block, 2 * block)):
                low, high = max(row, begin), min(stop, end)
                if low < high:
                    matrix.append((ctx * block + low - begin, high - low, base + (low - row) * part))
    cut = rest * part
    at = 0
    for ctx in range(ctx_count):
        size = share - cut
        down.append((at * LANES // D, size * LANES // D, (edge * ctx_count + ctx) * share + cut))
        at = at + size
    for dp in range(edge + 1, dp_count):
        down.append((at * LANES // D, rows * LANES // D, dp * rows))
        at = at + rows
    return part, gate, up, down


def unpack_mlp(flat, cot_slots, rows, dp_count, ctx_count):
    part, gate, up, down = mlp_pieces(rows, dp_count, ctx_count)
    hidden = part * LANES
    tiles = -(-D // LANES)
    tokens = cot_slots[0].shape[0]
    count = len(cot_slots)

    def kernel(flat_ref, *refs):
        cot_refs = refs[:count]
        gate_ref, up_ref, down_ref, act_ref, long_ref, tile_ref, turn_ref = refs[count:]
        long_ref[...] = flat_ref[...].astype(jnp.float32)
        for row, size, base in down:
            def put(tile, parity, block, row=row, size=size):
                tile_ref[tile, pl.ds(row + parity, size // 2, stride=2), :] = block

            pair_rows(long_ref, base, size // 2, D, 0, put)
        for tile in range(tiles):
            width = min(LANES, D - tile * LANES)
            down_ref[:, tile * LANES : tile * LANES + width] = tile_ref[tile][:, :width].astype(
                jnp.bfloat16
            )
        for slot in range(count):
            act_ref[slot * tokens : (slot + 1) * tokens, :] = dot_nt(
                cot_refs[slot][...], down_ref[...]
            )
        for runs, ref in ((gate, gate_ref), (up, up_ref)):
            for row, size, base in runs:
                for step in range(part):
                    turn_ref[step, row : row + size, :] = long_ref[
                        pl.ds(base + step, size, stride=part), :
                    ]
            for step in range(part):
                ref[:, step * LANES : (step + 1) * LANES] = turn_ref[step].astype(jnp.bfloat16)

    low, wide = jnp.bfloat16, jnp.float32
    return kernel_call(
        kernel,
        [
            ((D, hidden), low),
            ((D, hidden), low),
            ((hidden, D), low),
            ((count * tokens, hidden), wide),
        ],
        [
            (flat.shape, wide),
            ((tiles, hidden, LANES), wide),
            ((part, D, LANES), wide),
        ],
        flat, *cot_slots,
    )


def feed_forward(two_slots, w_gate, w_up, grad_active):
    count = len(two_slots)
    tokens = two_slots[0].shape[0]
    hidden = w_gate.shape[1]

    def kernel(*refs):
        two_refs = refs[:count]
        gate_ref, up_ref, act_ref = refs[count : count + 3]
        active_ref, dgate_ref, dup_ref, own_ref = refs[count + 3 : count + 7]
        term_refs = refs[count + 7 :]
        for slot in list(range(1, count)) + [0]:
            rows = slice(slot * tokens, (slot + 1) * tokens)
            two = two_refs[slot][...]
            gate = dot_nn(two, gate_ref[...])
            up = dot_nn(two, up_ref[...])
            grad = act_ref[rows, :]
            sigmoid = jax.nn.sigmoid(gate)
            active_ref[rows, :] = (gate * sigmoid * up).astype(jnp.bfloat16)
            dgate = (grad * up * sigmoid * (1.0 + gate * (1.0 - sigmoid))).astype(jnp.bfloat16)
            dup = (grad * gate * sigmoid).astype(jnp.bfloat16)
            dgate_ref[rows, :] = dgate
            dup_ref[rows, :] = dup
            term = dot_nt(dgate, gate_ref[...]) + dot_nt(dup, up_ref[...])
            if slot:
                term_refs[slot - 1][...] = term.astype(jnp.bfloat16)
            else:
                own_ref[...] = term

    low, wide = jnp.bfloat16, jnp.float32
    return kernel_call(
        kernel,
        [((count * tokens, hidden), low)] * 3
        + [((tokens, D), wide)]
        + [((tokens, D), low)] * (count - 1),
        [],
        *two_slots, w_gate, w_up, grad_active,
    )


def mlp_grads(places, active, dgate, dup, two_slots, cot_slots, w_down, rows, dp_count, ctx_count):
    count = len(two_slots)
    tokens = two_slots[0].shape[0]
    part, gate_runs, up_runs, down_runs = mlp_pieces(rows, dp_count, ctx_count)
    tiles = -(-D // LANES)
    hidden = part * LANES

    def kernel(place_ref, *refs):
        active_ref, dgate_ref, dup_ref = refs[:3]
        two_refs = refs[3 : 3 + count]
        cot_refs = refs[3 + count : 3 + 2 * count]
        down_ref = refs[3 + 2 * count]
        even_ref, odd_ref, own_ref = refs[4 + 2 * count : 7 + 2 * count]
        term_refs = refs[7 + 2 * count : 6 + 3 * count]
        long_ref, tile_ref, turn_ref = refs[6 + 3 * count :]
        for slot in range(count):
            term = dot_nn(active_ref[slot * tokens : (slot + 1) * tokens, :], down_ref[...])
            if slot:
                term_refs[slot - 1][...] = term.astype(jnp.bfloat16)
            else:
                own_ref[...] = term
        two = jnp.concatenate([ref[...] for ref in two_refs], axis=0)
        for runs, grad_ref in ((gate_runs, dgate_ref), (up_runs, dup_ref)):
            value = left_dot(two, grad_ref[...])
            for step in range(part):
                turn_ref[step] = value[:, step * LANES : (step + 1) * LANES]
            for row, size, base in runs:
                for step in range(part):
                    long_ref[pl.ds(base + step, size, stride=part), :] = turn_ref[
                        step, row : row + size, :
                    ]
        cot = jnp.concatenate([ref[...] for ref in cot_refs], axis=0)
        value = left_dot(active_ref[...], cot)
        for tile in range(tiles):
            width = min(LANES, D - tile * LANES)
            tile_ref[tile, :, :width] = value[:, tile * LANES : tile * LANES + width]
        for row, size, base in down_runs:
            def get(tile, parity, row=row, size=size):
                return tile_ref[tile, pl.ds(row + parity, size // 2, stride=2), :]

            flat_rows(get, long_ref, base, size // 2, D, 0)
        for odd, ref in enumerate((even_ref, odd_ref)):
            def move(step, carry, odd=odd, ref=ref):
                first = pl.multiple_of((place_ref[0] ^ (2 * step + odd)) * rows, 8)
                ref[step] = long_ref[pl.ds(first, rows), :].astype(jnp.bfloat16)
                return carry

            lax.fori_loop(0, dp_count // 2, move, 0)

    low, wide = jnp.bfloat16, jnp.float32
    total = rows * dp_count
    return kernel_call(
        kernel,
        [((dp_count // 2, rows, LANES), low)] * 2
        + [((tokens, D), wide)]
        + [((tokens, D), low)] * (count - 1),
        [((total, LANES), wide), ((tiles, hidden, LANES), wide), ((part, D, LANES), wide)],
        active, dgate, dup, *two_slots, *cot_slots, w_down,
        places=places,
    )


def middle_backward(own, others, middle, gain, cot_rows, w_out):
    tokens = own.shape[0]
    count = len(others)

    def kernel(own_ref, *refs):
        other_refs = refs[:count]
        mid_ref, gain_ref, cot_ref, out_ref = refs[count : count + 4]
        grad_ref, low_ref, mix_ref, sum_ref = refs[count + 4 :]
        grad = own_ref[...]
        for ref in other_refs:
            grad = grad + ref[...].astype(jnp.float32)
        middle = mid_ref[...]
        inverse = lax.rsqrt(jnp.mean(middle * middle, axis=-1, keepdims=True) + EPS)
        scaled = grad * gain_ref[...]
        cubed = inverse * inverse * inverse
        result = cot_ref[...] + (
            inverse * scaled - middle * cubed * jnp.mean(scaled * middle, axis=-1, keepdims=True)
        )
        grad_ref[...] = result
        low_ref[...] = result.astype(jnp.bfloat16)
        mix_ref[...] = dot_nt(low_ref[...], out_ref[...]).astype(jnp.bfloat16)
        sum_ref[...] = jnp.sum(grad * middle * inverse, axis=0, keepdims=True)

    low, wide = jnp.bfloat16, jnp.float32
    return kernel_call(
        kernel,
        [
            ((tokens, D), wide),
            ((tokens, D), low),
            ((tokens, HEADS * HEAD_DIM), low),
            ((1, D), wide),
        ],
        [],
        own, *others, middle, gain, cot_rows, w_out,
    )


def turn_back(block, tile, cosine, sine):
    width = KV_HEADS * HEAD_DIM - tile * LANES
    if width <= 0:
        return block
    turned = block * cosine - partner_lanes(block) * sine
    if width >= LANES:
        return turned
    lane = lax.broadcasted_iota(jnp.int32, block.shape, 1)
    return jnp.where(lane < width, turned, block)


def attend_backward(query, near_kv, grad_mix, logs, seg_col, seg_near, cosine, sine):
    tokens = query.shape[0]
    near_len = near_kv.shape[0]
    parts = near_len // tokens
    groups = HEADS // KV_HEADS
    qwidth, kwidth = HEADS * HEAD_DIM, KV_HEADS * HEAD_DIM
    scale = HEAD_DIM ** (-0.5)
    tiles = -(-qwidth // LANES)

    def kernel(
        query_ref, kv_ref, mix_ref, log_ref, seg_ref, near_ref, cos_ref, sin_ref, dquery_ref,
        near_out_ref, own_ref, *rest,
    ):
        part_refs = rest[: parts - 1]
        turn_ref, term_ref = rest[parts - 1 :]
        allowed = group_allowed(seg_ref, near_ref, tokens, near_len, groups)
        allowed = jnp.concatenate([allowed.astype(jnp.float32)] * groups, axis=0) > 0.5
        if tiles * LANES > qwidth:
            turn_ref[:, qwidth:] = jnp.zeros((tokens, tiles * LANES - qwidth), jnp.float32)
        for group in range(KV_HEADS):
            at = group * HEAD_DIM
            key = kv_ref[:, at : at + HEAD_DIM]
            value = kv_ref[:, kwidth + at : kwidth + at + HEAD_DIM]
            queries = group_rows(query_ref, group, groups)
            mixes = group_rows(mix_ref, group, groups)
            total = jnp.concatenate(
                [log_ref[:, group * groups + g : group * groups + g + 1] for g in range(groups)],
                axis=0,
            )
            scores = dot_nt(queries, key) * scale
            probs = jnp.exp(jnp.where(allowed, scores, -jnp.inf) - total)
            grad_probs = dot_nt(mixes, value)
            grad_scores = probs * (grad_probs - jnp.sum(probs * grad_probs, axis=-1, keepdims=True))
            grad_scores = (grad_scores * scale).astype(jnp.bfloat16)
            dquery = dot_nn(grad_scores, key)
            for g in range(groups):
                first = (group * groups + g) * HEAD_DIM
                turn_ref[:, first : first + HEAD_DIM] = dquery[g * tokens : (g + 1) * tokens]
            term_ref[:, at : at + HEAD_DIM] = left_dot(grad_scores, queries)
            term_ref[:, kwidth + at : kwidth + at + HEAD_DIM] = left_dot(
                probs.astype(jnp.bfloat16), mixes
            )
        for part in range(parts - 1):
            part_refs[part][...] = term_ref[part * tokens : (part + 1) * tokens, :].astype(
                jnp.bfloat16
            )
        own_ref[...] = term_ref[near_len - tokens :, :]
        for tile in range(2 * kwidth // LANES):
            span = slice(tile * LANES, (tile + 1) * LANES)
            near_out_ref[:, span] = turn_back(
                term_ref[:, span], tile, cos_ref[...], sin_ref[...]
            ).astype(jnp.bfloat16)
        for tile in range(tiles):
            width = min(LANES, qwidth - tile * LANES)
            block = turn_ref[:, tile * LANES : (tile + 1) * LANES]
            here = slice(near_len - tokens, near_len)
            block = block * cos_ref[here, :] - partner_lanes(block) * sin_ref[here, :]
            dquery_ref[:, tile * LANES : tile * LANES + width] = block[:, :width].astype(
                jnp.bfloat16
            )

    low, wide = jnp.bfloat16, jnp.float32
    return kernel_call(
        kernel,
        [((tokens, qwidth), low), ((near_len, 2 * kwidth), low), ((tokens, 2 * kwidth), wide)]
        + [((tokens, 2 * kwidth), low)] * (parts - 1),
        [((tokens, tiles * LANES), wide), ((near_len, 2 * kwidth), wide)],
        query, near_kv, grad_mix, logs, seg_col, seg_near, cosine, sine,
    )


def own_kv(own, others, cosine, sine):
    tokens = own.shape[0]
    kwidth = KV_HEADS * HEAD_DIM

    def kernel(own_ref, *refs):
        other_refs, (cos_ref, sin_ref, out_ref) = refs[:-3], refs[-3:]
        total = own_ref[...]
        for ref in other_refs:
            total = total + ref[...].astype(jnp.float32)
        for tile in range(2 * kwidth // LANES):
            block = total[:, tile * LANES : (tile + 1) * LANES]
            block = turn_back(block, tile, cos_ref[...], sin_ref[...])
            out_ref[:, tile * LANES : (tile + 1) * LANES] = block.astype(jnp.bfloat16)

    return kernel_call(
        kernel, [((tokens, 2 * kwidth), jnp.bfloat16)], [], own, *others, cosine, sine
    )[0]


def input_backward(grad_query, grad_kv, w_qkv, residual, gain, grad_middle):
    tokens = residual.shape[0]
    qwidth = HEADS * HEAD_DIM
    whole = w_qkv.shape[1]

    def kernel(query_ref, kv_ref, w_ref, res_ref, gain_ref, mid_ref, grad_ref, sum_ref, row_ref):
        row_ref[:, :qwidth] = query_ref[...]
        row_ref[:, qwidth:] = kv_ref[...]
        grad = dot_nt(row_ref[...], w_ref[...])
        residual = res_ref[...]
        inverse = lax.rsqrt(jnp.mean(residual * residual, axis=-1, keepdims=True) + EPS)
        scaled = grad * gain_ref[...]
        cubed = inverse * inverse * inverse
        grad_ref[...] = mid_ref[...] + (
            inverse * scaled
            - residual * cubed * jnp.mean(scaled * residual, axis=-1, keepdims=True)
        )
        sum_ref[...] = jnp.sum(grad * residual * inverse, axis=0, keepdims=True)

    return kernel_call(
        kernel,
        [((tokens, D), jnp.float32), ((1, D), jnp.float32)],
        [((tokens, whole), jnp.bfloat16)],
        grad_query, grad_kv, w_qkv, residual, gain, grad_middle,
    )


def attn_grads(
    places, normed_parts, head_mix, grad_query, near_kv, grad_mid, rows, dp_count, ctx_count
):
    parts = len(normed_parts)
    qwidth, kwidth = HEADS * HEAD_DIM, KV_HEADS * HEAD_DIM
    tiles = -(-max(qwidth, D) // LANES)
    runs = attn_pieces(rows, dp_count, ctx_count)
    share = rows * ctx_count

    def kernel(place_ref, *refs):
        normed_refs = refs[:parts]
        mix_ref, query_ref, kv_ref, mid_ref = refs[parts : parts + 4]
        even_ref, odd_ref, long_ref, tile_ref = refs[parts + 4 :]
        near = jnp.concatenate([ref[...] for ref in normed_refs], axis=0)
        for value, matrices in (
            (left_dot(normed_refs[-1][...], query_ref[...]), ((0, qwidth, runs[0]),)),
            (
                left_dot(near, kv_ref[...]),
                ((0, kwidth, runs[1]), (kwidth, kwidth, runs[2])),
            ),
            (left_dot(mix_ref[...], mid_ref[...]), ((0, D, runs[3]),)),
        ):
            span = value.shape[1]
            for tile in range(-(-span // LANES)):
                width = min(LANES, span - tile * LANES)
                tile_ref[tile, :, :width] = value[:, tile * LANES : tile * LANES + width]
            for first, width, matrix in matrices:
                lead, offset = divmod(first // HALF, 2)
                for row, count, base, _ in matrix:
                    def get(tile, parity, lead=lead, row=row, count=count):
                        return tile_ref[lead + tile, pl.ds(row + parity, count // 2, stride=2), :]

                    flat_rows(get, long_ref, base, count // 2, width, offset)
        for mask in range(dp_count):
            ref = odd_ref if mask % 2 else even_ref
            first = pl.multiple_of((place_ref[0] ^ mask) * share, 8)
            chunk = GRAIN

            def move(step, carry, ref=ref, mask=mask, first=first):
                at = pl.multiple_of(step * chunk, 8)
                ref[mask // 2, pl.ds(at, chunk), :] = long_ref[pl.ds(first + at, chunk), :].astype(
                    jnp.bfloat16
                )
                return carry

            lax.fori_loop(0, share // chunk, move, 0)

    half = (dp_count // 2, share, LANES)
    return kernel_call(
        kernel,
        [(half, jnp.bfloat16)] * 2,
        [((dp_count * share, LANES), jnp.float32), ((tiles, D, LANES), jnp.float32)],
        *normed_parts, head_mix, grad_query, near_kv, grad_mid,
        places=places,
    )


def after(value, *others):
    return lax.optimization_barrier((value,) + others)[0]


def from_chips(rows):
    return [(0, rows)] + [
        (mask, lax.ppermute(rows, "dp", swap_pairs("dp", mask)))
        for mask in range(2, lax.axis_size("dp"), 2)
    ]


def with_cores(held):
    return held + [
        (mask + 1, lax.ppermute(array, "dp", swap_pairs("dp", 1))) for mask, array in held
    ]


def reduce_cores(even, odd, *before):
    wide = jnp.float32
    moved = after(lax.ppermute(odd, "dp", swap_pairs("dp", 1)), *before)
    return [
        (even[at].astype(wide) + moved[at].astype(wide)).astype(jnp.bfloat16)
        for at in range(even.shape[0])
    ]


def reduce_chips(sums):
    total = sums[0].astype(jnp.float32)
    for at in range(1, len(sums)):
        moved = lax.ppermute(sums[at], "dp", swap_pairs("dp", 2 * at))
        total = total + moved.astype(jnp.float32)
    return total.astype(jnp.bfloat16)


def body(hidden_in, segments, attn_flat, mlp_flat, norm_one, norm_two, cotangent):
    dp_count, ctx_count = lax.axis_size("dp"), lax.axis_size("ctx")
    if not (
        hidden_in.shape[0] == 1
        and columns_apply(dp_count, ctx_count, mlp_flat.shape[0])
        and attn_fits(attn_flat.shape[0], dp_count, ctx_count)
    ):
        return body_rows(hidden_in, segments, attn_flat, mlp_flat, norm_one, norm_two, cotangent)
    return body_columns(hidden_in, segments, attn_flat, mlp_flat, norm_one, norm_two, cotangent)


def body_columns(hidden_in, segments, attn_flat, mlp_flat, norm_one, norm_two, cotangent):
    tokens = hidden_in.shape[1]
    seq_len = segments.shape[1]
    low = jnp.bfloat16
    dp_count = lax.axis_size("dp")
    ctx_count = lax.axis_size("ctx")
    attn_rows, mlp_rows = attn_flat.shape[0], mlp_flat.shape[0]
    back = -(-(seq_len // 2 - 1) // tokens)
    start_row = lax.axis_index("ctx") * tokens

    places = jnp.stack([lax.axis_index("dp"), lax.axis_index("ctx")]).astype(jnp.int32)
    up_pairs = [
        [(place, place + step) for place in range(ctx_count - step)] for step in range(back + 1)
    ]
    down_pairs = [[(right, left) for left, right in pairs] for pairs in up_pairs]
    residual = hidden_in.reshape(tokens, D)
    cot_rows = cotangent.reshape(tokens, D)
    normed_one = norm_forward(residual, norm_one)[1].astype(low)

    pos_near = lax.dynamic_slice_in_dim(
        jnp.pad(positions_of(segments), ((0, 0), (back * tokens, 0))),
        start_row,
        (back + 1) * tokens,
        1,
    )
    seg_col = lax.dynamic_slice_in_dim(segments, start_row, tokens, 1).reshape(tokens, 1)
    seg_near = lax.dynamic_slice_in_dim(
        jnp.pad(segments, ((0, 0), (back * tokens, 0)), constant_values=-1),
        start_row,
        (back + 1) * tokens,
        1,
    )
    cosine, sine = [table[:, 0] for table in rope_tables(pos_near.reshape(-1))]
    heads = 128 // HEAD_DIM
    cosine = jnp.concatenate([cosine, cosine] * heads, axis=1)
    sine = jnp.concatenate([-sine, sine] * heads, axis=1)
    gain_one, gain_two = norm_one.reshape(1, D), norm_two.reshape(1, D)

    padded = -(-attn_rows // 32) * 32
    flat = jnp.pad(attn_flat, ((0, padded - attn_rows), (0, 0)))
    own_blocks = from_chips(flat)
    others = jnp.concatenate(spread(flat)[1:], axis=0)
    others, window, *arrays = lax.optimization_barrier(
        (others, normed_one, *[array for _, array in own_blocks])
    )
    own_blocks = with_cores([(mask, array) for (mask, _), array in zip(own_blocks, arrays)])
    normed_parts = [
        lax.ppermute(window, "ctx", up_pairs[step]) for step in range(back, 0, -1)
    ] + [normed_one]
    mlp_near = trade_mlp(mlp_flat, others)
    other_blocks = from_chips(others)
    cot_low, cosine, sine, *arrays = lax.optimization_barrier(
        (cot_rows.astype(low), cosine, sine, *[array for _, array in other_blocks], *normed_parts[:-1], mlp_near)
    )
    other_blocks = with_cores([(mask, array) for (mask, _), array in zip(other_blocks, arrays)])
    cot_slots = spread(cot_low)
    held = [(mask, (0,), array) for mask, array in own_blocks]
    held += [(mask, tuple(range(1, ctx_count)), array) for mask, array in other_blocks]

    query, near_kv, w_qkv, w_out = project(
        places, held, normed_parts, cosine, sine, attn_rows, padded, dp_count, ctx_count
    )
    mlp_near = after(mlp_near, *[array for _, _, array in held])
    mlp_whole = lax.all_gather(mlp_near, "dp", axis=0, tiled=True)
    head_mix, logs, middle, normed_two = attend(
        query, near_kv, seg_col, seg_near, residual, w_out, gain_two
    )
    two_slots = spread(normed_two)

    w_gate, w_up, w_down, grad_active = unpack_mlp(
        mlp_whole, cot_slots, mlp_rows, dp_count, ctx_count
    )
    active, grad_gate, grad_up, *two_terms = feed_forward(two_slots, w_gate, w_up, grad_active)
    two_others = returned(two_terms[1:])
    mlp_even, mlp_odd, block_own, *block_terms = mlp_grads(
        places, active, grad_gate, grad_up, two_slots, cot_slots, w_down, mlp_rows, dp_count, ctx_count
    )
    grad_middle, grad_mid_low, grad_mix, grad_gain_two = middle_backward(
        after(two_terms[0], mlp_even), two_others, middle, gain_two, cot_rows, w_out
    )
    grad_query, near_grads, kv_own, *kv_terms = attend_backward(
        query, near_kv, grad_mix, logs, seg_col, seg_near, cosine, sine
    )
    mlp_sums = reduce_cores(mlp_even, after(mlp_odd, *two_others), grad_query)
    even, odd = attn_grads(
        after(places, *mlp_sums), normed_parts, head_mix, grad_query, near_grads, grad_mid_low,
        attn_rows, dp_count, ctx_count,
    )
    mlp_own = reduce_chips([after(mlp_sums[0], odd)] + mlp_sums[1:])
    block_others = returned([after(term, odd) for term in block_terms])
    sums = reduce_cores(even, after(odd, mlp_own))
    block_rows = middle + block_own
    for moved in block_others:
        block_rows = block_rows + moved.astype(jnp.float32)
    mlp_grad = scatter_mlp(after(mlp_own, *sums))
    kv_others = [
        lax.ppermute(after(kv_terms[back - step], *sums), "ctx", down_pairs[step]) for step in range(1, back + 1)
    ]
    total = reduce_chips([after(sums[0], *kv_others, *block_others)] + sums[1:])
    attn_blocks = trade(total.reshape(ctx_count, -1, 128))
    kv_own = after(kv_own, total)
    grad_kv = own_kv(kv_own, kv_others, cosine[-tokens:], sine[-tokens:])
    grad_in, grad_gain_one = input_backward(
        grad_query, grad_kv, w_qkv, residual, gain_one, grad_middle
    )
    gains = jnp.concatenate([grad_gain_one, grad_gain_two], axis=0)
    gains = add_swapped(after(gains, *attn_blocks[1:]), "dp", (1,))
    gains = add_swapped(gains, "dp", range(2, dp_count, 2))
    gain_sums = add_swapped(gains, "ctx", range(1, ctx_count))
    attn_grad = 0.0
    for block in attn_blocks:
        attn_grad = attn_grad + block.astype(jnp.float32)
    return (
        block_rows.reshape(hidden_in.shape),
        grad_in.reshape(hidden_in.shape),
        attn_grad,
        mlp_grad,
        gain_sums[0],
        gain_sums[1],
    )


def solution(mesh):
    in_specs = (
        P("dp", "ctx", None),
        P("dp", None),
        P(("dp", "ctx"), None),
        P(("dp", "ctx"), None),
        P(),
        P(),
        P("dp", "ctx", None),
    )
    out_specs = (
        P("dp", "ctx", None),
        P("dp", "ctx", None),
        P(("dp", "ctx"), None),
        P(("dp", "ctx"), None),
        P(),
        P(),
    )
    return jax.shard_map(body, mesh=mesh, in_specs=in_specs, out_specs=out_specs, check_vma=False)
```
